512 devices in a mesh: seq: 128 (over x, z, core), ch: 4 (over y).
Axes of the slice: x: 4, y: 4, z: 16, core: 2. Of those that a mesh axis runs over, the one named last changes fastest.
Arguments:
- signal: bfloat16 [512, 16448], P('seq'), may hold values from -6 to 6
- cotangent: bfloat16 [512, 16448], P('seq'), may hold values from -6 to 6
- counts: int32 [128], replicated, may hold values from 1 to 4, as said below
- freq_gain: float32 [64], replicated, may hold values from 0.5 to 1.5
- freq_in: bfloat16 [64, 256], P(None, 'ch'), may hold values from -0.75 to 0.75
- freq_taps: float32 [3, 256], P(None, 'ch'), may hold values from -3.5 to 3.5
- freq_out: bfloat16 [256, 64], P('ch'), may hold values from -0.375 to 0.375
- time_gain: float32 [64], replicated, may hold values from 0.5 to 1.5
- time_in: bfloat16 [64, 256], P(None, 'ch'), may hold values from -0.75 to 0.75
- time_taps: float32 [3, 3, 256], P(None, None, 'ch'), may hold values from -3.5 to 3.5
- time_out: bfloat16 [256, 64], P('ch'), may hold values from -0.375 to 0.375
Outputs:
- output: bfloat16 [512, 16448], P('seq')
- d_signal: bfloat16 [512, 16448], P('seq')
- grad_freq_gain: float32 [64], replicated
- grad_freq_in: float32 [64, 256], P(None, 'ch')
- grad_freq_taps: float32 [3, 256], P(None, 'ch')
- grad_freq_out: float32 [256, 64], P('ch')
- grad_time_gain: float32 [64], replicated
- grad_time_in: float32 [64, 256], P(None, 'ch')
- grad_time_taps: float32 [3, 3, 256], P(None, None, 'ch')
- grad_time_out: float32 [256, 64], P('ch')
The draws below stay inside these ranges and needn't reach their ends.
Inputs may be any that keep to these rules, and one draw needn't show every extreme that they name: counts[i] is the number of valid leading frames of frames i * 4 to (i + 1) * 4 - 1; some block is full.
All inputs are finite; a program needn't handle non-finite values.
Results may differ from the reference program's by a relative error of at most 0.024.
Values may be sent and summed in bfloat16 or wider, within the bound.
No kernel may reach another device: no remote copies, remote signals or barrier semaphores. Data moves between devices by JAX's collectives and lax.ppermute only.
A program may use at most 64 MiB of HBM per device.

```python
import math
import jax
import jax.numpy as jnp
from jax import lax

C = 64
F = 257
H = 256
LAYERS = 3
FR_DEV = 4
SPANS = 128
FRAMES = 512
FC = 16448
N_CH = 4


def draw_counts(key, part):
    first_key, second_key = jax.random.split(jax.random.fold_in(key, 11))
    drawn = jax.random.randint(first_key, (SPANS,), 1, FR_DEV + 1)
    full_index = jax.random.randint(second_key, (), 0, SPANS)
    return jnp.where(jnp.arange(SPANS) == full_index, FR_DEV, drawn).astype(jnp.int32)


def shard_levels(stream_key, dims, cuts, smallest, top_value):
    def one(axis_at, blocks):
        heights = jax.random.uniform(jax.random.fold_in(jax.random.fold_in(stream_key, 6), axis_at), (blocks,), jnp.float32, smallest / len(cuts), top_value / len(cuts))
        return jnp.repeat(jnp.exp(heights), dims[axis_at] // blocks).reshape((-1,) + (1,) * (len(dims) - axis_at - 1))

    level = one(*cuts[0])
    for cut in cuts[1:]:
        level = level * one(*cut)
    return level


def centred(stream_key, dims, deviation, reach, cuts=(), held_as=jnp.bfloat16):
    values = deviation * jax.random.normal(stream_key, dims, jnp.float32)
    if cuts:
        values = values * shard_levels(stream_key, dims, cuts, -0.22, 0.18)
    return jnp.clip(values, -reach, reach).astype(held_as)


def setup_inputs(seed: int = 0) -> dict:
    splits = jax.random.split(jax.random.key(seed), 12)
    return {
        "signal": centred(splits[0], (FRAMES, FC), 1.0, 6.0, ((0, 128),)),
        "cotangent": centred(splits[1], (FRAMES, FC), 1.0, 6.0, ((0, 128),)),
        "counts": draw_counts(jax.random.fold_in(splits[11], 71), 0),
        "freq_gain": jnp.clip(1.0 + 0.1 * jax.random.normal(splits[3], (C,), jnp.float32), 0.5, 1.5),
        "freq_in": centred(splits[4], (C, H), C ** -0.5, 0.75, ((1, 4),)),
        "freq_taps": centred(splits[5], (3, H), 3 ** -0.5, 3.5, ((1, 4),), jnp.float32),
        "freq_out": centred(splits[6], (H, C), H ** -0.5, 0.375, ((0, 4),)),
        "time_gain": jnp.clip(1.0 + 0.1 * jax.random.normal(splits[7], (C,), jnp.float32), 0.5, 1.5),
        "time_in": centred(splits[8], (C, H), C ** -0.5, 0.75, ((1, 4),)),
        "time_taps": centred(splits[9], (LAYERS, 3, H), 3 ** -0.5, 3.5, ((2, 4),), jnp.float32),
        "time_out": centred(splits[10], (H, C), H ** -0.5, 0.375, ((0, 4),)),
    }


EPS = 1e-05

def offset_rows(values, offset, axis_pos):
    length = values.shape[axis_pos]
    widths = [(0, 0)] * values.ndim
    widths[axis_pos] = (max(-offset, 0), max(offset, 0))
    padded = jnp.pad(values, widths)
    return lax.slice_in_dim(padded, max(offset, 0), max(offset, 0) + length, axis=axis_pos)

def dilated(values, tap_rows, spacing, axis_pos):
    return tap_rows[0] * offset_rows(values, -spacing, axis_pos) + tap_rows[1] * values + tap_rows[2] * offset_rows(values, spacing, axis_pos)

def dilated_back(grads, tap_rows, spacing, axis_pos):
    return tap_rows[0] * offset_rows(grads, spacing, axis_pos) + tap_rows[1] * grads + tap_rows[2] * offset_rows(grads, -spacing, axis_pos)

def tap_sums(drive, source, spacing, axis_pos):
    over_dims = tuple(range(drive.ndim - 1))
    return jnp.stack([lax.optimization_barrier(jnp.sum(drive * offset_rows(source, -spacing, axis_pos), axis=over_dims)), lax.optimization_barrier(jnp.sum(drive * source, axis=over_dims)), lax.optimization_barrier(jnp.sum(drive * offset_rows(source, spacing, axis_pos), axis=over_dims))])

def silu_slope(drive):
    sigmoid_part = jax.nn.sigmoid(drive)
    return sigmoid_part * (1.0 + drive * (1.0 - sigmoid_part))

def inverse_norm(features):
    return lax.rsqrt(lax.optimization_barrier(jnp.mean(features * features, axis=-1, keepdims=True)) + EPS)

def norm_back(d_normed, features, norm_scale, gain):
    summed = lax.optimization_barrier(jnp.sum(gain * d_normed * features, axis=-1, keepdims=True))
    return norm_scale * gain * d_normed - features * norm_scale * norm_scale * norm_scale * summed / features.shape[-1]

def spacing_for(layer_idx):
    if layer_idx == 0:
        return 1
    return FR_DEV * 4 ** (layer_idx - 1)

def grouped_out(hidden, weight):
    leading = hidden.shape[:-1]
    parts = jnp.einsum('ngh,ghc->ngc', hidden.reshape((-1, N_CH, H // N_CH)).astype(jnp.float32), weight.reshape(N_CH, H // N_CH, -1).astype(jnp.float32))
    rounded = lax.optimization_barrier(parts.astype(jnp.bfloat16)).astype(jnp.float32)
    return lax.optimization_barrier(jnp.sum(rounded, axis=1)).reshape(leading + (weight.shape[1],))

def grouped_back(d_pre, weight):
    leading = d_pre.shape[:-1]
    parts = jnp.einsum('ngh,cgh->ngc', d_pre.reshape((-1, N_CH, H // N_CH)).astype(jnp.float32), weight.reshape(weight.shape[0], N_CH, H // N_CH).astype(jnp.float32))
    rounded = lax.optimization_barrier(parts.astype(jnp.bfloat16)).astype(jnp.float32)
    return lax.optimization_barrier(jnp.sum(rounded, axis=1)).reshape(leading + (weight.shape[0],))

def reference(signal, cotangent, counts, freq_gain, freq_in, freq_taps, freq_out, time_gain, time_in, time_taps, time_out):
    frame_count = signal.shape[0]
    grad_scale = 1.0 / math.sqrt(frame_count * F)
    x_blocks = signal.reshape(frame_count // FR_DEV, FR_DEV, F, C)
    cot_all = cotangent.reshape(frame_count, F, C)
    valid = (jnp.arange(FR_DEV)[None, :] < counts[:, None]).astype(jnp.float32).reshape(frame_count)

    def freq_forward(x_block):
        features = x_block.astype(jnp.float32)
        norm_scale = inverse_norm(features)
        normed = (features * norm_scale * freq_gain).astype(jnp.bfloat16)
        hidden = jnp.einsum('tfc,ch->tfh', normed.astype(jnp.float32), freq_in.astype(jnp.float32))
        drive = dilated(hidden, freq_taps, 1, 1)
        active = jax.nn.silu(drive).astype(jnp.bfloat16)
        return (features, norm_scale, normed, hidden, drive, active)

    def freq_mixed(x_block):
        features, norm_scale, normed, hidden, drive, active = freq_forward(x_block)
        return (features + grouped_out(active, freq_out)).astype(jnp.bfloat16)
    x_one = lax.map(freq_mixed, x_blocks).reshape(frame_count, F, C)

    def time_column(inputs):
        x_column, g_column = inputs
        features = x_column.astype(jnp.float32)
        norm_scale = inverse_norm(features)
        normed = (features * norm_scale * time_gain).astype(jnp.bfloat16)
        hidden = jnp.dot(normed, time_in, preferred_element_type=jnp.float32) * valid[:, None]
        states = [hidden]
        drives = []
        for layer_idx in range(LAYERS):
            drive = dilated(hidden, time_taps[layer_idx], spacing_for(layer_idx), 0)
            drives.append(drive)
            hidden = hidden + jax.nn.silu(drive)
            states.append(hidden)
        top_hidden = hidden.astype(jnp.bfloat16)
        y_column = (features + grouped_out(top_hidden, time_out)).astype(jnp.bfloat16)
        grad_out = jnp.dot(top_hidden.T, g_column, preferred_element_type=jnp.float32)
        d_hidden = jnp.dot(g_column, time_out.T, preferred_element_type=jnp.float32)
        tap_list = [None] * LAYERS
        for layer_idx in reversed(range(LAYERS)):
            spacing = spacing_for(layer_idx)
            d_drive = d_hidden * silu_slope(drives[layer_idx])
            tap_list[layer_idx] = tap_sums(d_drive, states[layer_idx], spacing, 0)
            d_hidden = d_hidden + dilated_back(d_drive, time_taps[layer_idx], spacing, 0)
        d_pre = (d_hidden * valid[:, None]).astype(jnp.bfloat16)
        grad_in = jnp.dot(normed.T, d_pre, preferred_element_type=jnp.float32)
        d_normed = grouped_back(d_pre, time_in)
        grad_gain = lax.optimization_barrier(jnp.sum(d_normed * features * norm_scale, axis=0))
        d_column = (g_column.astype(jnp.float32) + norm_back(d_normed, features, norm_scale, time_gain)).astype(jnp.bfloat16)
        return (y_column, d_column, grad_gain, grad_in, jnp.stack(tap_list), grad_out)
    y_cols, d_cols, t_gain, t_in, t_taps, t_out = lax.map(time_column, (jnp.transpose(x_one, (1, 0, 2)), jnp.transpose(cot_all, (1, 0, 2))))
    output = jnp.transpose(y_cols, (1, 0, 2)).reshape(frame_count, F * C)
    d_one = jnp.transpose(d_cols, (1, 0, 2)).reshape(frame_count // FR_DEV, FR_DEV, F, C)

    def freq_back(inputs):
        x_block, d_block = inputs
        features, norm_scale, normed, hidden, drive, active = freq_forward(x_block)
        d_float = d_block.astype(jnp.float32)
        grad_out = jnp.einsum('tfh,tfc->hc', active.astype(jnp.float32), d_float)
        d_active = jnp.einsum('tfc,hc->tfh', d_float, freq_out.astype(jnp.float32))
        d_drive = d_active * silu_slope(drive)
        grad_taps = tap_sums(d_drive, hidden, 1, 1)
        d_hidden = dilated_back(d_drive, freq_taps, 1, 1).astype(jnp.bfloat16)
        grad_in = jnp.einsum('tfc,tfh->ch', normed.astype(jnp.float32), d_hidden.astype(jnp.float32))
        d_normed = grouped_back(d_hidden, freq_in)
        grad_gain = lax.optimization_barrier(jnp.sum(d_normed * features * norm_scale, axis=(0, 1)))
        d_x = (d_float + norm_back(d_normed, features, norm_scale, freq_gain)).astype(jnp.bfloat16)
        return (d_x, grad_gain, grad_in, grad_taps, grad_out)
    d_x, f_gain, f_in, f_taps, f_out = lax.map(freq_back, (x_blocks, d_one))
    d_signal = d_x.reshape(frame_count, F * C)
    return (output, d_signal, lax.optimization_barrier(jnp.sum(f_gain, axis=0)) * grad_scale, lax.optimization_barrier(jnp.sum(f_in, axis=0)) * grad_scale, lax.optimization_barrier(jnp.sum(f_taps, axis=0)) * grad_scale, lax.optimization_barrier(jnp.sum(f_out, axis=0)) * grad_scale, lax.optimization_barrier(jnp.sum(t_gain, axis=0)) * grad_scale, lax.optimization_barrier(jnp.sum(t_in, axis=0)) * grad_scale, lax.optimization_barrier(jnp.sum(t_taps, axis=0)) * grad_scale, lax.optimization_barrier(jnp.sum(t_out, axis=0)) * grad_scale)
```

```python
import math

import jax
import jax.numpy as jnp
from jax import lax
from jax.sharding import Mesh, PartitionSpec as P

EPS = 1e-05
FR = 4
ROWS = 80
LEAD = 8
BF = jnp.bfloat16
F32 = jnp.float32


def nt(a, b):
    return lax.dot_general(a, b, (((1,), (1,)), ((), ())), preferred_element_type=F32)


def nn(a, b):
    return lax.dot_general(a, b, (((1,), (0,)), ((), ())), preferred_element_type=F32)


def tn(a, b):
    return lax.dot_general(a, b, (((0,), (0,)), ((), ())), preferred_element_type=F32)


def roll_rows(values, amount):
    return jnp.roll(values, amount, 0)


def sigmoid(values):
    return 0.5 * jnp.tanh(0.5 * values) + 0.5


def inverse_norm(features):
    return lax.rsqrt(jnp.mean(features * features, axis=-1, keepdims=True) + EPS)


def norm_back(d_normed, features, scale, gain):
    scaled = d_normed * gain
    summed = jnp.sum(scaled * features, axis=-1, keepdims=True)
    return scale * scaled - features * (scale * scale * scale * summed * (1.0 / features.shape[-1]))


def bins_conv(values, taps):
    return taps[0:1] * roll_rows(values, 1) + taps[1:2] * values + taps[2:3] * roll_rows(values, -1)


def freq_forward(pair, weights, taps, gain):
    features = pair[:, :64].astype(F32)
    scale = inverse_norm(features)
    normed = (features * scale * gain).astype(BF)
    hidden = nt(normed, weights[:, :64])
    drive = bins_conv(hidden, taps)
    active = (drive * sigmoid(drive)).astype(BF)
    mixed = nn(active, weights[:, 64:])
    x_one = (features + mixed).astype(BF)
    return jnp.concatenate([x_one, pair[:, 64:]], axis=1), hidden


def own_bins(last_plane):
    row = lax.broadcasted_iota(jnp.int32, (ROWS, 1), 0)
    upper = LEAD + 64 + last_plane
    one = jnp.where((row >= LEAD) & (row < upper), 1.0, 0.0).astype(F32)
    return jnp.concatenate([one] * FR, axis=0)


def freq_backward(pair, hidden, back, weights, taps, gain, last_plane):
    own = own_bins(last_plane)
    features = pair[:, :64].astype(F32)
    scale = inverse_norm(features)
    grad = back[:, 64:]
    grad_own = grad.astype(F32) * own
    normed = (features * scale * gain * own).astype(BF)
    drive = bins_conv(hidden, taps)
    gate = sigmoid(drive)
    active = drive * gate
    slope = gate + active * (1.0 - gate)
    grad_out = tn(active.astype(BF), grad_own.astype(BF))
    d_drive = nt(grad, weights[:, 64:]) * slope
    d_own = d_drive * own
    tap_rows = [
        jnp.sum(d_own * roll_rows(hidden, 1), axis=0, keepdims=True),
        jnp.sum(d_own * hidden, axis=0, keepdims=True),
        jnp.sum(d_own * roll_rows(hidden, -1), axis=0, keepdims=True),
    ]
    d_hidden = (
        taps[0:1] * roll_rows(d_drive, -1) + taps[1:2] * d_drive + taps[2:3] * roll_rows(d_drive, 1)
    ).astype(BF)
    grad_in = tn(d_hidden, normed)
    d_normed = nn(d_hidden, weights[:, :64])
    grad_gain = jnp.sum(d_normed * features * scale * own, axis=0, keepdims=True)
    d_signal = (grad.astype(F32) + norm_back(d_normed, features, scale, gain)).astype(BF)
    return (
        jnp.concatenate([back[:, :64], d_signal], axis=1),
        jnp.concatenate([grad_out, grad_in], axis=1),
        jnp.concatenate(tap_rows, axis=0),
        grad_gain,
    )


def groups_on(values, count):
    split = 8 * abs(count)
    if count > 0:
        head = jnp.concatenate(
            [jnp.concatenate([values[8 * i + 4 : 8 * i + 8], values[8 * i : 8 * i + 4]], axis=0) for i in range(count)],
            axis=0,
        )
        return jnp.concatenate([values[split:], head], axis=0)
    base = values.shape[0] - split
    tail = jnp.concatenate(
        [
            jnp.concatenate([values[base + 8 * i + 4 : base + 8 * i + 8], values[base + 8 * i : base + 8 * i + 4]], axis=0)
            for i in range(-count)
        ],
        axis=0,
    )
    return jnp.concatenate([tail, values[:base]], axis=0)


def later(values, spacing):
    if spacing == 1:
        place = lax.broadcasted_iota(jnp.int32, values.shape, 0) & 3
        return jnp.where(place == 3, roll_rows(groups_on(values, 1), 3), roll_rows(values, -1))
    return groups_on(values, spacing // FR)


def earlier(values, spacing):
    if spacing == 1:
        place = lax.broadcasted_iota(jnp.int32, values.shape, 0) & 3
        return jnp.where(place == 0, roll_rows(groups_on(values, -1), -3), roll_rows(values, 1))
    return groups_on(values, -(spacing // FR))


def own_rows(values):
    tiles = values.reshape(values.shape[0] // 8, 8, values.shape[1])
    return jnp.sum(jnp.sum(tiles, axis=0)[:4], axis=0, keepdims=True)


def time_path(pair, marks, weights, taps, gain, share):
    valid, inside = marks[:, 0:1], marks[:, 1:2]
    place = lax.broadcasted_iota(jnp.int32, (pair.shape[0], 1), 0) & 7
    counted = jnp.where(place < 4, share, 0.0).astype(F32)
    features = pair[:, :64].astype(F32)
    grad = pair[:, 64:]
    scale = inverse_norm(features)
    normed = features * scale * gain
    weight_in, weight_out = weights[:, :64], weights[:, 64:]
    state = nt(normed.astype(BF), weight_in) * valid
    states, slopes = [], []
    for layer in range(3):
        spacing = (1, 4, 16)[layer]
        row = taps[3 * layer : 3 * layer + 3]
        drive = row[0:1] * earlier(state, spacing) + row[1:2] * state + row[2:3] * later(state, spacing)
        gate = sigmoid(drive)
        active = drive * gate
        states.append(state)
        slopes.append(gate + active * (1.0 - gate))
        state = state + active
        if layer < 2:
            state = state * inside
    top = state.astype(BF)
    output = (features + nn(top, weight_out)).astype(BF)
    grad_out = tn(top, (grad.astype(F32) * counted).astype(BF))
    d_state = nt(grad, weight_out)
    tap_rows = [None] * 9
    for layer in reversed(range(3)):
        spacing = (1, 4, 16)[layer]
        row = taps[3 * layer : 3 * layer + 3]
        d_drive = d_state * slopes[layer]
        if layer < 2:
            d_drive = d_drive * inside
        held = states[layer]
        tap_rows[3 * layer] = own_rows(d_drive * earlier(held, spacing))
        tap_rows[3 * layer + 1] = own_rows(d_drive * held)
        tap_rows[3 * layer + 2] = own_rows(d_drive * later(held, spacing))
        d_state = d_state + (
            row[0:1] * later(d_drive, spacing) + row[1:2] * d_drive + row[2:3] * earlier(d_drive, spacing)
        )
    d_pre = (d_state * valid).astype(BF)
    grad_in = tn(d_pre, (normed * counted).astype(BF))
    d_normed = nn(d_pre, weight_in)
    grad_gain = own_rows(d_normed * features * scale) * share
    d_one = (grad.astype(F32) + norm_back(d_normed, features, scale, gain)).astype(BF)
    return (
        jnp.concatenate([output, d_one], axis=1),
        jnp.concatenate([grad_out, grad_in], axis=1),
        jnp.concatenate(tap_rows, axis=0) * share,
        grad_gain,
    )


def plane_rows(values, plane):
    frames, width = values.shape
    padded = jnp.pad(values, ((0, 0), (LEAD * 64, (ROWS - LEAD + 192) * 64 - width)))
    cut = lax.dynamic_slice(padded, (0, plane * 4096), (frames, ROWS * 64))
    return cut.reshape(frames * ROWS, 64)


def begin(signal, cotangent, freq_in, freq_taps, freq_out, time_in, time_taps, time_out, plane):
    pair = jnp.concatenate([plane_rows(signal, plane), plane_rows(cotangent, plane)], axis=1)
    taps = jnp.concatenate([freq_taps, time_taps.reshape(9, 64)], axis=0)
    high = lax.reduce_precision(taps, 8, 7)
    low = lax.reduce_precision(taps - high, 8, 7)
    packed = jnp.concatenate(
        [
            jnp.concatenate([freq_in.T, freq_out], axis=1),
            jnp.concatenate([time_in.T, time_out], axis=1),
            jnp.concatenate([high, low], axis=1).astype(BF),
            jnp.zeros((4, 128), BF),
        ],
        axis=0,
    )
    return pair, packed


def unpack(gathered):
    freq_w = gathered[:, :64].reshape(256, 128)
    time_w = gathered[:, 64:128].reshape(256, 128)
    tap_rows = gathered[:, 128:140].astype(F32)
    taps = (tap_rows[:, :, :64] + tap_rows[:, :, 64:]).transpose(1, 0, 2).reshape(12, 256)
    return freq_w, time_w, taps


def to_bands(own, halo):
    both = jnp.concatenate([own.reshape(FR, ROWS, 128), halo.reshape(FR, ROWS, 128)], axis=0)
    mine = both[:, LEAD : LEAD + 64].reshape(2 * FR, 32, 2, 128).transpose(1, 2, 0, 3)
    edge = jnp.stack([both[:, LEAD - 1], both[:, LEAD + 64]], axis=0)[:, None]
    edge = jnp.pad(edge, ((0, 30), (0, 0), (0, 0), (0, 0)))
    return jnp.concatenate([mine, edge], axis=1).reshape(32, 24, 128)


def frame_marks(counts, x_at):
    by_plane = jnp.pad(counts.reshape(4, 32), ((1, 1), (0, 0)))
    window = lax.dynamic_slice(by_plane, (x_at, 0), (3, 32))
    spot = jnp.arange(32)
    halo_count = jnp.where(spot >= 16, window[0], window[2])
    halo_in = jnp.where(spot >= 16, (spot >= 21) & (x_at > 0), (spot <= 10) & (x_at < 3))
    limit = jnp.stack([window[1], halo_count], axis=1)
    valid = (jnp.arange(4) < limit[:, :, None]) & jnp.stack([spot >= 0, halo_in], axis=1)[:, :, None]
    inside = jnp.stack([spot >= 0, halo_in], axis=1)[:, :, None] & (jnp.arange(4) >= 0)
    return jnp.stack([valid.reshape(256), inside.reshape(256)], axis=1).astype(F32)


def to_frames(bands):
    return bands.reshape(3, 32, 8, 128)[:, :, :4].transpose(1, 0, 2, 3).reshape(32, 12, 128)


def from_frames(arrived, plane):
    rows = arrived.reshape(32, 3, FR, 128)
    mine = rows[:, :2].transpose(2, 0, 1, 3).reshape(FR, 64, 128)
    left = jnp.where(plane > 0, rows[0, 2], jnp.zeros((), BF))[:, None]
    right = rows[1, 2][:, None]
    return jnp.concatenate(
        [jnp.zeros((FR, LEAD - 1, 128), BF), left, mine, right, jnp.zeros((FR, ROWS - LEAD - 65, 128), BF)], axis=1
    ).reshape(FR * ROWS, 128)


def to_planes(done, freq_w, freq_t, freq_g, time_w, time_t, time_g):
    rows = done.reshape(FR, ROWS, 128)[:, LEAD : LEAD + 65].reshape(FR * 65, 128)
    rows = jnp.broadcast_to(rows, (4, FR * 65, 128))
    taps = jnp.concatenate([freq_t, time_t], axis=0).reshape(12, 4, 64).transpose(1, 0, 2).reshape(4, 6, 128)
    gains = jnp.broadcast_to(jnp.concatenate([freq_g, time_g], axis=1), (4, 1, 128))
    grads = jnp.concatenate(
        [freq_w.reshape(4, 64, 128), time_w.reshape(4, 64, 128), taps, gains, jnp.zeros((4, 1, 128), F32)], axis=1
    )
    return jnp.concatenate([rows, grads.astype(BF)], axis=1)


def outputs_of(arrived):
    rows = arrived[:, : FR * 65].reshape(4, FR, 65, 128)
    whole = jnp.concatenate([rows[0, :, :64], rows[1, :, :64], rows[2, :, :64], rows[3]], axis=1)
    return whole[:, :, :64].reshape(FR, -1), whole[:, :, 64:].reshape(FR, -1)


def grads_of(total, scale):
    total = total * scale
    taps = total[128:134].reshape(12, 64)
    return (
        total[134, :64],
        total[:64, 64:].T,
        taps[:3],
        total[:64, :64],
        total[134, 64:],
        total[64:128, 64:].T,
        taps[3:].reshape(3, 3, 64),
        total[64:128, :64],
    )


def halo_pairs():
    pairs = []
    for x_at in range(4):
        for spot in range(32):
            if spot <= 10 and x_at < 3:
                pairs.append(((x_at + 1) * 32 + spot, x_at * 32 + spot))
            if spot >= 21 and x_at > 0:
                pairs.append(((x_at - 1) * 32 + spot, x_at * 32 + spot))
    return pairs


SEQ = ("x", "z", "core")


def exchange(values, axes):
    return lax.all_to_all(values, axes, 0, 0)


def shards(
    signal, cotangent, counts, freq_gain, freq_in, freq_taps, freq_out, time_gain, time_in, time_taps, time_out
):
    plane = lax.axis_index("ch")
    x_at = lax.axis_index("x")
    spot = lax.axis_index(("z", "core"))
    grad_scale = 1.0 / math.sqrt(FR * 128 * (signal.shape[1] // 64))
    pair, packed = begin(signal, cotangent, freq_in, freq_taps, freq_out, time_in, time_taps, time_out, plane)
    halo = lax.ppermute(pair, SEQ, halo_pairs())
    gathered = exchange(jnp.broadcast_to(packed, (4,) + packed.shape), "ch")
    freq_w, time_w, taps = unpack(gathered)
    freq_t, time_t = taps[:3], taps[3:]
    gain_f, gain_t = freq_gain[None], time_gain[None]
    x_own, hidden = freq_forward(pair, freq_w, freq_t, gain_f)
    x_halo, _ = freq_forward(halo, freq_w, freq_t, gain_f)
    bands = exchange(to_bands(x_own, x_halo), ("z", "core")).reshape(32, 3, 8, 128)
    marks = frame_marks(counts, x_at)
    edge_share = jnp.where((plane == 3) & (spot == 1), 1.0, 0.0).astype(F32)
    mixed, sums = [], None
    for slot in range(3):
        share = edge_share if slot == 2 else jnp.ones((), F32)
        got = time_path(bands[:, slot].reshape(256, 128), marks, time_w, time_t, gain_t, share)
        mixed.append(got[0])
        sums = got[1:] if sums is None else tuple(a + b for a, b in zip(sums, got[1:]))
    arrived = exchange(to_frames(jnp.stack(mixed)), ("z", "core"))
    back = from_frames(arrived, plane)
    last_plane = jnp.where(plane == 3, 1, 0)
    done, grad_w, grad_t, grad_g = freq_backward(pair, hidden, back, freq_w, freq_t, gain_f, last_plane)
    planes = exchange(to_planes(done, grad_w, grad_t, grad_g, *sums), "ch")
    output, d_signal = outputs_of(planes)
    part = jnp.sum(planes[:, FR * 65 :].astype(F32), axis=0)
    part = jnp.sum(exchange(part.reshape(8, 17, 128), ("x", "core")), axis=0)
    part = jnp.sum(exchange(jnp.broadcast_to(part, (16, 17, 128)), "z"), axis=0)
    total = exchange(jnp.broadcast_to(part, (8, 17, 128)), ("x", "core")).reshape(136, 128)
    return (output, d_signal) + grads_of(total, grad_scale)


def solution(mesh):
    torus = Mesh(mesh.devices.reshape(4, 16, 2, 4), ("x", "z", "core", "ch"))
    return jax.shard_map(
        shards,
        mesh=torus,
        in_specs=(
            P(SEQ, None),
            P(SEQ, None),
            P(),
            P(),
            P(None, "ch"),
            P(None, "ch"),
            P("ch", None),
            P(),
            P(None, "ch"),
            P(None, None, "ch"),
            P("ch", None),
        ),
        out_specs=(
            P(SEQ, None),
            P(SEQ, None),
            P(),
            P(None, "ch"),
            P(None, "ch"),
            P("ch", None),
            P(),
            P(None, "ch"),
            P(None, None, "ch"),
            P("ch", None),
        ),
        check_vma=False,
    )
```

```python
import math

import jax
import jax.numpy as jnp
from jax import lax
from jax.experimental import pallas as pl
from jax.experimental.pallas import tpu as pltpu
from jax.sharding import Mesh, PartitionSpec as P

EPS = 1e-05
FR = 4
ROWS = 80
LEAD = 8
BF = jnp.bfloat16
F32 = jnp.float32


def nt(a, b):
    return lax.dot_general(a, b, (((1,), (1,)), ((), ())), preferred_element_type=F32)


def nn(a, b):
    return lax.dot_general(a, b, (((1,), (0,)), ((), ())), preferred_element_type=F32)


def tn(a, b):
    return lax.dot_general(a, b, (((0,), (0,)), ((), ())), preferred_element_type=F32)


def roll_rows(values, amount):
    return pltpu.roll(values, amount % values.shape[0], 0)


def sigmoid(values):
    return 0.5 * jnp.tanh(0.5 * values) + 0.5


def inverse_norm(features):
    return lax.rsqrt(jnp.mean(features * features, axis=-1, keepdims=True) + EPS)


def norm_back(d_normed, features, scale, gain):
    scaled = d_normed * gain
    summed = jnp.sum(scaled * features, axis=-1, keepdims=True)
    return scale * scaled - features * (scale * scale * scale * summed * (1.0 / features.shape[-1]))


def bins_conv(values, taps):
    return taps[0:1] * roll_rows(values, 1) + taps[1:2] * values + taps[2:3] * roll_rows(values, -1)


HALVES = (slice(0, 128), slice(128, 256))


def freq_forward_kernel(own_ref, halo_ref, weight_ref, taps_ref, gain_ref, own_out, halo_out, hidden_out):
    gain = gain_ref[...]
    for pair_ref, out_ref in ((own_ref, own_out), (halo_ref, halo_out)):
        features = pair_ref[:, :64].astype(F32)
        normed = (features * inverse_norm(features) * gain).astype(BF)
        mixed = features
        for lanes in HALVES:
            hidden = nt(normed, weight_ref[lanes, :64])
            if out_ref is own_out:
                hidden_out[:, lanes] = hidden
            drive = bins_conv(hidden, taps_ref[:, lanes])
            active = (drive * sigmoid(drive)).astype(BF)
            mixed = mixed + nn(active, weight_ref[lanes, 64:])
        out_ref[:, :64] = mixed.astype(BF)
        out_ref[:, 64:] = pair_ref[:, 64:]


def freq_forward(pair, halo, weights, taps, gain):
    rows = pair.shape[0]
    return pl.pallas_call(
        freq_forward_kernel,
        out_shape=(
            jax.ShapeDtypeStruct((rows, 128), BF),
            jax.ShapeDtypeStruct((rows, 128), BF),
            jax.ShapeDtypeStruct((rows, 256), F32),
        ),
        name="freq_forward",
    )(pair, halo, weights, taps, gain)


def freq_backward_kernel(flag_ref, pair_ref, hidden_ref, back_ref, weight_ref, taps_ref, gain_ref, out_ref, grad_ref, tap_ref, gain_out):
    gain = gain_ref[...]
    row = lax.broadcasted_iota(jnp.int32, (ROWS, 1), 0)
    upper = LEAD + 64 + flag_ref[0]
    one = jnp.where((row >= LEAD) & (row < upper), 1.0, 0.0).astype(F32)
    own = jnp.concatenate([one] * FR, axis=0)
    features = pair_ref[:, :64].astype(F32)
    scale = inverse_norm(features)
    grad = back_ref[:, 64:]
    grad_wide = grad.astype(F32)
    grad_own = (grad_wide * own).astype(BF)
    normed = (features * scale * gain * own).astype(BF)
    d_normed = None
    for lanes in HALVES:
        taps = taps_ref[:, lanes]
        hidden = hidden_ref[:, lanes]
        before, after = roll_rows(hidden, 1), roll_rows(hidden, -1)
        drive = taps[0:1] * before + taps[1:2] * hidden + taps[2:3] * after
        gate = sigmoid(drive)
        active = drive * gate
        slope = gate + active * (1.0 - gate)
        grad_ref[lanes, :64] = tn(active.astype(BF), grad_own)
        d_drive = nt(grad, weight_ref[lanes, 64:]) * slope
        d_own = d_drive * own
        tap_ref[0:1, lanes] = jnp.sum(d_own * before, axis=0, keepdims=True)
        tap_ref[1:2, lanes] = jnp.sum(d_own * hidden, axis=0, keepdims=True)
        tap_ref[2:3, lanes] = jnp.sum(d_own * after, axis=0, keepdims=True)
        d_hidden = (
            taps[0:1] * roll_rows(d_drive, -1) + taps[1:2] * d_drive + taps[2:3] * roll_rows(d_drive, 1)
        ).astype(BF)
        grad_ref[lanes, 64:] = tn(d_hidden, normed)
        part = nn(d_hidden, weight_ref[lanes, :64])
        d_normed = part if d_normed is None else d_normed + part
    gain_out[...] = jnp.sum(d_normed * features * (scale * own), axis=0, keepdims=True)
    out_ref[:, :64] = back_ref[:, :64]
    out_ref[:, 64:] = (grad_wide + norm_back(d_normed, features, scale, gain)).astype(BF)


def freq_backward(pair, hidden, back, weights, taps, gain, last_plane):
    vmem = pl.BlockSpec(memory_space=pltpu.VMEM)
    return pl.pallas_call(
        freq_backward_kernel,
        out_shape=(
            jax.ShapeDtypeStruct(pair.shape, BF),
            jax.ShapeDtypeStruct((256, 128), F32),
            jax.ShapeDtypeStruct((3, 256), F32),
            jax.ShapeDtypeStruct((1, 64), F32),
        ),
        in_specs=[pl.BlockSpec(memory_space=pltpu.SMEM)] + [vmem] * 6,
        name="freq_backward",
    )(last_plane.reshape(1), pair, hidden, back, weights, taps, gain)


def turned(tiles):
    return jnp.concatenate(
        [roll_rows(tiles[8 * i : 8 * i + 8], 4) for i in range(tiles.shape[0] // 8)], axis=0
    )


def groups_on(values, count):
    if count > 0:
        return jnp.concatenate([values[8 * count :], turned(values[: 8 * count])], axis=0)
    base = values.shape[0] + 8 * count
    return jnp.concatenate([turned(values[base:]), values[:base]], axis=0)


def later(values, spacing, place):
    if spacing == 1:
        return jnp.where(place == 3, roll_rows(groups_on(values, 1), 3), roll_rows(values, -1))
    return groups_on(values, spacing // FR)


def earlier(values, spacing, place):
    if spacing == 1:
        return jnp.where(place == 0, roll_rows(groups_on(values, -1), -3), roll_rows(values, 1))
    return groups_on(values, -(spacing // FR))


def own_rows(values):
    tiles = values.reshape(values.shape[0] // 8, 8, values.shape[1])
    return jnp.sum(jnp.sum(tiles, axis=0)[:4], axis=0, keepdims=True)


def time_kernel(flag_ref, pair_ref, marks_ref, weight_ref, taps_ref, gain_ref, out_ref, grad_ref, tap_ref, gain_out):
    slot = pl.program_id(0)
    share = jnp.where((slot < 2) | (flag_ref[0] > 0), 1.0, 0.0).astype(F32)

    @pl.when(slot == 0)
    def _():
        grad_ref[...] = jnp.zeros_like(grad_ref)
        tap_ref[...] = jnp.zeros_like(tap_ref)
        gain_out[...] = jnp.zeros_like(gain_out)

    pair = pair_ref[:, 0].astype(F32).reshape(256, 128)
    gain = gain_ref[...]
    valid, inside = marks_ref[:, 0:1], marks_ref[:, 1:2]
    spot = lax.broadcasted_iota(jnp.int32, (256, 1), 0)
    counted = jnp.where((spot & 7) < 4, share, 0.0).astype(F32)
    place = lax.broadcasted_iota(jnp.int32, (256, 128), 0) & 3
    features, grad_wide = pair[:, :64], pair[:, 64:]
    grad = grad_wide.astype(BF)
    grad_own = (grad_wide * counted).astype(BF)
    scale = inverse_norm(features)
    normed = features * scale * gain
    normed_own = (normed * counted).astype(BF)
    normed = normed.astype(BF)
    mixed, d_normed = features, None
    for lanes in HALVES:
        weight_in, weight_out = weight_ref[lanes, :64], weight_ref[lanes, 64:]
        state = nt(normed, weight_in) * valid
        states, slopes = [], []
        for layer in range(3):
            spacing = (1, 4, 16)[layer]
            row = taps_ref[3 * layer : 3 * layer + 3, lanes]
            drive = (
                row[0:1] * earlier(state, spacing, place) + row[1:2] * state + row[2:3] * later(state, spacing, place)
            )
            gate = sigmoid(drive)
            active = drive * gate
            states.append(state)
            slopes.append(gate + active * (1.0 - gate))
            state = state + active
            if layer < 2:
                state = state * inside
        top = state.astype(BF)
        mixed = mixed + nn(top, weight_out)
        grad_ref[lanes, :64] += tn(top, grad_own)
        d_state = nt(grad, weight_out)
        for layer in reversed(range(3)):
            spacing = (1, 4, 16)[layer]
            row = taps_ref[3 * layer : 3 * layer + 3, lanes]
            d_drive = d_state * slopes[layer]
            if layer < 2:
                d_drive = d_drive * inside
            held = states[layer]
            for j, moved in enumerate((earlier(held, spacing, place), held, later(held, spacing, place))):
                tap_ref[3 * layer + j : 3 * layer + j + 1, lanes] += own_rows(d_drive * moved) * share
            d_state = d_state + (
                row[0:1] * later(d_drive, spacing, place)
                + row[1:2] * d_drive
                + row[2:3] * earlier(d_drive, spacing, place)
            )
        d_pre = (d_state * valid).astype(BF)
        grad_ref[lanes, 64:] += tn(d_pre, normed_own)
        part = nn(d_pre, weight_in)
        d_normed = part if d_normed is None else d_normed + part
    gain_out[...] += own_rows(d_normed * features * scale) * share
    d_one = grad_wide + norm_back(d_normed, features, scale, gain)
    out_ref[:, 0] = jnp.concatenate([mixed, d_one], axis=1).reshape(32, 8, 128).astype(BF)


def time_path(bands, marks, weights, taps, gain, flag):
    whole = lambda shape: pl.BlockSpec(shape, lambda slot: (0, 0))
    slots = pl.BlockSpec((32, 1, 8, 128), lambda slot: (0, slot, 0, 0))
    return pl.pallas_call(
        time_kernel,
        grid=(3,),
        out_shape=(
            jax.ShapeDtypeStruct((32, 3, 8, 128), BF),
            jax.ShapeDtypeStruct((256, 128), F32),
            jax.ShapeDtypeStruct((9, 256), F32),
            jax.ShapeDtypeStruct((1, 64), F32),
        ),
        in_specs=[
            pl.BlockSpec(memory_space=pltpu.SMEM),
            slots,
            whole((256, 2)),
            whole((256, 128)),
            whole((9, 256)),
            whole((1, 64)),
        ],
        out_specs=(slots, whole((256, 128)), whole((9, 256)), whole((1, 64))),
        name="time_path",
    )(flag.reshape(1), bands, marks, weights, taps, gain)


def plane_rows(values, plane):
    frames, width = values.shape
    padded = jnp.pad(values, ((0, 0), (LEAD * 64, (ROWS - LEAD + 192) * 64 - width)))
    cut = lax.dynamic_slice(padded, (0, plane * 4096), (frames, ROWS * 64))
    return cut.reshape(frames * ROWS, 64)


def begin(signal, cotangent, freq_in, freq_taps, freq_out, time_in, time_taps, time_out, plane):
    pair = jnp.concatenate([plane_rows(signal, plane), plane_rows(cotangent, plane)], axis=1)
    taps = jnp.concatenate([freq_taps, time_taps.reshape(9, 64)], axis=0)
    high = lax.reduce_precision(taps, 8, 7)
    low = lax.reduce_precision(taps - high, 8, 7)
    packed = jnp.concatenate(
        [
            jnp.concatenate([freq_in.T, freq_out], axis=1),
            jnp.concatenate([time_in.T, time_out], axis=1),
            jnp.concatenate([high, low], axis=1).astype(BF),
            jnp.zeros((4, 128), BF),
        ],
        axis=0,
    )
    return pair, packed


def unpack(gathered):
    freq_w = gathered[:, :64].reshape(256, 128)
    time_w = gathered[:, 64:128].reshape(256, 128)
    tap_rows = gathered[:, 128:140].astype(F32)
    taps = (tap_rows[:, :, :64] + tap_rows[:, :, 64:]).transpose(1, 0, 2).reshape(12, 256)
    return freq_w, time_w, taps


def to_bands(own, halo):
    both = jnp.concatenate([own.reshape(FR, ROWS, 128), halo.reshape(FR, ROWS, 128)], axis=0)
    mine = both[:, LEAD : LEAD + 64].reshape(2 * FR, 32, 2, 128).transpose(1, 2, 0, 3)
    edge = jnp.stack([both[:, LEAD - 1], both[:, LEAD + 64]], axis=0)[:, None]
    edge = jnp.pad(edge, ((0, 30), (0, 0), (0, 0), (0, 0)))
    return jnp.concatenate([mine, edge], axis=1).reshape(32, 24, 128)


def frame_marks(counts, x_at):
    by_plane = jnp.pad(counts.reshape(4, 32), ((1, 1), (0, 0)))
    window = lax.dynamic_slice(by_plane, (x_at, 0), (3, 32))
    spot = jnp.arange(32)
    halo_count = jnp.where(spot >= 16, window[0], window[2])
    halo_in = jnp.where(spot >= 16, (spot >= 21) & (x_at > 0), (spot <= 10) & (x_at < 3))
    limit = jnp.stack([window[1], halo_count], axis=1)
    valid = (jnp.arange(4) < limit[:, :, None]) & jnp.stack([spot >= 0, halo_in], axis=1)[:, :, None]
    inside = jnp.stack([spot >= 0, halo_in], axis=1)[:, :, None] & (jnp.arange(4) >= 0)
    return jnp.stack([valid.reshape(256), inside.reshape(256)], axis=1).astype(F32)


def to_frames(bands):
    return bands[:, :, :4].reshape(32, 12, 128)


def from_frames(arrived, plane):
    rows = arrived.reshape(32, 3, FR, 128)
    mine = rows[:, :2].transpose(2, 0, 1, 3).reshape(FR, 64, 128)
    left = jnp.where(plane > 0, rows[0, 2], jnp.zeros((), BF))[:, None]
    right = rows[1, 2][:, None]
    return jnp.concatenate(
        [jnp.zeros((FR, LEAD - 1, 128), BF), left, mine, right, jnp.zeros((FR, ROWS - LEAD - 65, 128), BF)], axis=1
    ).reshape(FR * ROWS, 128)


def to_planes(done, freq_w, freq_t, freq_g, time_w, time_t, time_g):
    rows = done.reshape(FR, ROWS, 128)[:, LEAD : LEAD + 65].reshape(FR * 65, 128)
    rows = jnp.broadcast_to(rows, (4, FR * 65, 128))
    taps = jnp.concatenate([freq_t, time_t], axis=0).reshape(12, 4, 64).transpose(1, 0, 2).reshape(4, 6, 128)
    gains = jnp.broadcast_to(jnp.concatenate([freq_g, time_g], axis=1), (4, 1, 128))
    grads = jnp.concatenate(
        [freq_w.reshape(4, 64, 128), time_w.reshape(4, 64, 128), taps, gains, jnp.zeros((4, 1, 128), F32)], axis=1
    )
    return jnp.concatenate([rows, grads.astype(BF)], axis=1)


def outputs_of(arrived):
    rows = arrived[:, : FR * 65].reshape(4, FR, 65, 128)
    whole = jnp.concatenate([rows[0, :, :64], rows[1, :, :64], rows[2, :, :64], rows[3]], axis=1)
    return whole[:, :, :64].reshape(FR, -1), whole[:, :, 64:].reshape(FR, -1)


def grads_of(total, scale):
    total = total * scale
    taps = total[128:134].reshape(12, 64)
    return (
        total[134, :64],
        total[:64, 64:].T,
        taps[:3],
        total[:64, :64],
        total[134, 64:],
        total[64:128, 64:].T,
        taps[3:].reshape(3, 3, 64),
        total[64:128, :64],
    )


def halo_pairs():
    pairs = []
    for x_at in range(4):
        for spot in range(32):
            if spot <= 10 and x_at < 3:
                pairs.append(((x_at + 1) * 32 + spot, x_at * 32 + spot))
            if spot >= 21 and x_at > 0:
                pairs.append(((x_at - 1) * 32 + spot, x_at * 32 + spot))
    return pairs


SEQ = ("x", "z", "core")


def exchange(values, axes):
    return lax.all_to_all(values, axes, 0, 0)


def shards(
    signal, cotangent, counts, freq_gain, freq_in, freq_taps, freq_out, time_gain, time_in, time_taps, time_out
):
    plane = lax.axis_index("ch")
    x_at = lax.axis_index("x")
    spot = lax.axis_index(("z", "core"))
    grad_scale = 1.0 / math.sqrt(FR * 128 * (signal.shape[1] // 64))
    pair, packed = begin(signal, cotangent, freq_in, freq_taps, freq_out, time_in, time_taps, time_out, plane)
    halo = lax.ppermute(pair, SEQ, halo_pairs())
    gathered = exchange(jnp.broadcast_to(packed, (4,) + packed.shape), "ch")
    freq_w, time_w, taps = unpack(gathered)
    freq_t, time_t = taps[:3], taps[3:]
    gain_f, gain_t = freq_gain[None], time_gain[None]
    x_own, x_halo, hidden = freq_forward(pair, halo, freq_w, freq_t, gain_f)
    bands = exchange(to_bands(x_own, x_halo), ("z", "core")).reshape(32, 3, 8, 128)
    marks = frame_marks(counts, x_at)
    edge = jnp.where((plane == 3) & (spot == 1), 1, 0)
    mixed, *sums = time_path(bands, marks, time_w, time_t, gain_t, edge)
    arrived = exchange(to_frames(mixed), ("z", "core"))
    back = from_frames(arrived, plane)
    last_plane = jnp.where(plane == 3, 1, 0)
    done, grad_w, grad_t, grad_g = freq_backward(pair, hidden, back, freq_w, freq_t, gain_f, last_plane)
    planes = exchange(to_planes(done, grad_w, grad_t, grad_g, *sums), "ch")
    output, d_signal = outputs_of(planes)
    part = jnp.sum(planes[:, FR * 65 :].astype(F32), axis=0)
    part = jnp.sum(exchange(part.reshape(8, 17, 128), ("x", "core")), axis=0)
    part = jnp.sum(exchange(jnp.broadcast_to(part, (16, 17, 128)), "z"), axis=0)
    total = exchange(jnp.broadcast_to(part, (8, 17, 128)), ("x", "core")).reshape(136, 128)
    return (output, d_signal) + grads_of(total, grad_scale)


def solution(mesh):
    torus = Mesh(mesh.devices.reshape(4, 16, 2, 4), ("x", "z", "core", "ch"))
    return jax.shard_map(
        shards,
        mesh=torus,
        in_specs=(
            P(SEQ, None),
            P(SEQ, None),
            P(),
            P(),
            P(None, "ch"),
            P(None, "ch"),
            P("ch", None),
            P(),
            P(None, "ch"),
            P(None, None, "ch"),
            P("ch", None),
        ),
        out_specs=(
            P(SEQ, None),
            P(SEQ, None),
            P(),
            P(None, "ch"),
            P(None, "ch"),
            P("ch", None),
            P(),
            P(None, "ch"),
            P(None, None, "ch"),
            P("ch", None),
        ),
        check_vma=False,
    )
```

```python
import functools
import math

import jax
import jax.numpy as jnp
from jax import lax
from jax.experimental import pallas as pl
from jax.experimental.pallas import tpu as pltpu
from jax.sharding import Mesh, PartitionSpec as P

EPS = 1e-05
FR = 4
ROWS = 80
LEAD = 8
BF = jnp.bfloat16
F32 = jnp.float32


def nt(a, b):
    return lax.dot_general(a, b, (((1,), (1,)), ((), ())), preferred_element_type=F32)


def nn(a, b):
    return lax.dot_general(a, b, (((1,), (0,)), ((), ())), preferred_element_type=F32)


def tn(a, b):
    return lax.dot_general(a, b, (((0,), (0,)), ((), ())), preferred_element_type=F32)


def roll_rows(values, amount):
    return pltpu.roll(values, amount % values.shape[0], 0)


def sigmoid(values):
    return 0.5 * jnp.tanh(0.5 * values) + 0.5


def inverse_norm(features):
    return lax.rsqrt(jnp.mean(features * features, axis=-1, keepdims=True) + EPS)


def norm_back(d_normed, features, scale, gain):
    scaled = d_normed * gain
    summed = jnp.sum(scaled * features, axis=-1, keepdims=True)
    return scale * scaled - features * (scale * scale * scale * summed * (1.0 / features.shape[-1]))


def bins_conv(values, taps):
    return taps[0:1] * roll_rows(values, 1) + taps[1:2] * values + taps[2:3] * roll_rows(values, -1)


HALVES = (slice(0, 128), slice(128, 256))


def freq_forward_kernel(own_ref, halo_ref, weight_ref, taps_ref, gain_ref, own_out, halo_out, hidden_out):
    gain = gain_ref[...]
    for pair_ref, out_ref in ((own_ref, own_out), (halo_ref, halo_out)):
        features = pair_ref[...].astype(F32)
        normed = (features * inverse_norm(features) * gain).astype(BF)
        mixed = features
        for lanes in HALVES:
            hidden = nt(normed, weight_ref[lanes, :64])
            if out_ref is own_out:
                hidden_out[:, lanes] = hidden
            drive = bins_conv(hidden, taps_ref[:, lanes])
            active = (drive * sigmoid(drive)).astype(BF)
            mixed = mixed + nn(active, weight_ref[lanes, 64:])
        out_ref[...] = mixed.astype(BF)


def freq_forward(pair, halo, weights, taps, gain):
    rows = pair.shape[0]
    return pl.pallas_call(
        freq_forward_kernel,
        out_shape=(
            jax.ShapeDtypeStruct((rows, 64), BF),
            jax.ShapeDtypeStruct((rows, 64), BF),
            jax.ShapeDtypeStruct((rows, 256), F32),
        ),
        name="freq_forward",
    )(pair, halo, weights, taps, gain)


def freq_backward_kernel(flag_ref, pair_ref, hidden_ref, back_ref, weight_ref, taps_ref, gain_ref, out_ref, grad_ref, tap_ref, gain_out):
    gain = gain_ref[...]
    row = lax.broadcasted_iota(jnp.int32, (ROWS, 1), 0)
    upper = LEAD + 64 + flag_ref[0]
    one = jnp.where((row >= LEAD) & (row < upper), 1.0, 0.0).astype(F32)
    own = jnp.concatenate([one] * FR, axis=0)
    features = pair_ref[...].astype(F32)
    scale = inverse_norm(features)
    grad = back_ref[:, 64:]
    grad_wide = grad.astype(F32)
    grad_own = (grad_wide * own).astype(BF)
    normed = (features * scale * gain * own).astype(BF)
    d_normed = None
    for lanes in HALVES:
        taps = taps_ref[:, lanes]
        hidden = hidden_ref[:, lanes]
        before, after = roll_rows(hidden, 1), roll_rows(hidden, -1)
        drive = taps[0:1] * before + taps[1:2] * hidden + taps[2:3] * after
        gate = sigmoid(drive)
        active = drive * gate
        slope = gate + active * (1.0 - gate)
        grad_ref[lanes, :64] = tn(active.astype(BF), grad_own)
        d_drive = nt(grad, weight_ref[lanes, 64:]) * slope
        d_own = d_drive * own
        tap_ref[0:1, lanes] = jnp.sum(d_own * before, axis=0, keepdims=True)
        tap_ref[1:2, lanes] = jnp.sum(d_own * hidden, axis=0, keepdims=True)
        tap_ref[2:3, lanes] = jnp.sum(d_own * after, axis=0, keepdims=True)
        d_hidden = (
            taps[0:1] * roll_rows(d_drive, -1) + taps[1:2] * d_drive + taps[2:3] * roll_rows(d_drive, 1)
        ).astype(BF)
        grad_ref[lanes, 64:] = tn(d_hidden, normed)
        part = nn(d_hidden, weight_ref[lanes, :64])
        d_normed = part if d_normed is None else d_normed + part
    gain_out[...] = jnp.sum(d_normed * features * (scale * own), axis=0, keepdims=True)
    out_ref[:, :64] = back_ref[:, :64]
    out_ref[:, 64:] = (grad_wide + norm_back(d_normed, features, scale, gain)).astype(BF)


def freq_backward(pair, hidden, back, weights, taps, gain, last_plane):
    vmem = pl.BlockSpec(memory_space=pltpu.VMEM)
    return pl.pallas_call(
        freq_backward_kernel,
        out_shape=(
            jax.ShapeDtypeStruct(back.shape, BF),
            jax.ShapeDtypeStruct((256, 128), F32),
            jax.ShapeDtypeStruct((3, 256), F32),
            jax.ShapeDtypeStruct((1, 64), F32),
        ),
        in_specs=[pl.BlockSpec(memory_space=pltpu.SMEM)] + [vmem] * 6,
        name="freq_backward",
    )(last_plane.reshape(1), pair, hidden, back, weights, taps, gain)


def turned(tiles):
    return jnp.concatenate(
        [roll_rows(tiles[8 * i : 8 * i + 8], 4) for i in range(tiles.shape[0] // 8)], axis=0
    )


def groups_on(values, count):
    if count > 0:
        return jnp.concatenate([values[8 * count :], turned(values[: 8 * count])], axis=0)
    base = values.shape[0] + 8 * count
    return jnp.concatenate([turned(values[base:]), values[:base]], axis=0)


def later(values, spacing, place):
    if spacing == 1:
        return jnp.where(place == 3, roll_rows(groups_on(values, 1), 3), roll_rows(values, -1))
    return groups_on(values, spacing // FR)


def earlier(values, spacing, place):
    if spacing == 1:
        return jnp.where(place == 0, roll_rows(groups_on(values, -1), -3), roll_rows(values, 1))
    return groups_on(values, -(spacing // FR))


def own_rows(values):
    tiles = values.reshape(values.shape[0] // 8, 8, values.shape[1])
    return jnp.sum(jnp.sum(tiles, axis=0)[:4], axis=0, keepdims=True)


def one_bin(message, slot):
    if slot < 2:
        both = message[:, 0:8].astype(F32).reshape(256, 128)
        return both[:, 64 * slot : 64 * slot + 64]
    edge = message[:, 8:12].astype(F32)
    return jnp.concatenate([edge[:, :, :64], edge[:, :, 64:]], axis=1).reshape(256, 64)


def time_kernel(
    flag_ref, x_ref, cot_ref, marks_ref, weight_ref, taps_ref, gain_ref, out_ref, grad_ref, tap_ref, gain_out
):
    gain = gain_ref[...]
    valid, inside = marks_ref[:, 0:1], marks_ref[:, 1:2]
    spot = lax.broadcasted_iota(jnp.int32, (256, 1), 0)
    place = lax.broadcasted_iota(jnp.int32, (256, 128), 0) & 3
    for slot in range(3):
        share = jnp.where(flag_ref[0] > 0, 1.0, 0.0).astype(F32) if slot == 2 else 1.0

        def keep(ref, rows, lanes, value):
            if slot == 0:
                ref[rows, lanes] = value
            else:
                ref[rows, lanes] += value

        counted = jnp.where((spot & 7) < 4, share, 0.0).astype(F32)
        features, grad_wide = one_bin(x_ref, slot), one_bin(cot_ref, slot)
        grad = grad_wide.astype(BF)
        grad_own = (grad_wide * counted).astype(BF)
        scale = inverse_norm(features)
        normed = features * scale * gain
        normed_own = (normed * counted).astype(BF)
        normed = normed.astype(BF)
        mixed, d_normed = features, None
        for lanes in HALVES:
            weight_in, weight_out = weight_ref[lanes, :64], weight_ref[lanes, 64:]
            state = nt(normed, weight_in) * valid
            states, slopes = [], []
            for layer in range(3):
                spacing = (1, 4, 16)[layer]
                row = taps_ref[3 * layer : 3 * layer + 3, lanes]
                drive = (
                    row[0:1] * earlier(state, spacing, place)
                    + row[1:2] * state
                    + row[2:3] * later(state, spacing, place)
                )
                gate = sigmoid(drive)
                active = drive * gate
                states.append(state)
                slopes.append(gate + active * (1.0 - gate))
                state = state + active
                if layer < 2:
                    state = state * inside
            top = state.astype(BF)
            mixed = mixed + nn(top, weight_out)
            keep(grad_ref, lanes, slice(0, 64), tn(top, grad_own))
            d_state = nt(grad, weight_out)
            for layer in reversed(range(3)):
                spacing = (1, 4, 16)[layer]
                row = taps_ref[3 * layer : 3 * layer + 3, lanes]
                d_drive = d_state * slopes[layer]
                if layer < 2:
                    d_drive = d_drive * inside
                held = states[layer]
                for j, moved in enumerate((earlier(held, spacing, place), held, later(held, spacing, place))):
                    at = 3 * layer + j
                    keep(tap_ref, slice(at, at + 1), lanes, own_rows(d_drive * moved) * share)
                d_state = d_state + (
                    row[0:1] * later(d_drive, spacing, place)
                    + row[1:2] * d_drive
                    + row[2:3] * earlier(d_drive, spacing, place)
                )
            d_pre = (d_state * valid).astype(BF)
            keep(grad_ref, lanes, slice(64, 128), tn(d_pre, normed_own))
            part = nn(d_pre, weight_in)
            d_normed = part if d_normed is None else d_normed + part
        keep(gain_out, slice(0, 1), slice(0, 64), own_rows(d_normed * features * scale) * share)
        d_one = grad_wide + norm_back(d_normed, features, scale, gain)
        both = jnp.concatenate([mixed, d_one], axis=1).reshape(32, 8, 128)
        out_ref[:, 4 * slot : 4 * slot + 4] = both[:, :4].astype(BF)


def time_path(x_one, cot, marks, weights, taps, gain, flag):
    vmem = pl.BlockSpec(memory_space=pltpu.VMEM)
    return pl.pallas_call(
        time_kernel,
        out_shape=(
            jax.ShapeDtypeStruct((32, 12, 128), BF),
            jax.ShapeDtypeStruct((256, 128), F32),
            jax.ShapeDtypeStruct((9, 256), F32),
            jax.ShapeDtypeStruct((1, 64), F32),
        ),
        in_specs=[pl.BlockSpec(memory_space=pltpu.SMEM)] + [vmem] * 6,
        name="time_path",
    )(flag.reshape(1), x_one, cot, marks, weights, taps, gain)


def finish_kernel(scale, part_ref, freq_gain, freq_in, freq_taps, freq_out, time_gain, time_in, time_taps, time_out):
    freq_out[...] = part_ref[0:64, :64] * scale
    freq_in[...] = (part_ref[0:64, 64:] * scale).T
    time_out[...] = part_ref[64:128, :64] * scale
    time_in[...] = (part_ref[64:128, 64:] * scale).T
    gains = part_ref[134:135, :] * scale
    freq_gain[...] = gains[:, :64]
    time_gain[...] = gains[:, 64:]
    taps = part_ref[128:134, :] * scale
    for at in range(12):
        half = 64 * (at % 2)
        row = taps[at // 2 : at // 2 + 1, half : half + 64]
        if at < 3:
            freq_taps[at : at + 1, :] = row
        else:
            time_taps[at - 3 : at - 2, :] = row


def finish(total, scale):
    shape = lambda *dims: jax.ShapeDtypeStruct(dims, F32)
    got = pl.pallas_call(
        functools.partial(finish_kernel, scale),
        out_shape=(
            shape(1, 64),
            shape(64, 64),
            shape(3, 64),
            shape(64, 64),
            shape(1, 64),
            shape(64, 64),
            shape(9, 64),
            shape(64, 64),
        ),
        name="finish",
    )(total)
    return (got[0][0], got[1], got[2], got[3], got[4][0], got[5], got[6].reshape(3, 3, 64), got[7])


def plane_lanes(values, plane):
    frames, width = values.shape
    padded = jnp.pad(values, ((0, 0), (LEAD * 64, (ROWS - LEAD + 192) * 64 - width)))
    return lax.dynamic_slice(padded, (0, plane * 4096), (frames, ROWS * 64))


def pack(freq_in, freq_taps, freq_out, time_in, time_taps, time_out):
    taps = jnp.concatenate([freq_taps, time_taps.reshape(9, 64)], axis=0)
    high = lax.reduce_precision(taps, 8, 7)
    low = lax.reduce_precision(taps - high, 8, 7)
    packed = jnp.concatenate(
        [
            jnp.concatenate([freq_in.T, freq_out], axis=1),
            jnp.concatenate([time_in.T, time_out], axis=1),
            jnp.concatenate([high, low], axis=1).astype(BF),
            jnp.zeros((4, 128), BF),
        ],
        axis=0,
    )
    return packed


def unpack(gathered):
    freq_w = gathered[:, :64].reshape(256, 128)
    time_w = gathered[:, 64:128].reshape(256, 128)
    tap_rows = gathered[:, 128:140].astype(F32)
    taps = (tap_rows[:, :, :64] + tap_rows[:, :, 64:]).transpose(1, 0, 2).reshape(12, 256)
    return freq_w, time_w, taps


def message(mine, edge):
    edge = jnp.concatenate([edge[:, :FR], edge[:, FR:]], axis=2)
    return jnp.concatenate([mine, jnp.pad(edge, ((0, 30), (0, 0), (0, 0)))], axis=1)


def lanes_message(own, halo):
    both = jnp.concatenate([own, halo], axis=0)
    mine = both[:, LEAD * 64 : LEAD * 64 + 4096].reshape(2 * FR, 32, 128).transpose(1, 0, 2)
    edge = jnp.stack([both[:, LEAD * 64 - 64 : LEAD * 64], both[:, LEAD * 64 + 4096 : LEAD * 64 + 4160]], axis=0)
    return message(mine, edge)


def rows_message(own, halo):
    both = jnp.concatenate([own.reshape(FR, ROWS, 64), halo.reshape(FR, ROWS, 64)], axis=0)
    mine = both[:, LEAD : LEAD + 64].reshape(2 * FR, 32, 128).transpose(1, 0, 2)
    return message(mine, jnp.stack([both[:, LEAD - 1], both[:, LEAD + 64]], axis=0))


def frame_marks(counts, x_at):
    by_plane = jnp.pad(counts.reshape(4, 32), ((1, 1), (0, 0)))
    window = lax.dynamic_slice(by_plane, (x_at, 0), (3, 32))
    spot = jnp.arange(32)
    halo_count = jnp.where(spot >= 16, window[0], window[2])
    halo_in = jnp.where(spot >= 16, (spot >= 21) & (x_at > 0), (spot <= 10) & (x_at < 3))
    limit = jnp.stack([window[1], halo_count], axis=1)
    valid = (jnp.arange(4) < limit[:, :, None]) & jnp.stack([spot >= 0, halo_in], axis=1)[:, :, None]
    inside = jnp.stack([spot >= 0, halo_in], axis=1)[:, :, None] & (jnp.arange(4) >= 0)
    return jnp.stack([valid.reshape(256), inside.reshape(256)], axis=1).astype(F32)


def from_frames(arrived, plane):
    rows = arrived.reshape(32, 3, FR, 128)
    mine = rows[:, :2].transpose(2, 0, 1, 3).reshape(FR, 64, 128)
    left = jnp.where(plane > 0, rows[0, 2], jnp.zeros((), BF))[:, None]
    right = rows[1, 2][:, None]
    return jnp.concatenate(
        [jnp.zeros((FR, LEAD - 1, 128), BF), left, mine, right, jnp.zeros((FR, ROWS - LEAD - 65, 128), BF)], axis=1
    ).reshape(FR * ROWS, 128)


def own_part(done):
    return done.reshape(FR, ROWS, 128)[:, LEAD : LEAD + 65].reshape(FR * 65, 128)


def grad_parts(freq_w, freq_t, freq_g, time_w, time_t, time_g):
    taps = jnp.concatenate([freq_t, time_t], axis=0).reshape(12, 4, 64).transpose(1, 0, 2).reshape(4, 6, 128)
    gains = jnp.broadcast_to(jnp.concatenate([freq_g, time_g], axis=1), (4, 1, 128))
    grads = jnp.concatenate(
        [freq_w.reshape(4, 64, 128), time_w.reshape(4, 64, 128), taps, gains, jnp.zeros((4, 1, 128), F32)], axis=1
    )
    return grads.astype(BF).reshape(4, 8, 17, 128).transpose(1, 0, 2, 3).reshape(32, 17, 128)


def outputs_of(arrived):
    rows = arrived.reshape(4, FR, 65, 128)
    whole = jnp.concatenate([rows[0, :, :64], rows[1, :, :64], rows[2, :, :64], rows[3]], axis=1)
    return whole[:, :, :64].reshape(FR, -1), whole[:, :, 64:].reshape(FR, -1)


def halo_pairs():
    pairs = []
    for x_at in range(4):
        for spot in range(32):
            if spot <= 10 and x_at < 3:
                pairs.append(((x_at + 1) * 32 + spot, x_at * 32 + spot))
            if spot >= 21 and x_at > 0:
                pairs.append(((x_at - 1) * 32 + spot, x_at * 32 + spot))
    return pairs


SEQ = ("x", "z", "core")


def exchange(values, axes):
    return lax.all_to_all(values, axes, 0, 0)


def shards(
    signal, cotangent, counts, freq_gain, freq_in, freq_taps, freq_out, time_gain, time_in, time_taps, time_out
):
    plane = lax.axis_index("ch")
    x_at = lax.axis_index("x")
    spot = lax.axis_index(("z", "core"))
    grad_scale = 1.0 / math.sqrt(FR * 128 * (signal.shape[1] // 64))
    lanes = jnp.stack([plane_lanes(signal, plane), plane_lanes(cotangent, plane)], axis=0)
    halo = lax.ppermute(lanes, SEQ, halo_pairs())
    packed = pack(freq_in, freq_taps, freq_out, time_in, time_taps, time_out)
    gathered = exchange(jnp.broadcast_to(packed, (4,) + packed.shape), "ch")
    band_cot = exchange(lanes_message(lanes[1], halo[1]), ("z", "core"))
    freq_w, time_w, taps = unpack(gathered)
    freq_t, time_t = taps[:3], taps[3:]
    gain_f, gain_t = freq_gain[None], time_gain[None]
    x_rows, x_halo = lanes[0].reshape(FR * ROWS, 64), halo[0].reshape(FR * ROWS, 64)
    own, beside, hidden = freq_forward(x_rows, x_halo, freq_w, freq_t, gain_f)
    band_x = exchange(rows_message(own, beside), ("z", "core"))
    marks = frame_marks(counts, x_at)
    edge = jnp.where((plane == 3) & (spot == 1), 1, 0)
    mixed, *sums = time_path(band_x, band_cot, marks, time_w, time_t, gain_t, edge)
    back = from_frames(exchange(mixed, ("z", "core")), plane)
    last_plane = jnp.where(plane == 3, 1, 0)
    done, *freq_sums = freq_backward(x_rows, hidden, back, freq_w, freq_t, gain_f, last_plane)
    part = exchange(grad_parts(*freq_sums, *sums), ("x", "core", "ch"))
    planes = exchange(jnp.broadcast_to(own_part(done), (4, FR * 65, 128)), "ch")
    part = jnp.sum(part.astype(F32), axis=0).astype(BF)
    part = jnp.sum(exchange(jnp.broadcast_to(part, (16, 17, 128)), "z").astype(F32), axis=0)
    total = exchange(jnp.broadcast_to(part, (8, 17, 128)), ("x", "core")).reshape(136, 128)
    return outputs_of(planes) + finish(total, grad_scale)


def solution(mesh):
    torus = Mesh(mesh.devices.reshape(4, 16, 2, 4), ("x", "z", "core", "ch"))
    return jax.shard_map(
        shards,
        mesh=torus,
        in_specs=(
            P(SEQ, None),
            P(SEQ, None),
            P(),
            P(),
            P(None, "ch"),
            P(None, "ch"),
            P("ch", None),
            P(),
            P(None, "ch"),
            P(None, None, "ch"),
            P("ch", None),
        ),
        out_specs=(
            P(SEQ, None),
            P(SEQ, None),
            P(),
            P(None, "ch"),
            P(None, "ch"),
            P("ch", None),
            P(),
            P(None, "ch"),
            P(None, None, "ch"),
            P("ch", None),
        ),
        check_vma=False,
    )
```

```python
import functools
import math

import jax
import jax.numpy as jnp
from jax import lax
from jax.experimental import pallas as pl
from jax.experimental.pallas import tpu as pltpu
from jax.sharding import Mesh, PartitionSpec as P

EPS = 1e-05
FR = 4
ROWS = 80
LEAD = 8
BF = jnp.bfloat16
F32 = jnp.float32


def nt(a, b):
    return lax.dot_general(a, b, (((1,), (1,)), ((), ())), preferred_element_type=F32)


def nn(a, b):
    return lax.dot_general(a, b, (((1,), (0,)), ((), ())), preferred_element_type=F32)


def tn(a, b):
    return lax.dot_general(a, b, (((0,), (0,)), ((), ())), preferred_element_type=F32)


def roll_rows(values, amount):
    return pltpu.roll(values, amount % values.shape[0], 0)


def sigmoid(values):
    return 0.5 * jnp.tanh(0.5 * values) + 0.5


def inverse_norm(features):
    return lax.rsqrt(jnp.mean(features * features, axis=-1, keepdims=True) + EPS)


def norm_back(d_normed, features, scale, gain):
    scaled = d_normed * gain
    summed = jnp.sum(scaled * features, axis=-1, keepdims=True)
    return scale * scaled - features * (scale * scale * scale * summed * (1.0 / features.shape[-1]))


def bins_conv(values, taps):
    return taps[0:1] * roll_rows(values, 1) + taps[1:2] * values + taps[2:3] * roll_rows(values, -1)


HALVES = (slice(0, 128), slice(128, 256))


def half_weights(gathered_ref, half, first):
    return jnp.concatenate([gathered_ref[2 * half + i, first : first + 64, :] for i in range(2)], axis=0)


def half_taps(gathered_ref, half, first, count):
    parts = []
    for i in range(2):
        both = gathered_ref[2 * half + i, 128:144, :].astype(F32)
        parts.append((both[:, :64] + both[:, 64:])[first : first + count])
    return jnp.concatenate(parts, axis=1)


def pack_kernel(freq_in, freq_taps, freq_out, time_in, time_taps, time_out, packed_ref):
    taps = jnp.concatenate(
        [freq_taps[...]] + [time_taps[k] for k in range(3)] + [jnp.zeros((4, 64), F32)], axis=0
    )
    high = taps.astype(BF).astype(F32)
    low = taps - high
    turn = lambda ref: ref[...].astype(F32).T.astype(BF)
    freq_w = jnp.concatenate([turn(freq_in), freq_out[...]], axis=1)
    time_w = jnp.concatenate([turn(time_in), time_out[...]], axis=1)
    tap_w = jnp.concatenate([high, low], axis=1).astype(BF)
    for peer in range(4):
        packed_ref[peer, 0:64, :] = freq_w
        packed_ref[peer, 64:128, :] = time_w
        packed_ref[peer, 128:144, :] = tap_w


def pack(*weights):
    return pl.pallas_call(
        pack_kernel, out_shape=jax.ShapeDtypeStruct((4, 144, 128), BF), name="pack"
    )(*weights)


def freq_forward_kernel(
    own_ref, halo_ref, cot_ref, cot_edge_ref, gathered_ref, gain_ref, out_ref, hidden_out, rows_ref, tiles_ref
):
    gain = gain_ref[...]
    edges = []
    for part, pair_ref in enumerate((own_ref, halo_ref)):
        features = pair_ref[...].astype(F32)
        normed = (features * inverse_norm(features) * gain).astype(BF)
        mixed = features
        for half, lanes in enumerate(HALVES):
            weights = half_weights(gathered_ref, half, 0)
            hidden = nt(normed, weights[:, :64])
            if part == 0:
                hidden_out[:, lanes] = hidden
            drive = bins_conv(hidden, half_taps(gathered_ref, half, 0, 3))
            active = (drive * sigmoid(drive)).astype(BF)
            mixed = mixed + nn(active, weights[:, 64:])
        rows_ref[...] = mixed
        for f in range(FR):
            even = rows_ref[pl.ds(f * ROWS + LEAD, 32, stride=2), :]
            odd = rows_ref[pl.ds(f * ROWS + LEAD + 1, 32, stride=2), :]
            tiles_ref[pl.ds(FR * part + f, 32, stride=8), :] = jnp.concatenate([even, odd], axis=1)
        for bin_row in (LEAD - 1, LEAD + 64):
            edges.append(
                jnp.concatenate([mixed[f * ROWS + bin_row : f * ROWS + bin_row + 1] for f in range(FR)], axis=0)
            )
    out_ref[:, 0:8, :] = tiles_ref[...].reshape(32, 8, 128).astype(BF)
    out_ref[:, 8:16, :] = cot_ref[...]
    out_ref[2:32, 16:24, :] = jnp.zeros((30, 8, 128), BF)
    for side in range(2):
        x_edge = jnp.concatenate([edges[side], edges[2 + side]], axis=1)
        out_ref[side, 16:24, :] = jnp.concatenate([x_edge, cot_edge_ref[side].astype(F32)], axis=0).astype(BF)


def freq_forward(pair, halo, cot, cot_edge, gathered, gain):
    rows = pair.shape[0]
    return pl.pallas_call(
        freq_forward_kernel,
        out_shape=(jax.ShapeDtypeStruct((32, 24, 128), BF), jax.ShapeDtypeStruct((rows, 256), F32)),
        scratch_shapes=[pltpu.VMEM((rows, 64), F32), pltpu.VMEM((256, 128), F32)],
        name="freq_forward",
    )(pair, halo, cot, cot_edge, gathered, gain)


def freq_backward_kernel(
    flag_ref,
    pair_ref,
    hidden_ref,
    arrived_ref,
    gathered_ref,
    gain_ref,
    time_w_ref,
    time_t_ref,
    time_g_ref,
    out_ref,
    tiles_ref,
    back_ref,
):
    gain = gain_ref[...]
    spread = jnp.concatenate([arrived_ref[...].astype(F32), jnp.zeros((32, 4, 128), F32)], axis=1)
    tiles_ref[...] = spread.reshape(512, 128)
    back_ref[...] = jnp.zeros_like(back_ref)
    left = flag_ref[1].astype(F32)
    for f in range(FR):
        back_ref[pl.ds(f * ROWS + LEAD, 32, stride=2), :] = tiles_ref[pl.ds(f, 32, stride=16), :]
        back_ref[pl.ds(f * ROWS + LEAD + 1, 32, stride=2), :] = tiles_ref[pl.ds(FR + f, 32, stride=16), :]
        back_ref[f * ROWS + LEAD - 1 : f * ROWS + LEAD, :] = tiles_ref[8 + f : 9 + f, :] * left
        back_ref[f * ROWS + LEAD + 64 : f * ROWS + LEAD + 65, :] = tiles_ref[24 + f : 25 + f, :]
    row = lax.broadcasted_iota(jnp.int32, (ROWS, 1), 0)
    upper = LEAD + 64 + flag_ref[0]
    one = jnp.where((row >= LEAD) & (row < upper), 1.0, 0.0).astype(F32)
    own = jnp.concatenate([one] * FR, axis=0)
    features = pair_ref[...].astype(F32)
    scale = inverse_norm(features)
    output, grad_wide = back_ref[:, :64], back_ref[:, 64:]
    grad = grad_wide.astype(BF)
    grad_own = (grad_wide * own).astype(BF)
    normed = (features * scale * gain * own).astype(BF)
    d_normed = None
    tap_halves = []
    for half, lanes in enumerate(HALVES):
        weights = half_weights(gathered_ref, half, 0)
        taps = half_taps(gathered_ref, half, 0, 3)
        hidden = hidden_ref[:, lanes]
        before, after = roll_rows(hidden, 1), roll_rows(hidden, -1)
        drive = taps[0:1] * before + taps[1:2] * hidden + taps[2:3] * after
        gate = sigmoid(drive)
        active = drive * gate
        slope = gate + active * (1.0 - gate)
        grad_out = tn(active.astype(BF), grad_own)
        d_drive = nt(grad, weights[:, 64:]) * slope
        d_own = d_drive * own
        tap_halves.append(
            [jnp.sum(d_own * moved, axis=0, keepdims=True) for moved in (before, hidden, after)]
        )
        d_hidden = (
            taps[0:1] * roll_rows(d_drive, -1) + taps[1:2] * d_drive + taps[2:3] * roll_rows(d_drive, 1)
        ).astype(BF)
        grad_in = tn(d_hidden, normed)
        both = jnp.concatenate([grad_out, grad_in], axis=1).astype(BF)
        for i in range(2):
            out_ref[2 * half + i, 288:352, :] = both[64 * i : 64 * i + 64]
        part = nn(d_hidden, weights[:, :64])
        d_normed = part if d_normed is None else d_normed + part
    freq_g = jnp.sum(d_normed * features * (scale * own), axis=0, keepdims=True)
    d_signal = grad_wide + norm_back(d_normed, features, scale, gain)
    done = jnp.concatenate([output, d_signal], axis=1)
    done = jnp.concatenate([done[f * ROWS + LEAD : (f + 1) * ROWS] for f in range(FR)], axis=0).astype(BF)
    gains = jnp.concatenate([freq_g, time_g_ref[...]], axis=1)
    for peer in range(4):
        half, at = peer // 2, 64 * (peer % 2)
        rows = [tap[:, at : at + 64] for tap in tap_halves[half]]
        rows.append(time_t_ref[:, 64 * peer : 64 * peer + 64])
        taps = jnp.concatenate(rows, axis=0)
        taps = jnp.concatenate([taps, jnp.zeros((12, 64), F32)], axis=1)
        out_ref[peer, 0:288, :] = done
        out_ref[peer, 352:416, :] = time_w_ref[64 * peer : 64 * peer + 64, :].astype(BF)
        out_ref[peer, 416:432, :] = jnp.concatenate([taps, gains, jnp.zeros((3, 128), F32)], axis=0).astype(BF)


def freq_backward(pair, hidden, arrived, gathered, gain, flags, sums):
    vmem = pl.BlockSpec(memory_space=pltpu.VMEM)
    return pl.pallas_call(
        freq_backward_kernel,
        out_shape=jax.ShapeDtypeStruct((4, 432, 128), BF),
        in_specs=[pl.BlockSpec(memory_space=pltpu.SMEM)] + [vmem] * 8,
        scratch_shapes=[pltpu.VMEM((512, 128), F32), pltpu.VMEM((FR * ROWS, 128), F32)],
        name="freq_backward",
    )(flags, pair, hidden, arrived, gathered, gain, *sums)


def turned(tiles):
    return jnp.concatenate(
        [roll_rows(tiles[8 * i : 8 * i + 8], 4) for i in range(tiles.shape[0] // 8)], axis=0
    )


def groups_on(values, count):
    if count > 0:
        return jnp.concatenate([values[8 * count :], turned(values[: 8 * count])], axis=0)
    base = values.shape[0] + 8 * count
    return jnp.concatenate([turned(values[base:]), values[:base]], axis=0)


def later(values, spacing, place):
    if spacing == 1:
        return jnp.where(place == 3, roll_rows(groups_on(values, 1), 3), roll_rows(values, -1))
    return groups_on(values, spacing // FR)


def earlier(values, spacing, place):
    if spacing == 1:
        return jnp.where(place == 0, roll_rows(groups_on(values, -1), -3), roll_rows(values, 1))
    return groups_on(values, -(spacing // FR))


def own_rows(values):
    tiles = values.reshape(values.shape[0] // 8, 8, values.shape[1])
    return jnp.sum(jnp.sum(tiles, axis=0)[:4], axis=0, keepdims=True)


def one_bin(message_ref, first, slot):
    if slot < 2:
        both = message_ref[:, 8 * first : 8 * first + 8].astype(F32).reshape(256, 128)
        return both[:, 64 * slot : 64 * slot + 64]
    edge = message_ref[:, 16:24].astype(F32)[:, 4 * first : 4 * first + 4]
    return jnp.concatenate([edge[:, :, :64], edge[:, :, 64:]], axis=1).reshape(256, 64)


def time_kernel(flag_ref, message_ref, marks_ref, gathered_ref, gain_ref, out_ref, grad_ref, tap_ref, gain_out):
    gain = gain_ref[...]
    valid, inside = marks_ref[:, 0:1], marks_ref[:, 1:2]
    spot = lax.broadcasted_iota(jnp.int32, (256, 1), 0)
    place = lax.broadcasted_iota(jnp.int32, (256, 128), 0) & 3
    for slot in range(3):
        share = jnp.where(flag_ref[0] > 0, 1.0, 0.0).astype(F32) if slot == 2 else 1.0

        def keep(ref, rows, lanes, value):
            if slot == 0:
                ref[rows, lanes] = value
            else:
                ref[rows, lanes] += value

        counted = jnp.where((spot & 7) < 4, share, 0.0).astype(F32)
        features, grad_wide = one_bin(message_ref, 0, slot), one_bin(message_ref, 1, slot)
        grad = grad_wide.astype(BF)
        grad_own = (grad_wide * counted).astype(BF)
        scale = inverse_norm(features)
        normed = features * scale * gain
        normed_own = (normed * counted).astype(BF)
        normed = normed.astype(BF)
        mixed, d_normed = features, None
        for half, lanes in enumerate(HALVES):
            weights = half_weights(gathered_ref, half, 64)
            weight_in, weight_out = weights[:, :64], weights[:, 64:]
            taps = half_taps(gathered_ref, half, 3, 9)
            state = nt(normed, weight_in) * valid
            states, slopes = [], []
            for layer in range(3):
                spacing = (1, 4, 16)[layer]
                row = taps[3 * layer : 3 * layer + 3]
                drive = (
                    row[0:1] * earlier(state, spacing, place)
                    + row[1:2] * state
                    + row[2:3] * later(state, spacing, place)
                )
                gate = sigmoid(drive)
                active = drive * gate
                states.append(state)
                slopes.append(gate + active * (1.0 - gate))
                state = state + active
                if layer < 2:
                    state = state * inside
            top = state.astype(BF)
            mixed = mixed + nn(top, weight_out)
            keep(grad_ref, lanes, slice(0, 64), tn(top, grad_own))
            d_state = nt(grad, weight_out)
            for layer in reversed(range(3)):
                spacing = (1, 4, 16)[layer]
                row = taps[3 * layer : 3 * layer + 3]
                d_drive = d_state * slopes[layer]
                if layer < 2:
                    d_drive = d_drive * inside
                held = states[layer]
                for j, moved in enumerate((earlier(held, spacing, place), held, later(held, spacing, place))):
                    at = 3 * layer + j
                    keep(tap_ref, slice(at, at + 1), lanes, own_rows(d_drive * moved) * share)
                d_state = d_state + (
                    row[0:1] * later(d_drive, spacing, place)
                    + row[1:2] * d_drive
                    + row[2:3] * earlier(d_drive, spacing, place)
                )
            d_pre = (d_state * valid).astype(BF)
            keep(grad_ref, lanes, slice(64, 128), tn(d_pre, normed_own))
            part = nn(d_pre, weight_in)
            d_normed = part if d_normed is None else d_normed + part
        keep(gain_out, slice(0, 1), slice(0, 64), own_rows(d_normed * features * scale) * share)
        d_one = grad_wide + norm_back(d_normed, features, scale, gain)
        both = jnp.concatenate([mixed, d_one], axis=1).reshape(32, 8, 128)
        out_ref[:, 4 * slot : 4 * slot + 4] = both[:, :4].astype(BF)


def time_path(message, marks, gathered, gain, flag):
    vmem = pl.BlockSpec(memory_space=pltpu.VMEM)
    return pl.pallas_call(
        time_kernel,
        out_shape=(
            jax.ShapeDtypeStruct((32, 12, 128), BF),
            jax.ShapeDtypeStruct((256, 128), F32),
            jax.ShapeDtypeStruct((9, 256), F32),
            jax.ShapeDtypeStruct((1, 64), F32),
        ),
        in_specs=[pl.BlockSpec(memory_space=pltpu.SMEM)] + [vmem] * 4,
        name="time_path",
    )(flag.reshape(1), message, marks, gathered, gain)


def finish_kernel(
    scale, part_ref, freq_gain, freq_in, freq_taps, freq_out, time_gain, time_in, time_taps, time_out, rows_ref
):
    for i in range(8):
        rows_ref[18 * i : 18 * i + 18, :] = part_ref[i] * scale
    freq_out[...] = rows_ref[0:64, :64]
    freq_in[...] = rows_ref[0:64, :][:, 64:].T
    time_out[...] = rows_ref[64:128, :64]
    time_in[...] = rows_ref[64:128, :][:, 64:].T
    gains = rows_ref[140:141, :]
    freq_gain[...] = gains[:, :64]
    time_gain[...] = gains[:, 64:]
    freq_taps[...] = rows_ref[128:131, :64]
    for k in range(3):
        time_taps[k] = rows_ref[131 + 3 * k : 134 + 3 * k, :64]


def finish(total, scale):
    shape = lambda *dims: jax.ShapeDtypeStruct(dims, F32)
    got = pl.pallas_call(
        functools.partial(finish_kernel, scale),
        out_shape=(
            shape(1, 64),
            shape(64, 64),
            shape(3, 64),
            shape(64, 64),
            shape(1, 64),
            shape(64, 64),
            shape(3, 3, 64),
            shape(64, 64),
        ),
        scratch_shapes=[pltpu.VMEM((144, 128), F32)],
        name="finish",
    )(total)
    return (got[0][0], got[1], got[2], got[3], got[4][0], got[5], got[6], got[7])


def plane_lanes(values, plane):
    frames, width = values.shape
    padded = jnp.pad(values, ((0, 0), (LEAD * 64, (ROWS - LEAD + 192) * 64 - width)))
    return lax.dynamic_slice(padded, (0, plane * 4096), (frames, ROWS * 64))


def cot_message(own, halo):
    both = jnp.concatenate([own, halo], axis=0)
    mine = both[:, LEAD * 64 : LEAD * 64 + 4096].reshape(2 * FR, 32, 128).transpose(1, 0, 2)
    edge = jnp.stack([both[:, LEAD * 64 - 64 : LEAD * 64], both[:, LEAD * 64 + 4096 : LEAD * 64 + 4160]], axis=0)
    return mine, jnp.concatenate([edge[:, :FR], edge[:, FR:]], axis=2)


def frame_marks(counts, x_at):
    by_plane = jnp.pad(counts.reshape(4, 32), ((1, 1), (0, 0)))
    window = lax.dynamic_slice(by_plane, (x_at, 0), (3, 32))
    spot = jnp.arange(32)
    halo_count = jnp.where(spot >= 16, window[0], window[2])
    halo_in = jnp.where(spot >= 16, (spot >= 21) & (x_at > 0), (spot <= 10) & (x_at < 3))
    limit = jnp.stack([window[1], halo_count], axis=1)
    valid = (jnp.arange(4) < limit[:, :, None]) & jnp.stack([spot >= 0, halo_in], axis=1)[:, :, None]
    inside = jnp.stack([spot >= 0, halo_in], axis=1)[:, :, None] & (jnp.arange(4) >= 0)
    return jnp.stack([valid.reshape(256), inside.reshape(256)], axis=1).astype(F32)


def outputs_of(arrived):
    rows = arrived[:, :288].reshape(4, FR, 72, 128)
    whole = jnp.concatenate([rows[0, :, :64], rows[1, :, :64], rows[2, :, :64], rows[3, :, :65]], axis=1)
    return whole[:, :, :64].reshape(FR, -1), whole[:, :, 64:].reshape(FR, -1)


def halo_pairs():
    pairs = []
    for x_at in range(4):
        for spot in range(32):
            if spot <= 10 and x_at < 3:
                pairs.append(((x_at + 1) * 32 + spot, x_at * 32 + spot))
            if spot >= 21 and x_at > 0:
                pairs.append(((x_at - 1) * 32 + spot, x_at * 32 + spot))
    return pairs


SEQ = ("x", "z", "core")


def exchange(values, axes):
    return lax.all_to_all(values, axes, 0, 0)


def shards(
    signal, cotangent, counts, freq_gain, freq_in, freq_taps, freq_out, time_gain, time_in, time_taps, time_out
):
    plane = lax.axis_index("ch")
    x_at = lax.axis_index("x")
    spot = lax.axis_index(("z", "core"))
    grad_scale = 1.0 / math.sqrt(FR * 128 * (signal.shape[1] // 64))
    packed = pack(freq_in, freq_taps, freq_out, time_in, time_taps, time_out)
    gathered = exchange(packed, "ch")
    lanes = jnp.stack([plane_lanes(signal, plane), plane_lanes(cotangent, plane)], axis=0)
    halo = lax.ppermute(lanes, SEQ, halo_pairs())
    gain_f, gain_t = freq_gain[None], time_gain[None]
    x_rows, x_halo = lanes[0].reshape(FR * ROWS, 64), halo[0].reshape(FR * ROWS, 64)
    message, hidden = freq_forward(x_rows, x_halo, *cot_message(lanes[1], halo[1]), gathered, gain_f)
    bands = exchange(message, ("z", "core"))
    marks = frame_marks(counts, x_at)
    edge = jnp.where((plane == 3) & (spot == 1), 1, 0)
    mixed, *sums = time_path(bands, marks, gathered, gain_t, edge)
    arrived = exchange(mixed, ("z", "core"))
    flags = jnp.stack([jnp.where(plane == 3, 1, 0), jnp.where(plane > 0, 1, 0)])
    planes = exchange(freq_backward(x_rows, hidden, arrived, gathered, gain_f, flags, sums), "ch")
    part = jnp.sum(planes[:, 288:].astype(F32), axis=0).reshape(8, 18, 128)
    part = jnp.sum(exchange(part, ("x", "core")), axis=0).astype(BF)
    part = jnp.sum(exchange(jnp.broadcast_to(part, (16, 18, 128)), "z").astype(F32), axis=0)
    total = exchange(jnp.broadcast_to(part, (8, 18, 128)), ("x", "core"))
    return outputs_of(planes) + finish(total, grad_scale)


def solution(mesh):
    torus = Mesh(mesh.devices.reshape(4, 16, 2, 4), ("x", "z", "core", "ch"))
    return jax.shard_map(
        shards,
        mesh=torus,
        in_specs=(
            P(SEQ, None),
            P(SEQ, None),
            P(),
            P(),
            P(None, "ch"),
            P(None, "ch"),
            P("ch", None),
            P(),
            P(None, "ch"),
            P(None, None, "ch"),
            P("ch", None),
        ),
        out_specs=(
            P(SEQ, None),
            P(SEQ, None),
            P(),
            P(None, "ch"),
            P(None, "ch"),
            P("ch", None),
            P(),
            P(None, "ch"),
            P(None, None, "ch"),
            P("ch", None),
        ),
        check_vma=False,
    )
```

```python
import functools
import math

import jax
import jax.numpy as jnp
from jax import lax
from jax.experimental import pallas as pl
from jax.experimental.pallas import tpu as pltpu
from jax.sharding import Mesh, PartitionSpec as P

EPS = 1e-05
FR = 4
ROWS = 80
LEAD = 8
EDGE = 16
BF = jnp.bfloat16
F32 = jnp.float32


def nt(a, b):
    return lax.dot_general(a, b, (((1,), (1,)), ((), ())), preferred_element_type=F32)


def nn(a, b):
    return lax.dot_general(a, b, (((1,), (0,)), ((), ())), preferred_element_type=F32)


def tn(a, b):
    return lax.dot_general(a, b, (((0,), (0,)), ((), ())), preferred_element_type=F32)


def roll_rows(values, amount):
    return pltpu.roll(values, amount % values.shape[0], 0)


def sigmoid(values):
    return 0.5 * jnp.tanh(0.5 * values) + 0.5


def inverse_norm(features):
    return lax.rsqrt(jnp.mean(features * features, axis=-1, keepdims=True) + EPS)


def norm_back(d_normed, features, scale, gain):
    scaled = d_normed * gain
    summed = jnp.sum(scaled * features, axis=-1, keepdims=True)
    return scale * scaled - features * (scale * scale * scale * summed * (1.0 / features.shape[-1]))


def bins_conv(values, taps):
    return taps[0:1] * roll_rows(values, 1) + taps[1:2] * values + taps[2:3] * roll_rows(values, -1)


VMEM = pl.BlockSpec(memory_space=pltpu.VMEM)
SMEM = pl.BlockSpec(memory_space=pltpu.SMEM)


HALVES = (slice(0, 128), slice(128, 256))


def half_weights(gathered_ref, half, first):
    return jnp.concatenate([gathered_ref[2 * half + i, first : first + 64, :] for i in range(2)], axis=0)


def half_taps(gathered_ref, half, first, count):
    parts = []
    for i in range(2):
        both = gathered_ref[2 * half + i, 128:144, :].astype(F32)
        parts.append((both[:, :64] + both[:, 64:])[first : first + count])
    return jnp.concatenate(parts, axis=1)


def pack_kernel(freq_in, freq_taps, freq_out, time_in, time_taps, time_out, packed_ref):
    taps = jnp.concatenate(
        [freq_taps[...]] + [time_taps[k] for k in range(3)] + [jnp.zeros((4, 64), F32)], axis=0
    )
    high = taps.astype(BF).astype(F32)
    low = taps - high
    turn = lambda ref: ref[...].astype(F32).T.astype(BF)
    freq_w = jnp.concatenate([turn(freq_in), freq_out[...]], axis=1)
    time_w = jnp.concatenate([turn(time_in), time_out[...]], axis=1)
    tap_w = jnp.concatenate([high, low], axis=1).astype(BF)
    for peer in range(4):
        packed_ref[peer, 0:64, :] = freq_w
        packed_ref[peer, 64:128, :] = time_w
        packed_ref[peer, 128:144, :] = tap_w


def pack(*weights):
    return pl.pallas_call(
        pack_kernel, out_shape=jax.ShapeDtypeStruct((4, 144, 128), BF), name="pack"
    )(*weights)


def freq_forward_kernel(
    own_ref, halo_ref, cot_ref, cot_edge_ref, gathered_ref, gain_ref, out_ref, hidden_out, rows_ref, tiles_ref
):
    gain = gain_ref[...]
    edges = []
    for part, pair_ref in enumerate((own_ref, halo_ref)):
        features = pair_ref[...].astype(F32)
        normed = (features * inverse_norm(features) * gain).astype(BF)
        mixed = features
        for half, lanes in enumerate(HALVES):
            weights = half_weights(gathered_ref, half, 0)
            hidden = nt(normed, weights[:, :64])
            if part == 0:
                hidden_out[:, lanes] = hidden
            drive = bins_conv(hidden, half_taps(gathered_ref, half, 0, 3))
            active = (drive * sigmoid(drive)).astype(BF)
            mixed = mixed + nn(active, weights[:, 64:])
        rows_ref[...] = mixed
        for f in range(FR):
            even = rows_ref[pl.ds(f * ROWS + LEAD, 32, stride=2), :]
            odd = rows_ref[pl.ds(f * ROWS + LEAD + 1, 32, stride=2), :]
            tiles_ref[pl.ds(FR * part + f, 32, stride=8), :] = jnp.concatenate([even, odd], axis=1)
        for bin_row in (LEAD - 1, LEAD + 64):
            edges.append(
                jnp.concatenate([mixed[f * ROWS + bin_row : f * ROWS + bin_row + 1] for f in range(FR)], axis=0)
            )
    out_ref[:, 0:8, :] = tiles_ref[...].reshape(32, 8, 128).astype(BF)
    out_ref[:, 8:16, :] = cot_ref[...]
    out_ref[0:EDGE, 16:24, :] = jnp.zeros((EDGE, 8, 128), BF)
    out_ref[EDGE + 2 : 32, 16:24, :] = jnp.zeros((30 - EDGE, 8, 128), BF)
    for side in range(2):
        x_edge = jnp.concatenate([edges[side], edges[2 + side]], axis=1)
        out_ref[EDGE + side, 16:24, :] = jnp.concatenate([x_edge, cot_edge_ref[side].astype(F32)], axis=0).astype(BF)


def freq_forward(pair, halo, cot, cot_edge, gathered, gain):
    rows = pair.shape[0]
    return pl.pallas_call(
        freq_forward_kernel,
        out_shape=(jax.ShapeDtypeStruct((32, 24, 128), BF), jax.ShapeDtypeStruct((rows, 256), F32)),
        scratch_shapes=[
            pltpu.VMEM((rows, 64), F32),
            pltpu.VMEM((256, 128), F32),
        ],
        name="freq_forward",
    )(pair, halo, cot, cot_edge, gathered, gain)


def freq_backward_kernel(
    flag_ref,
    pair_ref,
    hidden_ref,
    arrived_ref,
    gathered_ref,
    gain_ref,
    time_w_ref,
    time_t_ref,
    time_g_ref,
    out_ref,
    tiles_ref,
    back_ref,
):
    gain = gain_ref[...]
    spread = jnp.concatenate([arrived_ref[...].astype(F32), jnp.zeros((32, 4, 128), F32)], axis=1)
    tiles_ref[...] = spread.reshape(512, 128)
    back_ref[...] = jnp.zeros_like(back_ref)
    left = flag_ref[1].astype(F32)
    for f in range(FR):
        back_ref[pl.ds(f * ROWS + LEAD, 32, stride=2), :] = tiles_ref[pl.ds(f, 32, stride=16), :]
        back_ref[pl.ds(f * ROWS + LEAD + 1, 32, stride=2), :] = tiles_ref[pl.ds(FR + f, 32, stride=16), :]
        back_ref[f * ROWS + LEAD - 1 : f * ROWS + LEAD, :] = tiles_ref[16 * EDGE + 8 + f : 16 * EDGE + 9 + f, :] * left
        back_ref[f * ROWS + LEAD + 64 : f * ROWS + LEAD + 65, :] = tiles_ref[16 * EDGE + 24 + f : 16 * EDGE + 25 + f, :]
    row = lax.broadcasted_iota(jnp.int32, (ROWS, 1), 0)
    upper = LEAD + 64 + flag_ref[0]
    one = jnp.where((row >= LEAD) & (row < upper), 1.0, 0.0).astype(F32)
    own = jnp.concatenate([one] * FR, axis=0)
    features = pair_ref[...].astype(F32)
    scale = inverse_norm(features)
    output, grad_wide = back_ref[:, :64], back_ref[:, 64:]
    grad = grad_wide.astype(BF)
    grad_own = (grad_wide * own).astype(BF)
    normed = (features * scale * gain * own).astype(BF)
    d_normed = None
    tap_halves, freq_w = [], []
    for half, lanes in enumerate(HALVES):
        weights = half_weights(gathered_ref, half, 0)
        taps = half_taps(gathered_ref, half, 0, 3)
        hidden = hidden_ref[:, lanes]
        before, after = roll_rows(hidden, 1), roll_rows(hidden, -1)
        drive = taps[0:1] * before + taps[1:2] * hidden + taps[2:3] * after
        gate = sigmoid(drive)
        active = drive * gate
        slope = gate + active * (1.0 - gate)
        grad_out = tn(active.astype(BF), grad_own)
        d_drive = nt(grad, weights[:, 64:]) * slope
        d_own = d_drive * own
        tap_halves.append(
            [jnp.sum(d_own * moved, axis=0, keepdims=True) for moved in (before, hidden, after)]
        )
        d_hidden = (
            taps[0:1] * roll_rows(d_drive, -1) + taps[1:2] * d_drive + taps[2:3] * roll_rows(d_drive, 1)
        ).astype(BF)
        grad_in = tn(d_hidden, normed)
        freq_w.append(jnp.concatenate([grad_out, grad_in], axis=1))
        part = nn(d_hidden, weights[:, :64])
        d_normed = part if d_normed is None else d_normed + part
    freq_g = jnp.sum(d_normed * features * (scale * own), axis=0, keepdims=True)
    d_signal = grad_wide + norm_back(d_normed, features, scale, gain)
    done = jnp.concatenate([output, d_signal], axis=1)
    done = jnp.concatenate([done[f * ROWS + LEAD : (f + 1) * ROWS] for f in range(FR)], axis=0).astype(BF)
    gains = jnp.concatenate([freq_g, time_g_ref[...]], axis=1)
    for peer in range(4):
        half, at = peer // 2, 64 * (peer % 2)
        rows = [tap[:, at : at + 64] for tap in tap_halves[half]]
        rows.append(time_t_ref[:, 64 * peer : 64 * peer + 64])
        taps = jnp.concatenate(rows, axis=0)
        taps = jnp.concatenate([taps, jnp.zeros((12, 64), F32)], axis=1)
        out_ref[peer, 0:288, :] = done
        taps = jnp.concatenate([taps, gains, jnp.zeros((3, 128), F32)], axis=0)
        pieces = []
        for i in range(8):
            if i < 4:
                pieces.append(freq_w[half][at + 16 * i : at + 16 * i + 16])
            else:
                pieces.append(time_w_ref[64 * peer + 16 * i - 64 : 64 * peer + 16 * i - 48, :])
            pieces.append(taps[8 * i : 8 * i + 8] if i < 2 else jnp.zeros((8, 128), F32))
        out_ref[peer, 288:480, :] = jnp.concatenate(pieces, axis=0).astype(BF)


def freq_backward(pair, hidden, arrived, gathered, gain, flags, sums):
    return pl.pallas_call(
        freq_backward_kernel,
        out_shape=jax.ShapeDtypeStruct((4, 480, 128), BF),
        in_specs=[SMEM] + [VMEM] * 8,
        scratch_shapes=[
            pltpu.VMEM((512, 128), F32),
            pltpu.VMEM((FR * ROWS, 128), F32),
        ],
        name="freq_backward",
    )(flags, pair, hidden, arrived, gathered, gain, *sums)


def turned(tiles):
    return jnp.concatenate(
        [roll_rows(tiles[8 * i : 8 * i + 8], 4) for i in range(tiles.shape[0] // 8)], axis=0
    )


def groups_on(values, count):
    if count > 0:
        return jnp.concatenate([values[8 * count :], turned(values[: 8 * count])], axis=0)
    base = values.shape[0] + 8 * count
    return jnp.concatenate([turned(values[base:]), values[:base]], axis=0)


def later(values, spacing, place):
    if spacing == 1:
        return jnp.where(place == 3, roll_rows(groups_on(values, 1), 3), roll_rows(values, -1))
    return groups_on(values, spacing // FR)


def earlier(values, spacing, place):
    if spacing == 1:
        return jnp.where(place == 0, roll_rows(groups_on(values, -1), -3), roll_rows(values, 1))
    return groups_on(values, -(spacing // FR))


def own_rows(values):
    tiles = values.reshape(values.shape[0] // 8, 8, values.shape[1])
    return jnp.sum(jnp.sum(tiles, axis=0)[:4], axis=0, keepdims=True)


def one_bin(message_ref, first, slot):
    if slot < 2:
        both = message_ref[:, 8 * first : 8 * first + 8].astype(F32).reshape(256, 128)
        return both[:, 64 * slot : 64 * slot + 64]
    edge = message_ref[:, 16:24].astype(F32)[:, 4 * first : 4 * first + 4]
    return jnp.concatenate([edge[:, :, :64], edge[:, :, 64:]], axis=1).reshape(256, 64)


def time_kernel(
    flag_ref,
    message_ref,
    marks_ref,
    gathered_ref,
    gain_ref,
    out_ref,
    grad_ref,
    tap_ref,
    gain_out,
):
    gain = gain_ref[...]
    valid, inside = marks_ref[:, 0:1], marks_ref[:, 1:2]
    spot = lax.broadcasted_iota(jnp.int32, (256, 1), 0)
    place = lax.broadcasted_iota(jnp.int32, (256, 128), 0) & 3
    def work(slot):
        share = jnp.where(flag_ref[0] > 0, 1.0, 0.0).astype(F32) if slot == 2 else 1.0

        def keep(ref, rows, lanes, value):
            if slot == 0:
                ref[rows, lanes] = value
            else:
                ref[rows, lanes] += value

        counted = jnp.where((spot & 7) < 4, share, 0.0).astype(F32)
        features, grad_wide = one_bin(message_ref, 0, slot), one_bin(message_ref, 1, slot)
        grad = grad_wide.astype(BF)
        grad_own = (grad_wide * counted).astype(BF)
        scale = inverse_norm(features)
        normed = features * scale * gain
        normed_own = (normed * counted).astype(BF)
        normed = normed.astype(BF)
        mixed, d_normed = features, None
        for half, lanes in enumerate(HALVES):
            weights = half_weights(gathered_ref, half, 64)
            weight_in, weight_out = weights[:, :64], weights[:, 64:]
            taps = half_taps(gathered_ref, half, 3, 9)
            state = nt(normed, weight_in) * valid
            states, slopes = [], []
            for layer in range(3):
                spacing = (1, 4, 16)[layer]
                row = taps[3 * layer : 3 * layer + 3]
                drive = (
                    row[0:1] * earlier(state, spacing, place)
                    + row[1:2] * state
                    + row[2:3] * later(state, spacing, place)
                )
                gate = sigmoid(drive)
                active = drive * gate
                states.append(state)
                slopes.append(gate + active * (1.0 - gate))
                state = state + active
                if layer < 2:
                    state = state * inside
            top = state.astype(BF)
            mixed = mixed + nn(top, weight_out)
            keep(grad_ref, lanes, slice(0, 64), tn(top, grad_own))
            d_state = nt(grad, weight_out)
            for layer in reversed(range(3)):
                spacing = (1, 4, 16)[layer]
                row = taps[3 * layer : 3 * layer + 3]
                d_drive = d_state * slopes[layer]
                if layer < 2:
                    d_drive = d_drive * inside
                held = states[layer]
                for j, moved in enumerate((earlier(held, spacing, place), held, later(held, spacing, place))):
                    at = 3 * layer + j
                    keep(tap_ref, slice(at, at + 1), lanes, own_rows(d_drive * moved) * share)
                d_state = d_state + (
                    row[0:1] * later(d_drive, spacing, place)
                    + row[1:2] * d_drive
                    + row[2:3] * earlier(d_drive, spacing, place)
                )
            d_pre = (d_state * valid).astype(BF)
            keep(grad_ref, lanes, slice(64, 128), tn(d_pre, normed_own))
            part = nn(d_pre, weight_in)
            d_normed = part if d_normed is None else d_normed + part
        keep(gain_out, slice(0, 1), slice(0, 64), own_rows(d_normed * features * scale) * share)
        d_one = grad_wide + norm_back(d_normed, features, scale, gain)
        both = jnp.concatenate([mixed, d_one], axis=1).reshape(32, 8, 128)
        out_ref[:, 4 * slot : 4 * slot + 4] = both[:, :4].astype(BF)

    work(0)
    work(1)

    @pl.when(flag_ref[1] > 0)
    def _():
        work(2)

    @pl.when(flag_ref[1] == 0)
    def _():
        out_ref[:, 8:12] = jnp.zeros((32, 4, 128), BF)


def time_path(message, marks, gathered, gain, flags):
    return pl.pallas_call(
        time_kernel,
        out_shape=(
            jax.ShapeDtypeStruct((32, 12, 128), BF),
            jax.ShapeDtypeStruct((256, 128), F32),
            jax.ShapeDtypeStruct((9, 256), F32),
            jax.ShapeDtypeStruct((1, 64), F32),
        ),
        in_specs=[SMEM] + [VMEM] * 4,
        name="time_path",
    )(flags, message, marks, gathered, gain)


def finish_kernel(
    scale, part_ref, freq_gain, freq_in, freq_taps, freq_out, time_gain, time_in, time_taps, time_out
):
    freq_w = jnp.concatenate([part_ref[i, 0:16, :] for i in range(4)], axis=0) * scale
    time_w = jnp.concatenate([part_ref[i, 0:16, :] for i in range(4, 8)], axis=0) * scale
    freq_out[...] = freq_w[:, :64]
    freq_in[...] = freq_w[:, 64:].T
    time_out[...] = time_w[:, :64]
    time_in[...] = time_w[:, 64:].T
    first, second = part_ref[0, 16:24, :] * scale, part_ref[1, 16:24, :] * scale
    freq_gain[...] = second[4:5, :64]
    time_gain[...] = second[4:5, 64:]
    freq_taps[...] = first[0:3, :64]
    time_taps[0] = first[3:6, :64]
    time_taps[1, 0:2] = first[6:8, :64]
    time_taps[1, 2:3] = second[0:1, :64]
    time_taps[2] = second[1:4, :64]


def finish(total, scale):
    shape = lambda *dims: jax.ShapeDtypeStruct(dims, F32)
    got = pl.pallas_call(
        functools.partial(finish_kernel, scale),
        out_shape=(
            shape(1, 64),
            shape(64, 64),
            shape(3, 64),
            shape(64, 64),
            shape(1, 64),
            shape(64, 64),
            shape(3, 3, 64),
            shape(64, 64),
        ),
        in_specs=[VMEM],
        name="finish",
    )(total)
    return (got[0][0], got[1], got[2], got[3], got[4][0], got[5], got[6], got[7])


def plane_lanes(values, plane):
    frames, width = values.shape
    padded = jnp.pad(values, ((0, 0), (LEAD * 64, (ROWS - LEAD + 192) * 64 - width)))
    return lax.dynamic_slice(padded, (0, plane * 4096), (frames, ROWS * 64))


def cot_message(own, halo):
    both = jnp.concatenate([own, halo], axis=0)
    mine = both[:, LEAD * 64 : LEAD * 64 + 4096].reshape(2 * FR, 32, 128).transpose(1, 0, 2)
    edge = jnp.stack([both[:, LEAD * 64 - 64 : LEAD * 64], both[:, LEAD * 64 + 4096 : LEAD * 64 + 4160]], axis=0)
    return near(mine), near(jnp.concatenate([edge[:, :FR], edge[:, FR:]], axis=2))


def frame_marks(counts, x_at):
    by_plane = jnp.pad(counts.reshape(4, 32), ((1, 1), (0, 0)))
    window = lax.dynamic_slice(by_plane, (x_at, 0), (3, 32))
    spot = jnp.arange(32)
    halo_count = jnp.where(spot >= 16, window[0], window[2])
    halo_in = jnp.where(spot >= 16, (spot >= 21) & (x_at > 0), (spot <= 10) & (x_at < 3))
    limit = jnp.stack([window[1], halo_count], axis=1)
    valid = (jnp.arange(4) < limit[:, :, None]) & jnp.stack([spot >= 0, halo_in], axis=1)[:, :, None]
    inside = jnp.stack([spot >= 0, halo_in], axis=1)[:, :, None] & (jnp.arange(4) >= 0)
    return jnp.stack([valid.reshape(256), inside.reshape(256)], axis=1).astype(F32)


def outputs_of(arrived):
    rows = arrived[:, :288].reshape(4, FR, 72, 128)
    whole = jnp.concatenate([rows[0, :, :64], rows[1, :, :64], rows[2, :, :64], rows[3, :, :65]], axis=1)
    return whole[:, :, :64].reshape(FR, -1), whole[:, :, 64:].reshape(FR, -1)


def halo_pairs():
    pairs = []
    for x_at in range(4):
        for spot in range(32):
            if spot <= 10 and x_at < 3:
                pairs.append(((x_at + 1) * 32 + spot, x_at * 32 + spot))
            if spot >= 21 and x_at > 0:
                pairs.append(((x_at - 1) * 32 + spot, x_at * 32 + spot))
    return pairs


SEQ = ("x", "z", "core")


def exchange(values, axes):
    return lax.all_to_all(values, axes, 0, 0)


def near(values):
    return pltpu.with_memory_space_constraint(values, pltpu.VMEM)


def shards(
    signal, cotangent, counts, freq_gain, freq_in, freq_taps, freq_out, time_gain, time_in, time_taps, time_out
):
    plane = lax.axis_index("ch")
    x_at = lax.axis_index("x")
    spot = lax.axis_index(("z", "core"))
    grad_scale = 1.0 / math.sqrt(FR * 128 * (signal.shape[1] // 64))
    packed = pack(freq_in, freq_taps, freq_out, time_in, time_taps, time_out)
    gathered = near(exchange(packed, "ch"))
    lanes = jnp.stack([plane_lanes(signal, plane), plane_lanes(cotangent, plane)], axis=0)
    halo = lax.ppermute(lanes, SEQ, halo_pairs())
    gain_f, gain_t = freq_gain[None], time_gain[None]
    x_rows, x_halo = near(lanes[0].reshape(FR * ROWS, 64)), near(halo[0].reshape(FR * ROWS, 64))
    message, hidden = freq_forward(x_rows, x_halo, *cot_message(lanes[1], halo[1]), gathered, gain_f)
    bands = near(exchange(message, ("z", "core")))
    marks = near(frame_marks(counts, x_at))
    beside = (spot == EDGE) | (spot == EDGE + 1)
    edge = jnp.stack([jnp.where((plane == 3) & (spot == EDGE + 1), 1, 0), jnp.where(beside, 1, 0)])
    mixed, *sums = time_path(bands, marks, gathered, gain_t, edge)
    arrived = near(exchange(mixed, ("z", "core")))
    flags = jnp.stack([jnp.where(plane == 3, 1, 0), jnp.where(plane > 0, 1, 0)])
    planes = exchange(freq_backward(x_rows, hidden, arrived, gathered, gain_f, flags, sums), "ch")
    part = jnp.sum(planes[:, 288:].astype(F32), axis=0).reshape(8, 24, 128).astype(BF)
    part = jnp.sum(exchange(part, ("x", "core")).astype(F32), axis=0).astype(BF)
    part = jnp.sum(exchange(jnp.broadcast_to(part, (16, 24, 128)), "z").astype(F32), axis=0)
    total = near(exchange(jnp.broadcast_to(part, (8, 24, 128)), ("x", "core")))
    return outputs_of(planes) + finish(total, grad_scale)


def solution(mesh):
    torus = Mesh(mesh.devices.reshape(4, 16, 2, 4), ("x", "z", "core", "ch"))
    return jax.shard_map(
        shards,
        mesh=torus,
        in_specs=(
            P(SEQ, None),
            P(SEQ, None),
            P(),
            P(),
            P(None, "ch"),
            P(None, "ch"),
            P("ch", None),
            P(),
            P(None, "ch"),
            P(None, None, "ch"),
            P("ch", None),
        ),
        out_specs=(
            P(SEQ, None),
            P(SEQ, None),
            P(),
            P(None, "ch"),
            P(None, "ch"),
            P("ch", None),
            P(),
            P(None, "ch"),
            P(None, None, "ch"),
            P("ch", None),
        ),
        check_vma=False,
    )
```

```python
import functools
import math

import jax
import jax.numpy as jnp
from jax import lax
from jax.experimental import pallas as pl
from jax.experimental.pallas import tpu as pltpu
from jax.sharding import Mesh, PartitionSpec as P


EPS = 1e-05
FR = 4
ROWS = 80
LEAD = 8
EDGE = 16
BF = jnp.bfloat16
F32 = jnp.float32


def nt(a, b):
    return lax.dot_general(a, b, (((1,), (1,)), ((), ())), preferred_element_type=F32)


def nn(a, b):
    return lax.dot_general(a, b, (((1,), (0,)), ((), ())), preferred_element_type=F32)


def tn(a, b):
    return lax.dot_general(a, b, (((0,), (0,)), ((), ())), preferred_element_type=F32)


def roll_rows(values, amount):
    return pltpu.roll(values, amount % values.shape[0], 0)


def sigmoid(values):
    return 0.5 * jnp.tanh(0.5 * values) + 0.5


def inverse_norm(features):
    return lax.rsqrt(jnp.mean(features * features, axis=-1, keepdims=True) + EPS)


def norm_back(d_normed, features, scale, gain):
    scaled = d_normed * gain
    summed = jnp.sum(scaled * features, axis=-1, keepdims=True)
    return scale * scaled - features * (scale * scale * scale * summed * (1.0 / features.shape[-1]))


def bins_conv(values, taps):
    return taps[0:1] * roll_rows(values, 1) + taps[1:2] * values + taps[2:3] * roll_rows(values, -1)


VMEM = pl.BlockSpec(memory_space=pltpu.VMEM)
SMEM = pl.BlockSpec(memory_space=pltpu.SMEM)


HALVES = (slice(0, 128), slice(128, 256))


def half_weights(gathered_ref, half, first):
    return jnp.concatenate([gathered_ref[2 * half + i, first : first + 64, :] for i in range(2)], axis=0)


def half_taps(gathered_ref, half, first, count):
    parts = []
    for i in range(2):
        both = gathered_ref[2 * half + i, 128:144, :].astype(F32)
        parts.append((both[:, :64] + both[:, 64:])[first : first + count])
    return jnp.concatenate(parts, axis=1)


def pack_kernel(freq_in, freq_taps, freq_out, time_in, time_taps, time_out, packed_ref):
    taps = jnp.concatenate(
        [freq_taps[...]] + [time_taps[k] for k in range(3)] + [jnp.zeros((4, 64), F32)], axis=0
    )
    high = taps.astype(BF).astype(F32)
    low = taps - high
    turn = lambda ref: ref[...].astype(F32).T.astype(BF)
    freq_w = jnp.concatenate([turn(freq_in), freq_out[...]], axis=1)
    time_w = jnp.concatenate([turn(time_in), time_out[...]], axis=1)
    tap_w = jnp.concatenate([high, low], axis=1).astype(BF)
    for peer in range(4):
        packed_ref[peer, 0:64, :] = freq_w
        packed_ref[peer, 64:128, :] = time_w
        packed_ref[peer, 128:144, :] = tap_w


def pack(*weights):
    return pl.pallas_call(
        pack_kernel, out_shape=jax.ShapeDtypeStruct((4, 144, 128), BF), name="pack"
    )(*weights)


def freq_forward_kernel(
    own_ref, halo_ref, cot_ref, cot_edge_ref, gathered_ref, gain_ref, out_ref, hidden_out, rows_ref, tiles_ref
):
    gain = gain_ref[...]
    edges = []
    for part, pair_ref in enumerate((own_ref, halo_ref)):
        features = pair_ref[...].astype(F32)
        normed = (features * inverse_norm(features) * gain).astype(BF)
        mixed = features
        for half, lanes in enumerate(HALVES):
            weights = half_weights(gathered_ref, half, 0)
            hidden = nt(normed, weights[:, :64])
            if part == 0:
                hidden_out[:, lanes] = hidden
            drive = bins_conv(hidden, half_taps(gathered_ref, half, 0, 3))
            active = (drive * sigmoid(drive)).astype(BF)
            mixed = mixed + nn(active, weights[:, 64:])
        rows_ref[...] = mixed
        for f in range(FR):
            even = rows_ref[pl.ds(f * ROWS + LEAD, 32, stride=2), :]
            odd = rows_ref[pl.ds(f * ROWS + LEAD + 1, 32, stride=2), :]
            tiles_ref[pl.ds(FR * part + f, 32, stride=8), :] = jnp.concatenate([even, odd], axis=1)
        for bin_row in (LEAD - 1, LEAD + 64):
            edges.append(
                jnp.concatenate([mixed[f * ROWS + bin_row : f * ROWS + bin_row + 1] for f in range(FR)], axis=0)
            )
    out_ref[:, 0:8, :] = tiles_ref[...].reshape(32, 8, 128).astype(BF)
    out_ref[:, 8:16, :] = cot_ref[...]
    out_ref[0:EDGE, 16:24, :] = jnp.zeros((EDGE, 8, 128), BF)
    out_ref[EDGE + 2 : 32, 16:24, :] = jnp.zeros((30 - EDGE, 8, 128), BF)
    for side in range(2):
        x_edge = jnp.concatenate([edges[side], edges[2 + side]], axis=1)
        out_ref[EDGE + side, 16:24, :] = jnp.concatenate([x_edge, cot_edge_ref[side].astype(F32)], axis=0).astype(BF)


def freq_forward(pair, halo, cot, cot_edge, gathered, gain):
    rows = pair.shape[0]
    return pl.pallas_call(
        freq_forward_kernel,
        out_shape=(jax.ShapeDtypeStruct((32, 24, 128), BF), jax.ShapeDtypeStruct((rows, 256), F32)),
        scratch_shapes=[
            pltpu.VMEM((rows, 64), F32),
            pltpu.VMEM((256, 128), F32),
        ],
        name="freq_forward",
    )(pair, halo, cot, cot_edge, gathered, gain)


def freq_backward_kernel(
    flag_ref,
    pair_ref,
    hidden_ref,
    arrived_ref,
    gathered_ref,
    gain_ref,
    time_w_ref,
    time_t_ref,
    time_g_ref,
    done_ref,
    out_ref,
    tiles_ref,
    back_ref,
):
    gain = gain_ref[...]
    spread = jnp.concatenate([arrived_ref[...].astype(F32), jnp.zeros((32, 4, 128), F32)], axis=1)
    tiles_ref[...] = spread.reshape(512, 128)
    back_ref[...] = jnp.zeros_like(back_ref)
    left = flag_ref[1].astype(F32)
    for f in range(FR):
        back_ref[pl.ds(f * ROWS + LEAD, 32, stride=2), :] = tiles_ref[pl.ds(f, 32, stride=16), :]
        back_ref[pl.ds(f * ROWS + LEAD + 1, 32, stride=2), :] = tiles_ref[pl.ds(FR + f, 32, stride=16), :]
        back_ref[f * ROWS + LEAD - 1 : f * ROWS + LEAD, :] = tiles_ref[16 * EDGE + 8 + f : 16 * EDGE + 9 + f, :] * left
        back_ref[f * ROWS + LEAD + 64 : f * ROWS + LEAD + 65, :] = tiles_ref[16 * EDGE + 24 + f : 16 * EDGE + 25 + f, :]
    row = lax.broadcasted_iota(jnp.int32, (ROWS, 1), 0)
    upper = LEAD + 64 + flag_ref[0]
    one = jnp.where((row >= LEAD) & (row < upper), 1.0, 0.0).astype(F32)
    own = jnp.concatenate([one] * FR, axis=0)
    features = pair_ref[...].astype(F32)
    scale = inverse_norm(features)
    output, grad_wide = back_ref[:, :64], back_ref[:, 64:]
    grad = grad_wide.astype(BF)
    grad_own = (grad_wide * own).astype(BF)
    normed = (features * scale * gain * own).astype(BF)
    d_normed = None
    tap_halves, freq_w = [], []
    for half, lanes in enumerate(HALVES):
        weights = half_weights(gathered_ref, half, 0)
        taps = half_taps(gathered_ref, half, 0, 3)
        hidden = hidden_ref[:, lanes]
        before, after = roll_rows(hidden, 1), roll_rows(hidden, -1)
        drive = taps[0:1] * before + taps[1:2] * hidden + taps[2:3] * after
        gate = sigmoid(drive)
        active = drive * gate
        slope = gate + active * (1.0 - gate)
        grad_out = tn(active.astype(BF), grad_own)
        d_drive = nt(grad, weights[:, 64:]) * slope
        d_own = d_drive * own
        tap_halves.append(
            [jnp.sum(d_own * moved, axis=0, keepdims=True) for moved in (before, hidden, after)]
        )
        d_hidden = (
            taps[0:1] * roll_rows(d_drive, -1) + taps[1:2] * d_drive + taps[2:3] * roll_rows(d_drive, 1)
        ).astype(BF)
        grad_in = tn(d_hidden, normed)
        freq_w.append(jnp.concatenate([grad_out, grad_in], axis=1))
        part = nn(d_hidden, weights[:, :64])
        d_normed = part if d_normed is None else d_normed + part
    freq_g = jnp.sum(d_normed * features * (scale * own), axis=0, keepdims=True)
    d_signal = grad_wide + norm_back(d_normed, features, scale, gain)
    done = jnp.concatenate([output, d_signal], axis=1)
    done = jnp.concatenate([done[f * ROWS + LEAD : (f + 1) * ROWS] for f in range(FR)], axis=0).astype(BF)
    done_ref[...] = done
    gains = jnp.concatenate([freq_g, time_g_ref[...]], axis=1)
    for peer in range(4):
        half, at = peer // 2, 64 * (peer % 2)
        rows = [tap[:, at : at + 64] for tap in tap_halves[half]]
        rows.append(time_t_ref[:, 64 * peer : 64 * peer + 64])
        taps = jnp.concatenate(rows, axis=0)
        taps = jnp.concatenate([taps, jnp.zeros((12, 64), F32)], axis=1)
        taps = jnp.concatenate([taps, gains, jnp.zeros((3, 128), F32)], axis=0)
        for i in range(8):
            if i < 4:
                piece = freq_w[half][at + 16 * i : at + 16 * i + 16]
            else:
                piece = time_w_ref[64 * peer + 16 * i - 64 : 64 * peer + 16 * i - 48, :]
            small = taps[8 * i : 8 * i + 8] if i < 2 else jnp.zeros((8, 128), F32)
            out_ref[4 * i + peer] = jnp.concatenate([piece, small], axis=0).astype(BF)


def freq_backward(pair, hidden, arrived, gathered, gain, flags, sums):
    return pl.pallas_call(
        freq_backward_kernel,
        out_shape=(jax.ShapeDtypeStruct((288, 128), BF), jax.ShapeDtypeStruct((32, 24, 128), BF)),
        in_specs=[SMEM] + [VMEM] * 8,
        scratch_shapes=[
            pltpu.VMEM((512, 128), F32),
            pltpu.VMEM((FR * ROWS, 128), F32),
        ],
        name="freq_backward",
    )(flags, pair, hidden, arrived, gathered, gain, *sums)


def turned(tiles):
    return jnp.concatenate(
        [roll_rows(tiles[8 * i : 8 * i + 8], 4) for i in range(tiles.shape[0] // 8)], axis=0
    )


def groups_on(values, count):
    if count > 0:
        return jnp.concatenate([values[8 * count :], turned(values[: 8 * count])], axis=0)
    base = values.shape[0] + 8 * count
    return jnp.concatenate([turned(values[base:]), values[:base]], axis=0)


def later(values, spacing, place):
    if spacing == 1:
        return jnp.where(place == 3, roll_rows(groups_on(values, 1), 3), roll_rows(values, -1))
    return groups_on(values, spacing // FR)


def earlier(values, spacing, place):
    if spacing == 1:
        return jnp.where(place == 0, roll_rows(groups_on(values, -1), -3), roll_rows(values, 1))
    return groups_on(values, -(spacing // FR))


def own_rows(values):
    tiles = values.reshape(values.shape[0] // 8, 8, values.shape[1])
    return jnp.sum(jnp.sum(tiles, axis=0)[:4], axis=0, keepdims=True)


def one_bin(message_ref, first, slot):
    if slot < 2:
        both = message_ref[:, 8 * first : 8 * first + 8].astype(F32).reshape(256, 128)
        return both[:, 64 * slot : 64 * slot + 64]
    edge = message_ref[:, 16:24].astype(F32)[:, 4 * first : 4 * first + 4]
    return jnp.concatenate([edge[:, :, :64], edge[:, :, 64:]], axis=1).reshape(256, 64)


def time_kernel(
    flag_ref,
    message_ref,
    marks_ref,
    gathered_ref,
    gain_ref,
    out_ref,
    grad_ref,
    tap_ref,
    gain_out,
):
    gain = gain_ref[...]
    valid, inside = marks_ref[:, 0:1], marks_ref[:, 1:2]
    spot = lax.broadcasted_iota(jnp.int32, (256, 1), 0)
    place = lax.broadcasted_iota(jnp.int32, (256, 128), 0) & 3

    def work(slot):
        share = jnp.where(flag_ref[0] > 0, 1.0, 0.0).astype(F32) if slot == 2 else 1.0

        def keep(ref, rows, lanes, value):
            if slot == 0:
                ref[rows, lanes] = value
            else:
                ref[rows, lanes] += value

        counted = jnp.where((spot & 7) < 4, share, 0.0).astype(F32)
        features, grad_wide = one_bin(message_ref, 0, slot), one_bin(message_ref, 1, slot)
        grad = grad_wide.astype(BF)
        grad_own = (grad_wide * counted).astype(BF)
        scale = inverse_norm(features)
        normed = features * scale * gain
        normed_own = (normed * counted).astype(BF)
        normed = normed.astype(BF)
        mixed, d_normed = features, None
        for half, lanes in enumerate(HALVES):
            weights = half_weights(gathered_ref, half, 64)
            weight_in, weight_out = weights[:, :64], weights[:, 64:]
            taps = half_taps(gathered_ref, half, 3, 9)
            state = nt(normed, weight_in) * valid
            states, slopes = [], []
            for layer in range(3):
                spacing = (1, 4, 16)[layer]
                row = taps[3 * layer : 3 * layer + 3]
                drive = (
                    row[0:1] * earlier(state, spacing, place)
                    + row[1:2] * state
                    + row[2:3] * later(state, spacing, place)
                )
                gate = sigmoid(drive)
                active = drive * gate
                states.append(state)
                slopes.append(gate + active * (1.0 - gate))
                state = state + active
                if layer < 2:
                    state = state * inside
            top = state.astype(BF)
            mixed = mixed + nn(top, weight_out)
            keep(grad_ref, lanes, slice(0, 64), tn(top, grad_own))
            d_state = nt(grad, weight_out)
            for layer in reversed(range(3)):
                spacing = (1, 4, 16)[layer]
                row = taps[3 * layer : 3 * layer + 3]
                d_drive = d_state * slopes[layer]
                if layer < 2:
                    d_drive = d_drive * inside
                held = states[layer]
                for j, moved in enumerate((earlier(held, spacing, place), held, later(held, spacing, place))):
                    at = 3 * layer + j
                    keep(tap_ref, slice(at, at + 1), lanes, own_rows(d_drive * moved) * share)
                d_state = d_state + (
                    row[0:1] * later(d_drive, spacing, place)
                    + row[1:2] * d_drive
                    + row[2:3] * earlier(d_drive, spacing, place)
                )
            d_pre = (d_state * valid).astype(BF)
            keep(grad_ref, lanes, slice(64, 128), tn(d_pre, normed_own))
            part = nn(d_pre, weight_in)
            d_normed = part if d_normed is None else d_normed + part
        keep(gain_out, slice(0, 1), slice(0, 64), own_rows(d_normed * features * scale) * share)
        d_one = grad_wide + norm_back(d_normed, features, scale, gain)
        both = jnp.concatenate([mixed, d_one], axis=1).reshape(32, 8, 128)
        out_ref[:, 4 * slot : 4 * slot + 4] = both[:, :4].astype(BF)

    work(0)
    work(1)

    @pl.when(flag_ref[1] > 0)
    def _():
        work(2)

    @pl.when(flag_ref[1] == 0)
    def _():
        out_ref[:, 8:12] = jnp.zeros((32, 4, 128), BF)


def time_path(message, marks, gathered, gain, flags):
    return pl.pallas_call(
        time_kernel,
        out_shape=(
            jax.ShapeDtypeStruct((32, 12, 128), BF),
            jax.ShapeDtypeStruct((256, 128), F32),
            jax.ShapeDtypeStruct((9, 256), F32),
            jax.ShapeDtypeStruct((1, 64), F32),
        ),
        in_specs=[SMEM] + [VMEM] * 4,
        name="time_path",
    )(flags, message, marks, gathered, gain)


def finish_kernel(
    scale, part_ref, freq_gain, freq_in, freq_taps, freq_out, time_gain, time_in, time_taps, time_out
):
    freq_w = jnp.concatenate([part_ref[i, 0:16, :] for i in range(4)], axis=0) * scale
    time_w = jnp.concatenate([part_ref[i, 0:16, :] for i in range(4, 8)], axis=0) * scale
    freq_out[...] = freq_w[:, :64]
    freq_in[...] = freq_w[:, 64:].T
    time_out[...] = time_w[:, :64]
    time_in[...] = time_w[:, 64:].T
    first, second = part_ref[0, 16:24, :] * scale, part_ref[1, 16:24, :] * scale
    freq_gain[...] = second[4:5, :64]
    time_gain[...] = second[4:5, 64:]
    freq_taps[...] = first[0:3, :64]
    time_taps[0] = first[3:6, :64]
    time_taps[1, 0:2] = first[6:8, :64]
    time_taps[1, 2:3] = second[0:1, :64]
    time_taps[2] = second[1:4, :64]


def finish(total, scale):
    shape = lambda *dims: jax.ShapeDtypeStruct(dims, F32)
    got = pl.pallas_call(
        functools.partial(finish_kernel, scale),
        out_shape=(
            shape(1, 64),
            shape(64, 64),
            shape(3, 64),
            shape(64, 64),
            shape(1, 64),
            shape(64, 64),
            shape(3, 3, 64),
            shape(64, 64),
        ),
        in_specs=[VMEM],
        name="finish",
    )(total)
    return (got[0][0], got[1], got[2], got[3], got[4][0], got[5], got[6], got[7])


def plane_lanes(values, plane):
    frames, width = values.shape
    padded = jnp.pad(values, ((0, 0), (LEAD * 64, (ROWS - LEAD + 192) * 64 - width)))
    return lax.dynamic_slice(padded, (0, plane * 4096), (frames, ROWS * 64))


def cot_message(own, halo):
    both = jnp.concatenate([own, halo], axis=0)
    mine = both[:, LEAD * 64 : LEAD * 64 + 4096].reshape(2 * FR, 32, 128).transpose(1, 0, 2)
    edge = jnp.stack([both[:, LEAD * 64 - 64 : LEAD * 64], both[:, LEAD * 64 + 4096 : LEAD * 64 + 4160]], axis=0)
    return near(mine), near(jnp.concatenate([edge[:, :FR], edge[:, FR:]], axis=2))


def frame_marks(counts, x_at):
    by_plane = jnp.pad(counts.reshape(4, 32), ((1, 1), (0, 0)))
    window = lax.dynamic_slice(by_plane, (x_at, 0), (3, 32))
    spot = jnp.arange(32)
    halo_count = jnp.where(spot >= 16, window[0], window[2])
    halo_in = jnp.where(spot >= 16, (spot >= 21) & (x_at > 0), (spot <= 10) & (x_at < 3))
    limit = jnp.stack([window[1], halo_count], axis=1)
    valid = (jnp.arange(4) < limit[:, :, None]) & jnp.stack([spot >= 0, halo_in], axis=1)[:, :, None]
    inside = jnp.stack([spot >= 0, halo_in], axis=1)[:, :, None] & (jnp.arange(4) >= 0)
    return jnp.stack([valid.reshape(256), inside.reshape(256)], axis=1).astype(F32)


def outputs_of(blocks, plane):
    twice = jnp.stack(blocks[::-1] + blocks[::-1], axis=0)
    rows = lax.dynamic_slice(twice, (3 - plane, 0, 0), (4, 288, 128)).reshape(4, FR, 72, 128)
    whole = jnp.concatenate([rows[0, :, :64], rows[1, :, :64], rows[2, :, :64], rows[3, :, :65]], axis=1)
    return whole[:, :, :64].reshape(FR, -1), whole[:, :, 64:].reshape(FR, -1)


def halo_pairs():
    pairs = []
    for x_at in range(4):
        for spot in range(32):
            if spot <= 10 and x_at < 3:
                pairs.append(((x_at + 1) * 32 + spot, x_at * 32 + spot))
            if spot >= 21 and x_at > 0:
                pairs.append(((x_at - 1) * 32 + spot, x_at * 32 + spot))
    return pairs


SEQ = ("x", "z", "core")


def exchange(values, axes):
    return lax.all_to_all(values, axes, 0, 0)


def near(values):
    return pltpu.with_memory_space_constraint(values, pltpu.VMEM)


def shards(
    signal, cotangent, counts, freq_gain, freq_in, freq_taps, freq_out, time_gain, time_in, time_taps, time_out
):
    plane = lax.axis_index("ch")
    x_at = lax.axis_index("x")
    spot = lax.axis_index(("z", "core"))
    grad_scale = 1.0 / math.sqrt(FR * 128 * (signal.shape[1] // 64))
    packed = pack(freq_in, freq_taps, freq_out, time_in, time_taps, time_out)
    gathered = near(exchange(packed, "ch"))
    lanes = jnp.stack([plane_lanes(signal, plane), plane_lanes(cotangent, plane)], axis=0)
    halo = lax.ppermute(lanes, SEQ, halo_pairs())
    gain_f, gain_t = freq_gain[None], time_gain[None]
    x_rows, x_halo = near(lanes[0].reshape(FR * ROWS, 64)), near(halo[0].reshape(FR * ROWS, 64))
    message, hidden = freq_forward(x_rows, x_halo, *cot_message(lanes[1], halo[1]), gathered, gain_f)
    bands = near(exchange(message, ("z", "core")))
    marks = near(frame_marks(counts, x_at))
    beside = (spot == EDGE) | (spot == EDGE + 1)
    edge = jnp.stack([jnp.where((plane == 3) & (spot == EDGE + 1), 1, 0), jnp.where(beside, 1, 0)])
    mixed, *sums = time_path(bands, marks, gathered, gain_t, edge)
    arrived = near(exchange(mixed, ("z", "core")))
    flags = jnp.stack([jnp.where(plane == 3, 1, 0), jnp.where(plane > 0, 1, 0)])
    done, pieces = freq_backward(x_rows, hidden, arrived, gathered, gain_f, flags, sums)
    part = exchange(pieces, ("x", "core", "ch"))
    part = jnp.broadcast_to(jnp.sum(part.astype(F32), axis=0).astype(BF), (16, 24, 128))
    blocks = [done]
    for shift in (1, 2, 3):
        blocks.append(lax.ppermute(done, "ch", [(i, (i + shift) % 4) for i in range(4)]))
    part = exchange(part, "z")
    part = jnp.sum(part.astype(F32), axis=0)
    total = near(exchange(jnp.broadcast_to(part, (8, 24, 128)), ("x", "core")))
    return outputs_of(blocks, plane) + finish(total, grad_scale)


def solution(mesh):
    torus = Mesh(mesh.devices.reshape(4, 16, 2, 4), ("x", "z", "core", "ch"))
    return jax.shard_map(
        shards,
        mesh=torus,
        in_specs=(
            P(SEQ, None),
            P(SEQ, None),
            P(),
            P(),
            P(None, "ch"),
            P(None, "ch"),
            P("ch", None),
            P(),
            P(None, "ch"),
            P(None, None, "ch"),
            P("ch", None),
        ),
        out_specs=(
            P(SEQ, None),
            P(SEQ, None),
            P(),
            P(None, "ch"),
            P(None, "ch"),
            P("ch", None),
            P(),
            P(None, "ch"),
            P(None, None, "ch"),
            P("ch", None),
        ),
        check_vma=False,
    )
```

```python
import functools
import math

import jax
import jax.numpy as jnp
from jax import lax
from jax.experimental import pallas as pl
from jax.experimental.pallas import tpu as pltpu
from jax.sharding import Mesh, PartitionSpec as P


EPS = 1e-05
FR = 4
ROWS = 80
LEAD = 8
EDGE = 16
BF = jnp.bfloat16
F32 = jnp.float32


def nt(a, b):
    return lax.dot_general(a, b, (((1,), (1,)), ((), ())), preferred_element_type=F32)


def nn(a, b):
    return lax.dot_general(a, b, (((1,), (0,)), ((), ())), preferred_element_type=F32)


def tn(a, b):
    return lax.dot_general(a, b, (((0,), (0,)), ((), ())), preferred_element_type=F32)


def roll_rows(values, amount):
    return pltpu.roll(values, amount % values.shape[0], 0)


def sigmoid(values):
    return 0.5 * jnp.tanh(0.5 * values) + 0.5


def inverse_norm(features):
    return lax.rsqrt(jnp.mean(features * features, axis=-1, keepdims=True) + EPS)


def norm_back(d_normed, features, scale, gain):
    scaled = d_normed * gain
    summed = jnp.sum(scaled * features, axis=-1, keepdims=True)
    return scale * scaled - features * (scale * scale * scale * summed * (1.0 / features.shape[-1]))


def bins_conv(values, taps):
    return taps[0:1] * roll_rows(values, 1) + taps[1:2] * values + taps[2:3] * roll_rows(values, -1)


VMEM = pl.BlockSpec(memory_space=pltpu.VMEM)
SMEM = pl.BlockSpec(memory_space=pltpu.SMEM)


HALVES = (slice(0, 128), slice(128, 256))


def half_weights(gathered_ref, half, first):
    return jnp.concatenate([gathered_ref[2 * half + i, first : first + 64, :] for i in range(2)], axis=0)


def half_taps(gathered_ref, half, first, count):
    parts = []
    for i in range(2):
        both = gathered_ref[2 * half + i, 128:144, :].astype(F32)
        parts.append((both[:, :64] + both[:, 64:])[first : first + count])
    return jnp.concatenate(parts, axis=1)


def pack_kernel(freq_in, freq_taps, freq_out, time_in, time_taps, time_out, packed_ref):
    taps = jnp.concatenate(
        [freq_taps[...]] + [time_taps[k] for k in range(3)] + [jnp.zeros((4, 64), F32)], axis=0
    )
    high = taps.astype(BF).astype(F32)
    low = taps - high
    turn = lambda ref: ref[...].astype(F32).T.astype(BF)
    freq_w = jnp.concatenate([turn(freq_in), freq_out[...]], axis=1)
    time_w = jnp.concatenate([turn(time_in), time_out[...]], axis=1)
    tap_w = jnp.concatenate([high, low], axis=1).astype(BF)
    for peer in range(4):
        packed_ref[peer, 0:64, :] = freq_w
        packed_ref[peer, 64:128, :] = time_w
        packed_ref[peer, 128:144, :] = tap_w


def pack(*weights):
    return pl.pallas_call(
        pack_kernel, out_shape=jax.ShapeDtypeStruct((4, 144, 128), BF), name="pack"
    )(*weights)


def freq_forward_kernel(
    own_ref, halo_ref, cot_ref, cot_edge_ref, gathered_ref, gain_ref, out_ref, hidden_out, rows_ref, tiles_ref
):
    gain = gain_ref[...]
    edges = []
    for part, pair_ref in enumerate((own_ref, halo_ref)):
        features = pair_ref[...].astype(F32)
        normed = (features * inverse_norm(features) * gain).astype(BF)
        mixed = features
        for half, lanes in enumerate(HALVES):
            weights = half_weights(gathered_ref, half, 0)
            hidden = nt(normed, weights[:, :64])
            if part == 0:
                hidden_out[:, lanes] = hidden
            drive = bins_conv(hidden, half_taps(gathered_ref, half, 0, 3))
            active = (drive * sigmoid(drive)).astype(BF)
            mixed = mixed + nn(active, weights[:, 64:])
        rows_ref[...] = mixed
        for f in range(FR):
            even = rows_ref[pl.ds(f * ROWS + LEAD, 32, stride=2), :]
            odd = rows_ref[pl.ds(f * ROWS + LEAD + 1, 32, stride=2), :]
            tiles_ref[pl.ds(FR * part + f, 32, stride=8), :] = jnp.concatenate([even, odd], axis=1)
        for bin_row in (LEAD - 1, LEAD + 64):
            edges.append(
                jnp.concatenate([mixed[f * ROWS + bin_row : f * ROWS + bin_row + 1] for f in range(FR)], axis=0)
            )
    out_ref[:, 0:8, :] = tiles_ref[...].reshape(32, 8, 128).astype(BF)
    out_ref[:, 8:16, :] = cot_ref[...]
    out_ref[0:EDGE, 16:24, :] = jnp.zeros((EDGE, 8, 128), BF)
    out_ref[EDGE + 2 : 32, 16:24, :] = jnp.zeros((30 - EDGE, 8, 128), BF)
    for side in range(2):
        x_edge = jnp.concatenate([edges[side], edges[2 + side]], axis=1)
        out_ref[EDGE + side, 16:24, :] = jnp.concatenate([x_edge, cot_edge_ref[side].astype(F32)], axis=0).astype(BF)


def freq_forward(pair, halo, cot, cot_edge, gathered, gain):
    rows = pair.shape[0]
    return pl.pallas_call(
        freq_forward_kernel,
        out_shape=(jax.ShapeDtypeStruct((32, 24, 128), BF), pltpu.VMEM((rows, 256), F32)),
        scratch_shapes=[
            pltpu.VMEM((rows, 64), F32),
            pltpu.VMEM((256, 128), F32),
        ],
        name="freq_forward",
    )(pair, halo, cot, cot_edge, gathered, gain)


def freq_backward_kernel(
    flag_ref,
    pair_ref,
    hidden_ref,
    arrived_ref,
    gathered_ref,
    gain_ref,
    time_w_ref,
    time_t_ref,
    time_g_ref,
    done_ref,
    out_ref,
    tiles_ref,
    back_ref,
):
    gain = gain_ref[...]
    spread = jnp.concatenate([arrived_ref[...].astype(F32), jnp.zeros((32, 4, 128), F32)], axis=1)
    tiles_ref[...] = spread.reshape(512, 128)
    back_ref[...] = jnp.zeros_like(back_ref)
    left = flag_ref[1].astype(F32)
    for f in range(FR):
        back_ref[pl.ds(f * ROWS + LEAD, 32, stride=2), :] = tiles_ref[pl.ds(f, 32, stride=16), :]
        back_ref[pl.ds(f * ROWS + LEAD + 1, 32, stride=2), :] = tiles_ref[pl.ds(FR + f, 32, stride=16), :]
        back_ref[f * ROWS + LEAD - 1 : f * ROWS + LEAD, :] = tiles_ref[16 * EDGE + 8 + f : 16 * EDGE + 9 + f, :] * left
        back_ref[f * ROWS + LEAD + 64 : f * ROWS + LEAD + 65, :] = tiles_ref[16 * EDGE + 24 + f : 16 * EDGE + 25 + f, :]
    row = lax.broadcasted_iota(jnp.int32, (ROWS, 1), 0)
    upper = LEAD + 64 + flag_ref[0]
    one = jnp.where((row >= LEAD) & (row < upper), 1.0, 0.0).astype(F32)
    own = jnp.concatenate([one] * FR, axis=0)
    features = pair_ref[...].astype(F32)
    scale = inverse_norm(features)
    output, grad_wide = back_ref[:, :64], back_ref[:, 64:]
    grad = grad_wide.astype(BF)
    grad_own = (grad_wide * own).astype(BF)
    normed = (features * scale * gain * own).astype(BF)
    d_normed = None
    tap_halves, freq_w = [], []
    for half, lanes in enumerate(HALVES):
        weights = half_weights(gathered_ref, half, 0)
        taps = half_taps(gathered_ref, half, 0, 3)
        hidden = hidden_ref[:, lanes]
        before, after = roll_rows(hidden, 1), roll_rows(hidden, -1)
        drive = taps[0:1] * before + taps[1:2] * hidden + taps[2:3] * after
        gate = sigmoid(drive)
        active = drive * gate
        slope = gate + active * (1.0 - gate)
        grad_out = tn(active.astype(BF), grad_own)
        d_drive = nt(grad, weights[:, 64:]) * slope
        d_own = d_drive * own
        tap_halves.append(
            [jnp.sum(d_own * moved, axis=0, keepdims=True) for moved in (before, hidden, after)]
        )
        d_hidden = (
            taps[0:1] * roll_rows(d_drive, -1) + taps[1:2] * d_drive + taps[2:3] * roll_rows(d_drive, 1)
        ).astype(BF)
        grad_in = tn(d_hidden, normed)
        freq_w.append(jnp.concatenate([grad_out, grad_in], axis=1))
        part = nn(d_hidden, weights[:, :64])
        d_normed = part if d_normed is None else d_normed + part
    freq_g = jnp.sum(d_normed * features * (scale * own), axis=0, keepdims=True)
    d_signal = grad_wide + norm_back(d_normed, features, scale, gain)
    done = jnp.concatenate([output, d_signal], axis=1)
    done = jnp.concatenate([done[f * ROWS + LEAD : (f + 1) * ROWS] for f in range(FR)], axis=0).astype(BF)
    done_ref[...] = done
    gains = jnp.concatenate([freq_g, time_g_ref[...]], axis=1)
    for peer in range(4):
        half, at = peer // 2, 64 * (peer % 2)
        rows = [tap[:, at : at + 64] for tap in tap_halves[half]]
        rows.append(time_t_ref[:, 64 * peer : 64 * peer + 64])
        taps = jnp.concatenate(rows, axis=0)
        taps = jnp.concatenate([taps, jnp.zeros((12, 64), F32)], axis=1)
        taps = jnp.concatenate([taps, gains, jnp.zeros((3, 128), F32)], axis=0)
        for i in range(8):
            if i < 4:
                piece = freq_w[half][at + 16 * i : at + 16 * i + 16]
            else:
                piece = time_w_ref[64 * peer + 16 * i - 64 : 64 * peer + 16 * i - 48, :]
            small = taps[8 * i : 8 * i + 8] if i < 2 else jnp.zeros((8, 128), F32)
            out_ref[4 * i + peer] = jnp.concatenate([piece, small], axis=0).astype(BF)


def freq_backward(pair, hidden, arrived, gathered, gain, flags, sums):
    return pl.pallas_call(
        freq_backward_kernel,
        out_shape=(jax.ShapeDtypeStruct((288, 128), BF), jax.ShapeDtypeStruct((32, 24, 128), BF)),
        in_specs=[SMEM] + [VMEM] * 8,
        scratch_shapes=[
            pltpu.VMEM((512, 128), F32),
            pltpu.VMEM((FR * ROWS, 128), F32),
        ],
        name="freq_backward",
    )(flags, pair, near(hidden), arrived, gathered, gain, *[near(part) for part in sums])


def turned(tiles):
    return jnp.concatenate(
        [roll_rows(tiles[8 * i : 8 * i + 8], 4) for i in range(tiles.shape[0] // 8)], axis=0
    )


def groups_on(values, count):
    if count > 0:
        return jnp.concatenate([values[8 * count :], turned(values[: 8 * count])], axis=0)
    base = values.shape[0] + 8 * count
    return jnp.concatenate([turned(values[base:]), values[:base]], axis=0)


def in_tiles(values, amount):
    tiles = values.reshape(values.shape[0] // 8, 8, values.shape[1])
    return pltpu.roll(tiles, amount % 8, 1).reshape(values.shape)


def later(values, spacing, place):
    if spacing == 1:
        return jnp.where(place == 3, in_tiles(groups_on(values, 1), 3), in_tiles(values, -1))
    return groups_on(values, spacing // FR)


def earlier(values, spacing, place):
    if spacing == 1:
        return jnp.where(place == 0, in_tiles(groups_on(values, -1), -3), in_tiles(values, 1))
    return groups_on(values, -(spacing // FR))


def own_rows(values):
    tiles = values.reshape(values.shape[0] // 8, 8, values.shape[1])
    return jnp.sum(jnp.sum(tiles, axis=0)[:4], axis=0, keepdims=True)


def one_bin(message_ref, first, slot):
    if slot < 2:
        both = message_ref[:, 8 * first : 8 * first + 8].astype(F32).reshape(256, 128)
        return both[:, 64 * slot : 64 * slot + 64]
    edge = message_ref[:, 16:24].astype(F32)[:, 4 * first : 4 * first + 4]
    return jnp.concatenate([edge[:, :, :64], edge[:, :, 64:]], axis=1).reshape(256, 64)


def time_kernel(
    flag_ref,
    message_ref,
    marks_ref,
    gathered_ref,
    gain_ref,
    out_ref,
    grad_ref,
    tap_ref,
    gain_out,
):
    gain = gain_ref[...]
    valid, inside = marks_ref[:, 0:1], marks_ref[:, 1:2]
    spot = lax.broadcasted_iota(jnp.int32, (256, 1), 0)
    place = lax.broadcasted_iota(jnp.int32, (256, 128), 0) & 3

    def work(slot):
        share = jnp.where(flag_ref[0] > 0, 1.0, 0.0).astype(F32) if slot == 2 else 1.0

        def keep(ref, rows, lanes, value):
            if slot == 0:
                ref[rows, lanes] = value
            else:
                ref[rows, lanes] += value

        counted = jnp.where((spot & 7) < 4, share, 0.0).astype(F32)
        features, grad_wide = one_bin(message_ref, 0, slot), one_bin(message_ref, 1, slot)
        grad = grad_wide.astype(BF)
        grad_own = (grad_wide * counted).astype(BF)
        scale = inverse_norm(features)
        normed = features * scale * gain
        normed_own = (normed * counted).astype(BF)
        normed = normed.astype(BF)
        mixed, d_normed = features, None
        for side, lanes in enumerate(HALVES):
            weights = half_weights(gathered_ref, side, 64)
            weight_in, weight_out = weights[:, :64], weights[:, 64:]
            half = 0.5 * half_taps(gathered_ref, side, 3, 9)
            state = nt(normed, weight_in) * valid
            states, slopes = [], []
            for layer in range(3):
                spacing = (1, 4, 16)[layer]
                row = half[3 * layer : 3 * layer + 3]
                around = (earlier(state, spacing, place), state, later(state, spacing, place))
                drive = row[0:1] * around[0] + row[1:2] * state + row[2:3] * around[2]
                opened = jnp.tanh(drive) + 1.0
                active = drive * opened
                states.append(around)
                slopes.append(opened + active * (2.0 - opened))
                state = state + active
                if layer < 2:
                    state = state * inside
            top = state.astype(BF)
            mixed = mixed + nn(top, weight_out)
            keep(grad_ref, lanes, slice(0, 64), tn(top, grad_own))
            d_state = nt(grad, weight_out)
            for layer in reversed(range(3)):
                spacing = (1, 4, 16)[layer]
                row = half[3 * layer : 3 * layer + 3]
                d_drive = d_state * slopes[layer]
                if layer < 2:
                    d_drive = d_drive * inside
                for j, moved in enumerate(states[layer]):
                    at = 3 * layer + j
                    keep(tap_ref, slice(at, at + 1), lanes, own_rows(d_drive * moved) * (0.5 * share))
                d_state = d_state + (
                    row[0:1] * later(d_drive, spacing, place)
                    + row[1:2] * d_drive
                    + row[2:3] * earlier(d_drive, spacing, place)
                )
            d_pre = (d_state * valid).astype(BF)
            keep(grad_ref, lanes, slice(64, 128), tn(d_pre, normed_own))
            part = nn(d_pre, weight_in)
            d_normed = part if d_normed is None else d_normed + part
        keep(gain_out, slice(0, 1), slice(0, 64), own_rows(d_normed * features * scale) * share)
        d_one = grad_wide + norm_back(d_normed, features, scale, gain)
        both = jnp.concatenate([mixed, d_one], axis=1).reshape(32, 8, 128)
        out_ref[:, 4 * slot : 4 * slot + 4] = both[:, :4].astype(BF)

    work(0)
    work(1)

    @pl.when(flag_ref[1] > 0)
    def _():
        work(2)

    @pl.when(flag_ref[1] == 0)
    def _():
        out_ref[:, 8:12] = jnp.zeros((32, 4, 128), BF)


def time_path(message, marks, gathered, gain, flags):
    return pl.pallas_call(
        time_kernel,
        out_shape=(
            jax.ShapeDtypeStruct((32, 12, 128), BF),
            pltpu.VMEM((256, 128), F32),
            pltpu.VMEM((9, 256), F32),
            pltpu.VMEM((1, 64), F32),
        ),
        in_specs=[SMEM] + [VMEM] * 4,
        name="time_path",
    )(flags, message, marks, gathered, gain)


def finish_kernel(
    scale, part_ref, freq_gain, freq_in, freq_taps, freq_out, time_gain, time_in, time_taps, time_out
):
    freq_w = jnp.concatenate([part_ref[i, 0:16, :] for i in range(4)], axis=0) * scale
    time_w = jnp.concatenate([part_ref[i, 0:16, :] for i in range(4, 8)], axis=0) * scale
    freq_out[...] = freq_w[:, :64]
    freq_in[...] = freq_w[:, 64:].T
    time_out[...] = time_w[:, :64]
    time_in[...] = time_w[:, 64:].T
    first, second = part_ref[0, 16:24, :] * scale, part_ref[1, 16:24, :] * scale
    freq_gain[...] = second[4:5, :64]
    time_gain[...] = second[4:5, 64:]
    freq_taps[...] = first[0:3, :64]
    time_taps[0] = first[3:6, :64]
    time_taps[1, 0:2] = first[6:8, :64]
    time_taps[1, 2:3] = second[0:1, :64]
    time_taps[2] = second[1:4, :64]


def finish(total, scale):
    shape = lambda *dims: jax.ShapeDtypeStruct(dims, F32)
    got = pl.pallas_call(
        functools.partial(finish_kernel, scale),
        out_shape=(
            shape(1, 64),
            shape(64, 64),
            shape(3, 64),
            shape(64, 64),
            shape(1, 64),
            shape(64, 64),
            shape(3, 3, 64),
            shape(64, 64),
        ),
        in_specs=[VMEM],
        name="finish",
    )(total)
    return (got[0][0], got[1], got[2], got[3], got[4][0], got[5], got[6], got[7])


def plane_lanes(values, plane):
    frames, width = values.shape
    padded = jnp.pad(values, ((0, 0), (LEAD * 64, (ROWS - LEAD + 192) * 64 - width)))
    return lax.dynamic_slice(padded, (0, plane * 4096), (frames, ROWS * 64))


def cot_message(own, halo):
    both = jnp.concatenate([own, halo], axis=0)
    mine = both[:, LEAD * 64 : LEAD * 64 + 4096].reshape(2 * FR, 32, 128).transpose(1, 0, 2)
    edge = jnp.stack([both[:, LEAD * 64 - 64 : LEAD * 64], both[:, LEAD * 64 + 4096 : LEAD * 64 + 4160]], axis=0)
    return near(mine), near(jnp.concatenate([edge[:, :FR], edge[:, FR:]], axis=2))


def frame_marks(counts, x_at):
    by_plane = jnp.pad(counts.reshape(4, 32), ((1, 1), (0, 0)))
    window = lax.dynamic_slice(by_plane, (x_at, 0), (3, 32))
    spot = jnp.arange(32)
    halo_count = jnp.where(spot >= 16, window[0], window[2])
    halo_in = jnp.where(spot >= 16, (spot >= 21) & (x_at > 0), (spot <= 10) & (x_at < 3))
    limit = jnp.stack([window[1], halo_count], axis=1)
    valid = (jnp.arange(4) < limit[:, :, None]) & jnp.stack([spot >= 0, halo_in], axis=1)[:, :, None]
    inside = jnp.stack([spot >= 0, halo_in], axis=1)[:, :, None] & (jnp.arange(4) >= 0)
    return jnp.stack([valid.reshape(256), inside.reshape(256)], axis=1).astype(F32)


def outputs_of(blocks, plane):
    twice = jnp.stack(blocks[::-1] + blocks[::-1], axis=0)
    rows = lax.dynamic_slice(twice, (3 - plane, 0, 0), (4, 288, 128)).reshape(4, FR, 72, 128)
    whole = jnp.concatenate([rows[0, :, :64], rows[1, :, :64], rows[2, :, :64], rows[3, :, :65]], axis=1)
    return whole[:, :, :64].reshape(FR, -1), whole[:, :, 64:].reshape(FR, -1)


def halo_pairs():
    pairs = []
    for x_at in range(4):
        for spot in range(32):
            if spot <= 10 and x_at < 3:
                pairs.append(((x_at + 1) * 32 + spot, x_at * 32 + spot))
            if spot >= 21 and x_at > 0:
                pairs.append(((x_at - 1) * 32 + spot, x_at * 32 + spot))
    return pairs


SEQ = ("x", "z", "core")


def exchange(values, axes):
    return lax.all_to_all(values, axes, 0, 0)


def near(values):
    return pltpu.with_memory_space_constraint(values, pltpu.VMEM)


def shards(
    signal, cotangent, counts, freq_gain, freq_in, freq_taps, freq_out, time_gain, time_in, time_taps, time_out
):
    plane = lax.axis_index("ch")
    x_at = lax.axis_index("x")
    spot = lax.axis_index(("z", "core"))
    grad_scale = 1.0 / math.sqrt(FR * 128 * (signal.shape[1] // 64))
    packed = pack(freq_in, freq_taps, freq_out, time_in, time_taps, time_out)
    gathered = exchange(packed, "ch")
    gathered = near(gathered)
    lanes = jnp.stack([plane_lanes(signal, plane), plane_lanes(cotangent, plane)], axis=0)
    halo = lax.ppermute(lanes, SEQ, halo_pairs())
    gain_f, gain_t = freq_gain[None], time_gain[None]
    x_rows, x_halo = near(lanes[0].reshape(FR * ROWS, 64)), near(halo[0].reshape(FR * ROWS, 64))
    message, hidden = freq_forward(x_rows, x_halo, *cot_message(lanes[1], halo[1]), gathered, gain_f)
    bands = near(exchange(message, ("z", "core")))
    marks = near(frame_marks(counts, x_at))
    beside = (spot == EDGE) | (spot == EDGE + 1)
    edge = jnp.stack([jnp.where((plane == 3) & (spot == EDGE + 1), 1, 0), jnp.where(beside, 1, 0)])
    mixed, *sums = time_path(bands, marks, gathered, gain_t, edge)
    arrived = near(exchange(mixed, ("z", "core")))
    flags = jnp.stack([jnp.where(plane == 3, 1, 0), jnp.where(plane > 0, 1, 0)])
    done, pieces = freq_backward(x_rows, hidden, arrived, gathered, gain_f, flags, sums)
    part = exchange(pieces, ("x", "core", "ch"))
    part = jnp.broadcast_to(jnp.sum(part.astype(F32), axis=0).astype(BF), (16, 24, 128))
    blocks = [done]
    for shift in (1, 2, 3):
        blocks.append(lax.ppermute(done, "ch", [(i, (i + shift) % 4) for i in range(4)]))
    part = exchange(part, "z")
    part = jnp.sum(part.astype(F32), axis=0)
    total = near(exchange(jnp.broadcast_to(part, (8, 24, 128)), ("x", "core")))
    return outputs_of(blocks, plane) + finish(total, grad_scale)


def solution(mesh):
    torus = Mesh(mesh.devices.reshape(4, 16, 2, 4), ("x", "z", "core", "ch"))
    return jax.shard_map(
        shards,
        mesh=torus,
        in_specs=(
            P(SEQ, None),
            P(SEQ, None),
            P(),
            P(),
            P(None, "ch"),
            P(None, "ch"),
            P("ch", None),
            P(),
            P(None, "ch"),
            P(None, None, "ch"),
            P("ch", None),
        ),
        out_specs=(
            P(SEQ, None),
            P(SEQ, None),
            P(),
            P(None, "ch"),
            P(None, "ch"),
            P("ch", None),
            P(),
            P(None, "ch"),
            P(None, None, "ch"),
            P("ch", None),
        ),
        check_vma=False,
    )
```

```python
import functools
import math

import jax
import jax.numpy as jnp
from jax import lax
from jax.experimental import pallas as pl
from jax.experimental.pallas import tpu as pltpu
from jax.sharding import Mesh, PartitionSpec as P


EPS = 1e-05
FR = 4
ROWS = 80
LEAD = 8
EDGE = 16
BF = jnp.bfloat16
F32 = jnp.float32


def nt(a, b):
    return lax.dot_general(a, b, (((1,), (1,)), ((), ())), preferred_element_type=F32)


def nn(a, b):
    return lax.dot_general(a, b, (((1,), (0,)), ((), ())), preferred_element_type=F32)


def tn(a, b):
    return lax.dot_general(a, b, (((0,), (0,)), ((), ())), preferred_element_type=F32)


def roll_rows(values, amount):
    return pltpu.roll(values, amount % values.shape[0], 0)


def sigmoid(values):
    return 0.5 * jnp.tanh(0.5 * values) + 0.5


def inverse_norm(features):
    return lax.rsqrt(jnp.mean(features * features, axis=-1, keepdims=True) + EPS)


def norm_back(d_normed, features, scale, gain):
    scaled = d_normed * gain
    summed = jnp.sum(scaled * features, axis=-1, keepdims=True)
    return scale * scaled - features * (scale * scale * scale * summed * (1.0 / features.shape[-1]))


def bins_conv(values, taps):
    return taps[0:1] * roll_rows(values, 1) + taps[1:2] * values + taps[2:3] * roll_rows(values, -1)


VMEM = pl.BlockSpec(memory_space=pltpu.VMEM)
SMEM = pl.BlockSpec(memory_space=pltpu.SMEM)


HALVES = (slice(0, 128), slice(128, 256))


def half_weights(gathered_ref, half, first):
    return jnp.concatenate([gathered_ref[2 * half + i, first : first + 64, :] for i in range(2)], axis=0)


def half_taps(gathered_ref, half, first, count):
    parts = []
    for i in range(2):
        both = gathered_ref[2 * half + i, 128:144, :].astype(F32)
        parts.append((both[:, :64] + both[:, 64:])[first : first + count])
    return jnp.concatenate(parts, axis=1)


def pack_kernel(freq_in, freq_taps, freq_out, time_in, time_taps, time_out, packed_ref):
    taps = jnp.concatenate(
        [freq_taps[...]] + [time_taps[k] for k in range(3)] + [jnp.zeros((4, 64), F32)], axis=0
    )
    high = taps.astype(BF).astype(F32)
    low = taps - high
    turn = lambda ref: ref[...].astype(F32).T.astype(BF)
    freq_w = jnp.concatenate([turn(freq_in), freq_out[...]], axis=1)
    time_w = jnp.concatenate([turn(time_in), time_out[...]], axis=1)
    tap_w = jnp.concatenate([high, low], axis=1).astype(BF)
    for peer in range(4):
        packed_ref[peer, 0:64, :] = freq_w
        packed_ref[peer, 64:128, :] = time_w
        packed_ref[peer, 128:144, :] = tap_w


def pack(*weights):
    return pl.pallas_call(
        pack_kernel, out_shape=pltpu.VMEM((4, 144, 128), BF), name="pack"
    )(*weights)


def freq_forward_kernel(
    own_ref, halo_ref, cot_ref, cot_edge_ref, gathered_ref, gain_ref, out_ref, hidden_out, rows_ref, tiles_ref
):
    gain = gain_ref[...]
    edges = []
    for part, pair_ref in enumerate((own_ref, halo_ref)):
        features = pair_ref[...].astype(F32)
        normed = (features * inverse_norm(features) * gain).astype(BF)
        mixed = features
        for half, lanes in enumerate(HALVES):
            weights = half_weights(gathered_ref, half, 0)
            hidden = nt(normed, weights[:, :64])
            if part == 0:
                hidden_out[:, lanes] = hidden
            drive = bins_conv(hidden, half_taps(gathered_ref, half, 0, 3))
            active = (drive * sigmoid(drive)).astype(BF)
            mixed = mixed + nn(active, weights[:, 64:])
        rows_ref[...] = mixed
        for f in range(FR):
            even = rows_ref[pl.ds(f * ROWS + LEAD, 32, stride=2), :]
            odd = rows_ref[pl.ds(f * ROWS + LEAD + 1, 32, stride=2), :]
            tiles_ref[pl.ds(FR * part + f, 32, stride=8), :] = jnp.concatenate([even, odd], axis=1)
        for bin_row in (LEAD - 1, LEAD + 64):
            edges.append(
                jnp.concatenate([mixed[f * ROWS + bin_row : f * ROWS + bin_row + 1] for f in range(FR)], axis=0)
            )
    out_ref[:, 0:8, :] = tiles_ref[...].reshape(32, 8, 128).astype(BF)
    out_ref[:, 8:16, :] = cot_ref[...]
    out_ref[0:EDGE, 16:24, :] = jnp.zeros((EDGE, 8, 128), BF)
    out_ref[EDGE + 2 : 32, 16:24, :] = jnp.zeros((30 - EDGE, 8, 128), BF)
    for side in range(2):
        x_edge = jnp.concatenate([edges[side], edges[2 + side]], axis=1)
        out_ref[EDGE + side, 16:24, :] = jnp.concatenate([x_edge, cot_edge_ref[side].astype(F32)], axis=0).astype(BF)


def freq_forward(pair, halo, cot, cot_edge, gathered, gain):
    rows = pair.shape[0]
    return pl.pallas_call(
        freq_forward_kernel,
        out_shape=(pltpu.VMEM((32, 24, 128), BF), pltpu.VMEM((rows, 256), F32)),
        scratch_shapes=[
            pltpu.VMEM((rows, 64), F32),
            pltpu.VMEM((256, 128), F32),
        ],
        name="freq_forward",
    )(pair, halo, cot, cot_edge, gathered, gain)


def freq_backward_kernel(
    flag_ref,
    pair_ref,
    hidden_ref,
    arrived_ref,
    gathered_ref,
    gain_ref,
    time_w_ref,
    time_t_ref,
    time_g_ref,
    done_ref,
    out_ref,
    tiles_ref,
    back_ref,
):
    gain = gain_ref[...]
    spread = jnp.concatenate([arrived_ref[...].astype(F32), jnp.zeros((32, 4, 128), F32)], axis=1)
    tiles_ref[...] = spread.reshape(512, 128)
    back_ref[...] = jnp.zeros_like(back_ref)
    left = flag_ref[1].astype(F32)
    for f in range(FR):
        back_ref[pl.ds(f * ROWS + LEAD, 32, stride=2), :] = tiles_ref[pl.ds(f, 32, stride=16), :]
        back_ref[pl.ds(f * ROWS + LEAD + 1, 32, stride=2), :] = tiles_ref[pl.ds(FR + f, 32, stride=16), :]
        back_ref[f * ROWS + LEAD - 1 : f * ROWS + LEAD, :] = tiles_ref[16 * EDGE + 8 + f : 16 * EDGE + 9 + f, :] * left
        back_ref[f * ROWS + LEAD + 64 : f * ROWS + LEAD + 65, :] = tiles_ref[16 * EDGE + 24 + f : 16 * EDGE + 25 + f, :]
    row = lax.broadcasted_iota(jnp.int32, (ROWS, 1), 0)
    upper = LEAD + 64 + flag_ref[0]
    one = jnp.where((row >= LEAD) & (row < upper), 1.0, 0.0).astype(F32)
    own = jnp.concatenate([one] * FR, axis=0)
    features = pair_ref[...].astype(F32)
    scale = inverse_norm(features)
    output, grad_wide = back_ref[:, :64], back_ref[:, 64:]
    grad = grad_wide.astype(BF)
    grad_own = (grad_wide * own).astype(BF)
    normed = (features * scale * gain * own).astype(BF)
    d_normed = None
    tap_halves, freq_w = [], []
    for half, lanes in enumerate(HALVES):
        weights = half_weights(gathered_ref, half, 0)
        taps = half_taps(gathered_ref, half, 0, 3)
        hidden = hidden_ref[:, lanes]
        before, after = roll_rows(hidden, 1), roll_rows(hidden, -1)
        drive = taps[0:1] * before + taps[1:2] * hidden + taps[2:3] * after
        gate = sigmoid(drive)
        active = drive * gate
        slope = gate + active * (1.0 - gate)
        grad_out = tn(active.astype(BF), grad_own)
        d_drive = nt(grad, weights[:, 64:]) * slope
        d_own = d_drive * own
        tap_halves.append(
            [jnp.sum(d_own * moved, axis=0, keepdims=True) for moved in (before, hidden, after)]
        )
        d_hidden = (
            taps[0:1] * roll_rows(d_drive, -1) + taps[1:2] * d_drive + taps[2:3] * roll_rows(d_drive, 1)
        ).astype(BF)
        grad_in = tn(d_hidden, normed)
        freq_w.append(jnp.concatenate([grad_out, grad_in], axis=1))
        part = nn(d_hidden, weights[:, :64])
        d_normed = part if d_normed is None else d_normed + part
    freq_g = jnp.sum(d_normed * features * (scale * own), axis=0, keepdims=True)
    d_signal = grad_wide + norm_back(d_normed, features, scale, gain)
    done = jnp.concatenate([output, d_signal], axis=1)
    done = jnp.concatenate([done[f * ROWS + LEAD : (f + 1) * ROWS] for f in range(FR)], axis=0).astype(BF)
    done_ref[...] = done
    gains = jnp.concatenate([freq_g, time_g_ref[...]], axis=1)
    for peer in range(4):
        half, at = peer // 2, 64 * (peer % 2)
        rows = [tap[:, at : at + 64] for tap in tap_halves[half]]
        rows.append(time_t_ref[:, 64 * peer : 64 * peer + 64])
        taps = jnp.concatenate(rows, axis=0)
        taps = jnp.concatenate([taps, jnp.zeros((12, 64), F32)], axis=1)
        taps = jnp.concatenate([taps, gains, jnp.zeros((3, 128), F32)], axis=0)
        for i in range(8):
            if i < 4:
                piece = freq_w[half][at + 16 * i : at + 16 * i + 16]
            else:
                piece = time_w_ref[64 * peer + 16 * i - 64 : 64 * peer + 16 * i - 48, :]
            small = taps[8 * i : 8 * i + 8] if i < 2 else jnp.zeros((8, 128), F32)
            out_ref[4 * i + peer] = jnp.concatenate([piece, small], axis=0).astype(BF)


def freq_backward(pair, hidden, arrived, gathered, gain, flags, sums):
    return pl.pallas_call(
        freq_backward_kernel,
        out_shape=(pltpu.VMEM((288, 128), BF), pltpu.VMEM((32, 24, 128), BF)),
        in_specs=[SMEM] + [VMEM] * 8,
        scratch_shapes=[
            pltpu.VMEM((512, 128), F32),
            pltpu.VMEM((FR * ROWS, 128), F32),
        ],
        name="freq_backward",
    )(flags, pair, near(hidden), arrived, gathered, gain, *[near(part) for part in sums])


def turned(tiles):
    return jnp.concatenate(
        [roll_rows(tiles[8 * i : 8 * i + 8], 4) for i in range(tiles.shape[0] // 8)], axis=0
    )


def groups_on(values, count):
    if count > 0:
        return jnp.concatenate([values[8 * count :], turned(values[: 8 * count])], axis=0)
    base = values.shape[0] + 8 * count
    return jnp.concatenate([turned(values[base:]), values[:base]], axis=0)


def tiled(values):
    return values.reshape(values.shape[0] // 8, 8, values.shape[1])


def next_frame(values, place, edge, amount):
    near_rows = pltpu.roll(tiled(values), amount % 8, 1)
    far_rows = pltpu.roll(tiled(groups_on(values, -amount)), (-3 * amount) % 8, 1)
    return jnp.where((place == edge)[None], far_rows, near_rows).reshape(values.shape)


def later(values, spacing, place):
    return next_frame(values, place, 3, -1) if spacing == 1 else groups_on(values, spacing // FR)


def earlier(values, spacing, place):
    return next_frame(values, place, 0, 1) if spacing == 1 else groups_on(values, -(spacing // FR))


def own_rows(values):
    tiles = values.reshape(values.shape[0] // 8, 8, values.shape[1])
    return jnp.sum(jnp.sum(tiles, axis=0)[:4], axis=0, keepdims=True)


def one_bin(message_ref, first, slot):
    if slot < 2:
        both = message_ref[:, 8 * first : 8 * first + 8].astype(F32).reshape(256, 128)
        return both[:, 64 * slot : 64 * slot + 64]
    edge = message_ref[:, 16:24].astype(F32)[:, 4 * first : 4 * first + 4]
    return jnp.concatenate([edge[:, :, :64], edge[:, :, 64:]], axis=1).reshape(256, 64)


def time_kernel(
    flag_ref,
    message_ref,
    marks_ref,
    gathered_ref,
    gain_ref,
    out_ref,
    grad_ref,
    tap_ref,
    gain_out,
):
    gain = gain_ref[...]
    valid, inside = marks_ref[:, 0:1], marks_ref[:, 1:2]
    spot = lax.broadcasted_iota(jnp.int32, (256, 1), 0)
    place = lax.broadcasted_iota(jnp.int32, (8, 128), 0) & 3

    def work(slot):
        share = jnp.where(flag_ref[0] > 0, 1.0, 0.0).astype(F32) if slot == 2 else 1.0

        def keep(ref, rows, lanes, value):
            if slot == 0:
                ref[rows, lanes] = value
            else:
                ref[rows, lanes] += value

        counted = jnp.where((spot & 7) < 4, share, 0.0).astype(F32)
        features, grad_wide = one_bin(message_ref, 0, slot), one_bin(message_ref, 1, slot)
        grad = grad_wide.astype(BF)
        grad_own = (grad_wide * counted).astype(BF)
        scale = inverse_norm(features)
        normed = features * scale * gain
        normed_own = (normed * counted).astype(BF)
        normed = normed.astype(BF)
        mixed, d_normed = features, None
        for side, lanes in enumerate(HALVES):
            weights = half_weights(gathered_ref, side, 64)
            weight_in, weight_out = weights[:, :64], weights[:, 64:]
            half = 0.5 * half_taps(gathered_ref, side, 3, 9)
            state = nt(normed, weight_in) * valid
            states, slopes = [], []
            for layer in range(3):
                spacing = (1, 4, 16)[layer]
                row = half[3 * layer : 3 * layer + 3]
                around = (earlier(state, spacing, place), state, later(state, spacing, place))
                drive = row[0:1] * around[0] + row[1:2] * state + row[2:3] * around[2]
                opened = jnp.tanh(drive) + 1.0
                active = drive * opened
                states.append(around)
                slopes.append(opened + active * (2.0 - opened))
                state = state + active
                if layer < 2:
                    state = state * inside
            top = state.astype(BF)
            mixed = mixed + nn(top, weight_out)
            keep(grad_ref, lanes, slice(0, 64), tn(top, grad_own))
            d_state = nt(grad, weight_out)
            for layer in reversed(range(3)):
                spacing = (1, 4, 16)[layer]
                row = half[3 * layer : 3 * layer + 3]
                d_drive = d_state * slopes[layer]
                if layer < 2:
                    d_drive = d_drive * inside
                for j, moved in enumerate(states[layer]):
                    at = 3 * layer + j
                    keep(tap_ref, slice(at, at + 1), lanes, own_rows(d_drive * moved) * (0.5 * share))
                d_state = d_state + (
                    row[0:1] * later(d_drive, spacing, place)
                    + row[1:2] * d_drive
                    + row[2:3] * earlier(d_drive, spacing, place)
                )
            d_pre = (d_state * valid).astype(BF)
            keep(grad_ref, lanes, slice(64, 128), tn(d_pre, normed_own))
            part = nn(d_pre, weight_in)
            d_normed = part if d_normed is None else d_normed + part
        keep(gain_out, slice(0, 1), slice(0, 64), own_rows(d_normed * features * scale) * share)
        d_one = grad_wide + norm_back(d_normed, features, scale, gain)
        both = jnp.concatenate([mixed, d_one], axis=1).reshape(32, 8, 128)
        out_ref[:, 4 * slot : 4 * slot + 4] = both[:, :4].astype(BF)

    work(0)
    work(1)

    @pl.when(flag_ref[1] > 0)
    def _():
        work(2)

    @pl.when(flag_ref[1] == 0)
    def _():
        out_ref[:, 8:12] = jnp.zeros((32, 4, 128), BF)


def time_path(message, marks, gathered, gain, flags):
    return pl.pallas_call(
        time_kernel,
        out_shape=(
            pltpu.VMEM((32, 12, 128), BF),
            pltpu.VMEM((256, 128), F32),
            pltpu.VMEM((9, 256), F32),
            pltpu.VMEM((1, 64), F32),
        ),
        in_specs=[SMEM] + [VMEM] * 4,
        name="time_path",
    )(flags, message, marks, gathered, gain)


def finish_kernel(
    scale, part_ref, freq_gain, freq_in, freq_taps, freq_out, time_gain, time_in, time_taps, time_out
):
    freq_w = jnp.concatenate([part_ref[i, 0:16, :] for i in range(4)], axis=0) * scale
    time_w = jnp.concatenate([part_ref[i, 0:16, :] for i in range(4, 8)], axis=0) * scale
    freq_out[...] = freq_w[:, :64]
    freq_in[...] = freq_w[:, 64:].T
    time_out[...] = time_w[:, :64]
    time_in[...] = time_w[:, 64:].T
    first, second = part_ref[0, 16:24, :] * scale, part_ref[1, 16:24, :] * scale
    freq_gain[...] = second[4:5, :64]
    time_gain[...] = second[4:5, 64:]
    freq_taps[...] = first[0:3, :64]
    time_taps[0] = first[3:6, :64]
    time_taps[1, 0:2] = first[6:8, :64]
    time_taps[1, 2:3] = second[0:1, :64]
    time_taps[2] = second[1:4, :64]


def finish(total, scale):
    shape = lambda *dims: jax.ShapeDtypeStruct(dims, F32)
    got = pl.pallas_call(
        functools.partial(finish_kernel, scale),
        out_shape=(
            shape(1, 64),
            shape(64, 64),
            shape(3, 64),
            shape(64, 64),
            shape(1, 64),
            shape(64, 64),
            shape(3, 3, 64),
            shape(64, 64),
        ),
        in_specs=[VMEM],
        name="finish",
    )(total)
    return (got[0][0], got[1], got[2], got[3], got[4][0], got[5], got[6], got[7])


def plane_lanes(values, plane):
    frames, width = values.shape
    padded = jnp.pad(values, ((0, 0), (LEAD * 64, (ROWS - LEAD + 192) * 64 - width)))
    return lax.dynamic_slice(padded, (0, plane * 4096), (frames, ROWS * 64))


def cot_message(own, halo):
    both = jnp.concatenate([own, halo], axis=0)
    mine = both[:, LEAD * 64 : LEAD * 64 + 4096].reshape(2 * FR, 32, 128).transpose(1, 0, 2)
    edge = jnp.stack([both[:, LEAD * 64 - 64 : LEAD * 64], both[:, LEAD * 64 + 4096 : LEAD * 64 + 4160]], axis=0)
    return near(mine), near(jnp.concatenate([edge[:, :FR], edge[:, FR:]], axis=2))


def frame_marks(counts, x_at):
    by_plane = jnp.pad(counts.reshape(4, 32), ((1, 1), (0, 0)))
    window = lax.dynamic_slice(by_plane, (x_at, 0), (3, 32))
    spot = jnp.arange(32)
    halo_count = jnp.where(spot >= 16, window[0], window[2])
    halo_in = jnp.where(spot >= 16, (spot >= 21) & (x_at > 0), (spot <= 10) & (x_at < 3))
    limit = jnp.stack([window[1], halo_count], axis=1)
    valid = (jnp.arange(4) < limit[:, :, None]) & jnp.stack([spot >= 0, halo_in], axis=1)[:, :, None]
    inside = jnp.stack([spot >= 0, halo_in], axis=1)[:, :, None] & (jnp.arange(4) >= 0)
    return jnp.stack([valid.reshape(256), inside.reshape(256)], axis=1).astype(F32)


def outputs_of(blocks, plane):
    twice = jnp.stack(blocks[::-1] + blocks[::-1], axis=0)
    rows = lax.dynamic_slice(twice, (3 - plane, 0, 0), (4, 288, 128)).reshape(4, FR, 72, 128)
    whole = jnp.concatenate([rows[0, :, :64], rows[1, :, :64], rows[2, :, :64], rows[3, :, :65]], axis=1)
    return whole[:, :, :64].reshape(FR, -1), whole[:, :, 64:].reshape(FR, -1)


def halo_pairs():
    pairs = []
    for x_at in range(4):
        for spot in range(32):
            if spot <= 10 and x_at < 3:
                pairs.append(((x_at + 1) * 32 + spot, x_at * 32 + spot))
            if spot >= 21 and x_at > 0:
                pairs.append(((x_at - 1) * 32 + spot, x_at * 32 + spot))
    return pairs


SEQ = ("x", "z", "core")


def exchange(values, axes):
    return lax.all_to_all(values, axes, 0, 0)


def near(values):
    return pltpu.with_memory_space_constraint(values, pltpu.VMEM)


def shards(
    signal, cotangent, counts, freq_gain, freq_in, freq_taps, freq_out, time_gain, time_in, time_taps, time_out
):
    plane = lax.axis_index("ch")
    x_at = lax.axis_index("x")
    spot = lax.axis_index(("z", "core"))
    grad_scale = 1.0 / math.sqrt(FR * 128 * (signal.shape[1] // 64))
    packed = pack(freq_in, freq_taps, freq_out, time_in, time_taps, time_out)
    gathered = exchange(packed, "ch")
    gathered = near(gathered)
    lanes = jnp.stack([plane_lanes(signal, plane), plane_lanes(cotangent, plane)], axis=0)
    halo = lax.ppermute(lanes, SEQ, halo_pairs())
    gain_f, gain_t = freq_gain[None], time_gain[None]
    x_rows, x_halo = near(lanes[0].reshape(FR * ROWS, 64)), near(halo[0].reshape(FR * ROWS, 64))
    message, hidden = freq_forward(x_rows, x_halo, *cot_message(lanes[1], halo[1]), gathered, gain_f)
    bands = near(exchange(message, ("z", "core")))
    marks = near(frame_marks(counts, x_at))
    beside = (spot == EDGE) | (spot == EDGE + 1)
    edge = jnp.stack([jnp.where((plane == 3) & (spot == EDGE + 1), 1, 0), jnp.where(beside, 1, 0)])
    mixed, *sums = time_path(bands, marks, gathered, gain_t, edge)
    arrived = near(exchange(mixed, ("z", "core")))
    flags = jnp.stack([jnp.where(plane == 3, 1, 0), jnp.where(plane > 0, 1, 0)])
    done, pieces = freq_backward(x_rows, hidden, arrived, gathered, gain_f, flags, sums)
    part = exchange(pieces, ("x", "core", "ch"))
    part = jnp.broadcast_to(jnp.sum(part.astype(F32), axis=0).astype(BF), (16, 24, 128))
    blocks = [done]
    for shift in (1, 2, 3):
        blocks.append(lax.ppermute(done, "ch", [(i, (i + shift) % 4) for i in range(4)]))
    part = exchange(part, "z")
    part = jnp.sum(part.astype(F32), axis=0)
    total = near(exchange(jnp.broadcast_to(part, (8, 24, 128)), ("x", "core")))
    return outputs_of(blocks, plane) + finish(total, grad_scale)


def solution(mesh):
    torus = Mesh(mesh.devices.reshape(4, 16, 2, 4), ("x", "z", "core", "ch"))
    return jax.shard_map(
        shards,
        mesh=torus,
        in_specs=(
            P(SEQ, None),
            P(SEQ, None),
            P(),
            P(),
            P(None, "ch"),
            P(None, "ch"),
            P("ch", None),
            P(),
            P(None, "ch"),
            P(None, None, "ch"),
            P("ch", None),
        ),
        out_specs=(
            P(SEQ, None),
            P(SEQ, None),
            P(),
            P(None, "ch"),
            P(None, "ch"),
            P("ch", None),
            P(),
            P(None, "ch"),
            P(None, None, "ch"),
            P("ch", None),
        ),
        check_vma=False,
    )
```

```python
import functools
import math

import jax
import jax.numpy as jnp
from jax import lax
from jax.experimental import pallas as pl
from jax.experimental.pallas import tpu as pltpu
from jax.sharding import Mesh, PartitionSpec as P


EPS = 1e-05
FR = 4
ROWS = 80
LEAD = 8
EDGE = 16
BF = jnp.bfloat16
F32 = jnp.float32


def nt(a, b):
    return lax.dot_general(a, b, (((1,), (1,)), ((), ())), preferred_element_type=F32)


def nn(a, b):
    return lax.dot_general(a, b, (((1,), (0,)), ((), ())), preferred_element_type=F32)


def tn(a, b):
    return lax.dot_general(a, b, (((0,), (0,)), ((), ())), preferred_element_type=F32)


def roll_rows(values, amount):
    return pltpu.roll(values, amount % values.shape[0], 0)


def sigmoid(values):
    return 0.5 * jnp.tanh(0.5 * values) + 0.5


def inverse_norm(features):
    return lax.rsqrt(jnp.mean(features * features, axis=-1, keepdims=True) + EPS)


def norm_back(d_normed, features, scale, gain):
    scaled = d_normed * gain
    summed = jnp.sum(scaled * features, axis=-1, keepdims=True)
    return scale * scaled - features * (scale * scale * scale * summed * (1.0 / features.shape[-1]))


def bins_conv(values, taps):
    return taps[0:1] * roll_rows(values, 1) + taps[1:2] * values + taps[2:3] * roll_rows(values, -1)


VMEM = pl.BlockSpec(memory_space=pltpu.VMEM)
SMEM = pl.BlockSpec(memory_space=pltpu.SMEM)


HALVES = (slice(0, 128), slice(128, 256))


def half_weights(gathered_ref, half, first):
    return jnp.concatenate([gathered_ref[2 * half + i, first : first + 64, :] for i in range(2)], axis=0)


def half_taps(gathered_ref, half, first, count):
    parts = []
    for i in range(2):
        both = gathered_ref[2 * half + i, 128:144, :].astype(F32)
        parts.append((both[:, :64] + both[:, 64:])[first : first + count])
    return jnp.concatenate(parts, axis=1)


def pack_kernel(freq_in, freq_taps, freq_out, time_in, time_taps, time_out, packed_ref):
    taps = jnp.concatenate(
        [freq_taps[...]] + [time_taps[k] for k in range(3)] + [jnp.zeros((4, 64), F32)], axis=0
    )
    high = taps.astype(BF).astype(F32)
    low = taps - high
    turn = lambda ref: ref[...].astype(F32).T.astype(BF)
    freq_w = jnp.concatenate([turn(freq_in), freq_out[...]], axis=1)
    time_w = jnp.concatenate([turn(time_in), time_out[...]], axis=1)
    tap_w = jnp.concatenate([high, low], axis=1).astype(BF)
    for peer in range(4):
        packed_ref[peer, 0:64, :] = freq_w
        packed_ref[peer, 64:128, :] = time_w
        packed_ref[peer, 128:144, :] = tap_w


def pack(*weights):
    return pl.pallas_call(
        pack_kernel, out_shape=pltpu.VMEM((4, 144, 128), BF), name="pack"
    )(*weights)


def freq_forward_kernel(
    own_ref, halo_ref, cot_ref, cot_edge_ref, gathered_ref, gain_ref, out_ref, hidden_out, rows_ref, tiles_ref
):
    gain = gain_ref[...]
    edges = []
    for part, pair_ref in enumerate((own_ref, halo_ref)):
        features = pair_ref[...].astype(F32)
        normed = (features * inverse_norm(features) * gain).astype(BF)
        mixed = features
        for half, lanes in enumerate(HALVES):
            weights = half_weights(gathered_ref, half, 0)
            hidden = nt(normed, weights[:, :64])
            if part == 0:
                hidden_out[:, lanes] = hidden
            drive = bins_conv(hidden, half_taps(gathered_ref, half, 0, 3))
            active = (drive * sigmoid(drive)).astype(BF)
            mixed = mixed + nn(active, weights[:, 64:])
        rows_ref[...] = mixed
        for f in range(FR):
            even = rows_ref[pl.ds(f * ROWS + LEAD, 32, stride=2), :]
            odd = rows_ref[pl.ds(f * ROWS + LEAD + 1, 32, stride=2), :]
            tiles_ref[pl.ds(FR * part + f, 32, stride=8), :] = jnp.concatenate([even, odd], axis=1)
        for bin_row in (LEAD - 1, LEAD + 64):
            edges.append(
                jnp.concatenate([mixed[f * ROWS + bin_row : f * ROWS + bin_row + 1] for f in range(FR)], axis=0)
            )
    out_ref[:, 0:8, :] = tiles_ref[...].reshape(32, 8, 128).astype(BF)
    out_ref[:, 8:16, :] = cot_ref[...]
    out_ref[0:EDGE, 16:24, :] = jnp.zeros((EDGE, 8, 128), BF)
    out_ref[EDGE + 2 : 32, 16:24, :] = jnp.zeros((30 - EDGE, 8, 128), BF)
    for side in range(2):
        x_edge = jnp.concatenate([edges[side], edges[2 + side]], axis=1)
        out_ref[EDGE + side, 16:24, :] = jnp.concatenate([x_edge, cot_edge_ref[side].astype(F32)], axis=0).astype(BF)


def freq_forward(pair, halo, cot, cot_edge, gathered, gain):
    rows = pair.shape[0]
    return pl.pallas_call(
        freq_forward_kernel,
        out_shape=(pltpu.VMEM((32, 24, 128), BF), pltpu.VMEM((rows, 256), F32)),
        scratch_shapes=[
            pltpu.VMEM((rows, 64), F32),
            pltpu.VMEM((256, 128), F32),
        ],
        name="freq_forward",
    )(pair, halo, cot, cot_edge, gathered, gain)


def freq_backward_kernel(
    flag_ref,
    pair_ref,
    hidden_ref,
    arrived_ref,
    gathered_ref,
    gain_ref,
    time_w_ref,
    time_t_ref,
    time_g_ref,
    done_ref,
    out_ref,
    tiles_ref,
    back_ref,
):
    gain = gain_ref[...]
    spread = jnp.concatenate([arrived_ref[...].astype(F32), jnp.zeros((32, 4, 128), F32)], axis=1)
    tiles_ref[...] = spread.reshape(512, 128)
    back_ref[...] = jnp.zeros_like(back_ref)
    left = flag_ref[1].astype(F32)
    for f in range(FR):
        back_ref[pl.ds(f * ROWS + LEAD, 32, stride=2), :] = tiles_ref[pl.ds(f, 32, stride=16), :]
        back_ref[pl.ds(f * ROWS + LEAD + 1, 32, stride=2), :] = tiles_ref[pl.ds(FR + f, 32, stride=16), :]
        back_ref[f * ROWS + LEAD - 1 : f * ROWS + LEAD, :] = tiles_ref[16 * EDGE + 8 + f : 16 * EDGE + 9 + f, :] * left
        back_ref[f * ROWS + LEAD + 64 : f * ROWS + LEAD + 65, :] = tiles_ref[16 * EDGE + 24 + f : 16 * EDGE + 25 + f, :]
    row = lax.broadcasted_iota(jnp.int32, (ROWS, 1), 0)
    upper = LEAD + 64 + flag_ref[0]
    one = jnp.where((row >= LEAD) & (row < upper), 1.0, 0.0).astype(F32)
    own = jnp.concatenate([one] * FR, axis=0)
    features = pair_ref[...].astype(F32)
    scale = inverse_norm(features)
    output, grad_wide = back_ref[:, :64], back_ref[:, 64:]
    grad = grad_wide.astype(BF)
    grad_own = (grad_wide * own).astype(BF)
    normed = (features * scale * gain * own).astype(BF)
    d_normed = None
    tap_halves, freq_w = [], []
    for half, lanes in enumerate(HALVES):
        weights = half_weights(gathered_ref, half, 0)
        taps = half_taps(gathered_ref, half, 0, 3)
        hidden = hidden_ref[:, lanes]
        before, after = roll_rows(hidden, 1), roll_rows(hidden, -1)
        drive = taps[0:1] * before + taps[1:2] * hidden + taps[2:3] * after
        gate = sigmoid(drive)
        active = drive * gate
        slope = gate + active * (1.0 - gate)
        grad_out = tn(active.astype(BF), grad_own)
        d_drive = nt(grad, weights[:, 64:]) * slope
        d_own = d_drive * own
        tap_halves.append(
            [jnp.sum(d_own * moved, axis=0, keepdims=True) for moved in (before, hidden, after)]
        )
        d_hidden = (
            taps[0:1] * roll_rows(d_drive, -1) + taps[1:2] * d_drive + taps[2:3] * roll_rows(d_drive, 1)
        ).astype(BF)
        grad_in = tn(d_hidden, normed)
        freq_w.append(jnp.concatenate([grad_out, grad_in], axis=1))
        part = nn(d_hidden, weights[:, :64])
        d_normed = part if d_normed is None else d_normed + part
    freq_g = jnp.sum(d_normed * features * (scale * own), axis=0, keepdims=True)
    d_signal = grad_wide + norm_back(d_normed, features, scale, gain)
    done = jnp.concatenate([output, d_signal], axis=1)
    done = jnp.concatenate([done[f * ROWS + LEAD : (f + 1) * ROWS] for f in range(FR)], axis=0).astype(BF)
    done_ref[...] = done
    gains = jnp.concatenate([freq_g, time_g_ref[...]], axis=1)
    for peer in range(4):
        half, at = peer // 2, 64 * (peer % 2)
        rows = [tap[:, at : at + 64] for tap in tap_halves[half]]
        rows.append(time_t_ref[:, 64 * peer : 64 * peer + 64])
        taps = jnp.concatenate(rows, axis=0)
        taps = jnp.concatenate([taps, jnp.zeros((12, 64), F32)], axis=1)
        taps = jnp.concatenate([taps, gains, jnp.zeros((3, 128), F32)], axis=0)
        for i in range(8):
            if i < 4:
                piece = freq_w[half][at + 16 * i : at + 16 * i + 16]
            else:
                piece = time_w_ref[64 * peer + 16 * i - 64 : 64 * peer + 16 * i - 48, :]
            small = taps[8 * i : 8 * i + 8] if i < 2 else jnp.zeros((8, 128), F32)
            out_ref[4 * i + peer] = jnp.concatenate([piece, small], axis=0).astype(BF)


def freq_backward(pair, hidden, arrived, gathered, gain, flags, sums):
    return pl.pallas_call(
        freq_backward_kernel,
        out_shape=(pltpu.VMEM((288, 128), BF), pltpu.VMEM((32, 24, 128), BF)),
        in_specs=[SMEM] + [VMEM] * 8,
        scratch_shapes=[
            pltpu.VMEM((512, 128), F32),
            pltpu.VMEM((FR * ROWS, 128), F32),
        ],
        name="freq_backward",
    )(flags, pair, near(hidden), arrived, gathered, gain, *[near(part) for part in sums])


def turned(tiles):
    return jnp.concatenate(
        [roll_rows(tiles[8 * i : 8 * i + 8], 4) for i in range(tiles.shape[0] // 8)], axis=0
    )


def groups_on(values, count):
    if count > 0:
        return jnp.concatenate([values[8 * count :], turned(values[: 8 * count])], axis=0)
    base = values.shape[0] + 8 * count
    return jnp.concatenate([turned(values[base:]), values[:base]], axis=0)


def tiled(values):
    return values.reshape(values.shape[0] // 8, 8, values.shape[1])


def next_frame(values, place, edge, amount):
    near_rows = pltpu.roll(tiled(values), amount % 8, 1)
    far_rows = pltpu.roll(tiled(groups_on(values, -amount)), (-3 * amount) % 8, 1)
    return jnp.where((place == edge)[None], far_rows, near_rows).reshape(values.shape)


def later(values, spacing, place):
    return next_frame(values, place, 3, -1) if spacing == 1 else groups_on(values, spacing // FR)


def earlier(values, spacing, place):
    return next_frame(values, place, 0, 1) if spacing == 1 else groups_on(values, -(spacing // FR))


def own_rows(values):
    tiles = values.reshape(values.shape[0] // 8, 8, values.shape[1])
    return jnp.sum(jnp.sum(tiles, axis=0)[:4], axis=0, keepdims=True)


def one_bin(message_ref, first, slot):
    if slot < 2:
        both = message_ref[:, 8 * first : 8 * first + 8].astype(F32).reshape(256, 128)
        return both[:, 64 * slot : 64 * slot + 64]
    edge = message_ref[:, 16:24].astype(F32)[:, 4 * first : 4 * first + 4]
    return jnp.concatenate([edge[:, :, :64], edge[:, :, 64:]], axis=1).reshape(256, 64)


def time_kernel(
    flag_ref,
    message_ref,
    marks_ref,
    gathered_ref,
    gain_ref,
    out_ref,
    grad_ref,
    tap_ref,
    gain_out,
):
    gain = gain_ref[...]
    valid, inside = marks_ref[:, 0:1], marks_ref[:, 1:2]
    spot = lax.broadcasted_iota(jnp.int32, (256, 1), 0)
    place = lax.broadcasted_iota(jnp.int32, (8, 128), 0) & 3

    def work(slot):
        share = jnp.where(flag_ref[0] > 0, 1.0, 0.0).astype(F32) if slot == 2 else 1.0

        def keep(ref, rows, lanes, value):
            if slot == 0:
                ref[rows, lanes] = value
            else:
                ref[rows, lanes] += value

        counted = jnp.where((spot & 7) < 4, share, 0.0).astype(F32)
        features, grad_wide = one_bin(message_ref, 0, slot), one_bin(message_ref, 1, slot)
        grad = grad_wide.astype(BF)
        grad_own = (grad_wide * counted).astype(BF)
        scale = inverse_norm(features)
        normed = features * scale * gain
        normed_own = (normed * counted).astype(BF)
        normed = normed.astype(BF)
        mixed, d_normed = features, None
        for side, lanes in enumerate(HALVES):
            weights = half_weights(gathered_ref, side, 64)
            weight_in, weight_out = weights[:, :64], weights[:, 64:]
            half = 0.5 * half_taps(gathered_ref, side, 3, 9)
            state = nt(normed, weight_in) * valid
            states, slopes = [], []
            for layer in range(3):
                spacing = (1, 4, 16)[layer]
                row = half[3 * layer : 3 * layer + 3]
                around = (earlier(state, spacing, place), state, later(state, spacing, place))
                drive = row[0:1] * around[0] + row[1:2] * state + row[2:3] * around[2]
                opened = jnp.tanh(drive) + 1.0
                active = drive * opened
                states.append(around)
                slopes.append(opened + active * (2.0 - opened))
                state = state + active
                if layer < 2:
                    state = state * inside
            top = state.astype(BF)
            mixed = mixed + nn(top, weight_out)
            keep(grad_ref, lanes, slice(0, 64), tn(top, grad_own))
            d_state = nt(grad, weight_out)
            for layer in reversed(range(3)):
                spacing = (1, 4, 16)[layer]
                row = half[3 * layer : 3 * layer + 3]
                d_drive = d_state * slopes[layer]
                if layer < 2:
                    d_drive = d_drive * inside
                for j, moved in enumerate(states[layer]):
                    at = 3 * layer + j
                    keep(tap_ref, slice(at, at + 1), lanes, own_rows(d_drive * moved) * (0.5 * share))
                d_state = d_state + (
                    row[0:1] * later(d_drive, spacing, place)
                    + row[1:2] * d_drive
                    + row[2:3] * earlier(d_drive, spacing, place)
                )
            d_pre = (d_state * valid).astype(BF)
            keep(grad_ref, lanes, slice(64, 128), tn(d_pre, normed_own))
            part = nn(d_pre, weight_in)
            d_normed = part if d_normed is None else d_normed + part
        keep(gain_out, slice(0, 1), slice(0, 64), own_rows(d_normed * features * scale) * share)
        d_one = grad_wide + norm_back(d_normed, features, scale, gain)
        both = jnp.concatenate([mixed, d_one], axis=1).reshape(32, 8, 128)
        out_ref[:, 4 * slot : 4 * slot + 4] = both[:, :4].astype(BF)

    work(0)
    work(1)

    @pl.when(flag_ref[1] > 0)
    def _():
        work(2)

    @pl.when(flag_ref[1] == 0)
    def _():
        out_ref[:, 8:12] = jnp.zeros((32, 4, 128), BF)


def time_path(message, marks, gathered, gain, flags):
    return pl.pallas_call(
        time_kernel,
        out_shape=(
            pltpu.VMEM((32, 12, 128), BF),
            pltpu.VMEM((256, 128), F32),
            pltpu.VMEM((9, 256), F32),
            pltpu.VMEM((1, 64), F32),
        ),
        in_specs=[SMEM] + [VMEM] * 4,
        name="time_path",
    )(flags, message, marks, gathered, gain)


def finish_kernel(
    scale, part_ref, freq_gain, freq_in, freq_taps, freq_out, time_gain, time_in, time_taps, time_out
):
    freq_w = jnp.concatenate([part_ref[i, 0:16, :] for i in range(4)], axis=0) * scale
    time_w = jnp.concatenate([part_ref[i, 0:16, :] for i in range(4, 8)], axis=0) * scale
    freq_out[...] = freq_w[:, :64]
    freq_in[...] = freq_w[:, 64:].T
    time_out[...] = time_w[:, :64]
    time_in[...] = time_w[:, 64:].T
    first, second = part_ref[0, 16:24, :] * scale, part_ref[1, 16:24, :] * scale
    freq_gain[...] = second[4:5, :64]
    time_gain[...] = second[4:5, 64:]
    freq_taps[...] = first[0:3, :64]
    time_taps[0] = first[3:6, :64]
    time_taps[1, 0:2] = first[6:8, :64]
    time_taps[1, 2:3] = second[0:1, :64]
    time_taps[2] = second[1:4, :64]


def finish(total, scale):
    shape = lambda *dims: jax.ShapeDtypeStruct(dims, F32)
    got = pl.pallas_call(
        functools.partial(finish_kernel, scale),
        out_shape=(
            shape(1, 64),
            shape(64, 64),
            shape(3, 64),
            shape(64, 64),
            shape(1, 64),
            shape(64, 64),
            shape(3, 3, 64),
            shape(64, 64),
        ),
        in_specs=[VMEM],
        name="finish",
    )(total)
    return (got[0][0], got[1], got[2], got[3], got[4][0], got[5], got[6], got[7])


def plane_lanes(values, plane):
    frames, width = values.shape
    padded = jnp.pad(values, ((0, 0), (LEAD * 64, (ROWS - LEAD + 192) * 64 - width)))
    return lax.dynamic_slice(padded, (0, plane * 4096), (frames, ROWS * 64))


def cot_message(own, halo):
    both = jnp.concatenate([own, halo], axis=0)
    mine = both[:, LEAD * 64 : LEAD * 64 + 4096].reshape(2 * FR, 32, 128).transpose(1, 0, 2)
    edge = jnp.stack([both[:, LEAD * 64 - 64 : LEAD * 64], both[:, LEAD * 64 + 4096 : LEAD * 64 + 4160]], axis=0)
    return near(mine), near(jnp.concatenate([edge[:, :FR], edge[:, FR:]], axis=2))


def frame_marks(counts, x_at):
    by_plane = jnp.pad(counts.reshape(4, 32), ((1, 1), (0, 0)))
    window = lax.dynamic_slice(by_plane, (x_at, 0), (3, 32))
    spot = jnp.arange(32)
    halo_count = jnp.where(spot >= 16, window[0], window[2])
    halo_in = jnp.where(spot >= 16, (spot >= 21) & (x_at > 0), (spot <= 10) & (x_at < 3))
    limit = jnp.stack([window[1], halo_count], axis=1)
    valid = (jnp.arange(4) < limit[:, :, None]) & jnp.stack([spot >= 0, halo_in], axis=1)[:, :, None]
    inside = jnp.stack([spot >= 0, halo_in], axis=1)[:, :, None] & (jnp.arange(4) >= 0)
    return jnp.stack([valid.reshape(256), inside.reshape(256)], axis=1).astype(F32)


def outputs_of(blocks, plane):
    twice = jnp.stack(blocks[::-1] + blocks[::-1], axis=0)
    rows = lax.dynamic_slice(twice, (3 - plane, 0, 0), (4, 288, 128)).reshape(4, FR, 72, 128)
    whole = jnp.concatenate([rows[0, :, :64], rows[1, :, :64], rows[2, :, :64], rows[3, :, :65]], axis=1)
    return whole[:, :, :64].reshape(FR, -1), whole[:, :, 64:].reshape(FR, -1)


def halo_pairs():
    pairs = []
    for x_at in range(4):
        for spot in range(32):
            if spot <= 10 and x_at < 3:
                pairs.append(((x_at + 1) * 32 + spot, x_at * 32 + spot))
            if spot >= 21 and x_at > 0:
                pairs.append(((x_at - 1) * 32 + spot, x_at * 32 + spot))
    return pairs


SEQ = ("x", "z", "core")


def exchange(values, axes):
    return lax.all_to_all(values, axes, 0, 0)


def near(values):
    return pltpu.with_memory_space_constraint(values, pltpu.VMEM)


def shards(
    signal, cotangent, counts, freq_gain, freq_in, freq_taps, freq_out, time_gain, time_in, time_taps, time_out
):
    plane = lax.axis_index("ch")
    x_at = lax.axis_index("x")
    spot = lax.axis_index(("z", "core"))
    grad_scale = 1.0 / math.sqrt(FR * 128 * (signal.shape[1] // 64))
    packed = pack(freq_in, freq_taps, freq_out, time_in, time_taps, time_out)
    gathered = exchange(packed, "ch")
    gathered = near(gathered)
    lanes = jnp.stack([plane_lanes(signal, plane), plane_lanes(cotangent, plane)], axis=0)
    halo = lax.ppermute(lanes, SEQ, halo_pairs())
    gain_f, gain_t = freq_gain[None], time_gain[None]
    marks = frame_marks(counts, x_at)
    beside = (spot == EDGE) | (spot == EDGE + 1)
    edge = jnp.stack([jnp.where((plane == 3) & (spot == EDGE + 1), 1, 0), jnp.where(beside, 1, 0)])
    flags = jnp.stack([jnp.where(plane == 3, 1, 0), jnp.where(plane > 0, 1, 0)])
    x_rows = lanes[0].reshape(FR * ROWS, 64)
    x_rows, marks, edge, flags = lax.optimization_barrier((x_rows, marks, edge, flags))
    marks, x_rows, x_halo = near(marks), near(x_rows), near(halo[0].reshape(FR * ROWS, 64))
    message, hidden = freq_forward(x_rows, x_halo, *cot_message(lanes[1], halo[1]), gathered, gain_f)
    bands = near(exchange(message, ("z", "core")))
    mixed, *sums = time_path(bands, marks, gathered, gain_t, edge)
    arrived = near(exchange(mixed, ("z", "core")))
    done, pieces = freq_backward(x_rows, hidden, arrived, gathered, gain_f, flags, sums)
    part = exchange(pieces, ("x", "core", "ch"))
    part = jnp.broadcast_to(jnp.sum(part.astype(F32), axis=0).astype(BF), (16, 24, 128))
    blocks = [done]
    for shift in (1, 2, 3):
        blocks.append(lax.ppermute(done, "ch", [(i, (i + shift) % 4) for i in range(4)]))
    part = exchange(part, "z")
    part = jnp.sum(part.astype(F32), axis=0)
    total = near(exchange(jnp.broadcast_to(part, (8, 24, 128)), ("x", "core")))
    return outputs_of(blocks, plane) + finish(total, grad_scale)


def solution(mesh):
    torus = Mesh(mesh.devices.reshape(4, 16, 2, 4), ("x", "z", "core", "ch"))
    return jax.shard_map(
        shards,
        mesh=torus,
        in_specs=(
            P(SEQ, None),
            P(SEQ, None),
            P(),
            P(),
            P(None, "ch"),
            P(None, "ch"),
            P("ch", None),
            P(),
            P(None, "ch"),
            P(None, None, "ch"),
            P("ch", None),
        ),
        out_specs=(
            P(SEQ, None),
            P(SEQ, None),
            P(),
            P(None, "ch"),
            P(None, "ch"),
            P("ch", None),
            P(),
            P(None, "ch"),
            P(None, None, "ch"),
            P("ch", None),
        ),
        check_vma=False,
    )
```

```python
import functools
import math

import jax
import jax.numpy as jnp
from jax import lax
from jax.experimental import pallas as pl
from jax.experimental.pallas import tpu as pltpu
from jax.sharding import Mesh, PartitionSpec as P


EPS = 1e-05
FR = 4
ROWS = 80
LEAD = 8
EDGE = 16
BF = jnp.bfloat16
F32 = jnp.float32


def nt(a, b):
    return lax.dot_general(a, b, (((1,), (1,)), ((), ())), preferred_element_type=F32)


def nn(a, b):
    return lax.dot_general(a, b, (((1,), (0,)), ((), ())), preferred_element_type=F32)


def tn(a, b):
    return lax.dot_general(a, b, (((0,), (0,)), ((), ())), preferred_element_type=F32)


def roll_rows(values, amount):
    return pltpu.roll(values, amount % values.shape[0], 0)


def sigmoid(values):
    return 0.5 * jnp.tanh(0.5 * values) + 0.5


def inverse_norm(features):
    return lax.rsqrt(jnp.mean(features * features, axis=-1, keepdims=True) + EPS)


def norm_back(d_normed, features, scale, gain):
    scaled = d_normed * gain
    summed = jnp.sum(scaled * features, axis=-1, keepdims=True)
    return scale * scaled - features * (scale * scale * scale * summed * (1.0 / features.shape[-1]))


def bins_conv(values, taps):
    return taps[0:1] * roll_rows(values, 1) + taps[1:2] * values + taps[2:3] * roll_rows(values, -1)


VMEM = pl.BlockSpec(memory_space=pltpu.VMEM)
SMEM = pl.BlockSpec(memory_space=pltpu.SMEM)


HALVES = (slice(0, 128), slice(128, 256))


def half_weights(gathered_ref, half, first):
    return jnp.concatenate([gathered_ref[2 * half + i, first : first + 64, :] for i in range(2)], axis=0)


def half_taps(gathered_ref, half, first, count):
    parts = []
    for i in range(2):
        both = gathered_ref[2 * half + i, 128:144, :].astype(F32)
        parts.append((both[:, :64] + both[:, 64:])[first : first + count])
    return jnp.concatenate(parts, axis=1)


def pack_kernel(
    plane_ref, signal, cotangent, freq_in, freq_taps, freq_out, time_in, time_taps, time_out, packed_ref, lanes_ref
):
    width = signal.shape[1]
    for plane in range(4):

        @pl.when(plane_ref[0] == plane)
        def _():
            first = 4096 * plane - 64 * LEAD
            low, high = max(first, 0), min(first + 64 * ROWS, width)
            if high - low < 64 * ROWS:
                lanes_ref[...] = jnp.zeros_like(lanes_ref)
            for i, source in enumerate((signal, cotangent)):
                lanes_ref[i, :, low - first : high - first] = source[:, low:high]

    taps = jnp.concatenate(
        [freq_taps[...]] + [time_taps[k] for k in range(3)] + [jnp.zeros((4, 64), F32)], axis=0
    )
    high = taps.astype(BF).astype(F32)
    low = taps - high
    turn = lambda ref: ref[...].astype(F32).T.astype(BF)
    freq_w = jnp.concatenate([turn(freq_in), freq_out[...]], axis=1)
    time_w = jnp.concatenate([turn(time_in), time_out[...]], axis=1)
    tap_w = jnp.concatenate([high, low], axis=1).astype(BF)
    for peer in range(4):
        packed_ref[peer, 0:64, :] = freq_w
        packed_ref[peer, 64:128, :] = time_w
        packed_ref[peer, 128:144, :] = tap_w


def pack(plane, signal, cotangent, *weights):
    return pl.pallas_call(
        pack_kernel,
        out_shape=(pltpu.VMEM((4, 144, 128), BF), pltpu.VMEM((2, FR, 64 * ROWS), BF)),
        in_specs=[SMEM] + [VMEM] * 8,
        name="pack",
    )(plane.reshape(1), signal, cotangent, *weights)


def freq_forward_kernel(
    own_ref, halo_ref, cot_ref, cot_edge_ref, gathered_ref, gain_ref, out_ref, hidden_out, rows_ref, tiles_ref
):
    gain = gain_ref[...]
    edges = []
    for part, pair_ref in enumerate((own_ref, halo_ref)):
        features = pair_ref[...].astype(F32)
        normed = (features * inverse_norm(features) * gain).astype(BF)
        mixed = features
        for half, lanes in enumerate(HALVES):
            weights = half_weights(gathered_ref, half, 0)
            hidden = nt(normed, weights[:, :64])
            if part == 0:
                hidden_out[:, lanes] = hidden
            drive = bins_conv(hidden, half_taps(gathered_ref, half, 0, 3))
            active = (drive * sigmoid(drive)).astype(BF)
            mixed = mixed + nn(active, weights[:, 64:])
        rows_ref[...] = mixed
        for f in range(FR):
            even = rows_ref[pl.ds(f * ROWS + LEAD, 32, stride=2), :]
            odd = rows_ref[pl.ds(f * ROWS + LEAD + 1, 32, stride=2), :]
            tiles_ref[pl.ds(FR * part + f, 32, stride=8), :] = jnp.concatenate([even, odd], axis=1)
        for bin_row in (LEAD - 1, LEAD + 64):
            edges.append(
                jnp.concatenate([mixed[f * ROWS + bin_row : f * ROWS + bin_row + 1] for f in range(FR)], axis=0)
            )
    out_ref[:, 0:8, :] = tiles_ref[...].reshape(32, 8, 128).astype(BF)
    out_ref[:, 8:16, :] = cot_ref[...]
    out_ref[0:EDGE, 16:24, :] = jnp.zeros((EDGE, 8, 128), BF)
    out_ref[EDGE + 2 : 32, 16:24, :] = jnp.zeros((30 - EDGE, 8, 128), BF)
    for side in range(2):
        x_edge = jnp.concatenate([edges[side], edges[2 + side]], axis=1)
        out_ref[EDGE + side, 16:24, :] = jnp.concatenate([x_edge, cot_edge_ref[side].astype(F32)], axis=0).astype(BF)


def freq_forward(pair, halo, cot, cot_edge, gathered, gain):
    rows = pair.shape[0]
    return pl.pallas_call(
        freq_forward_kernel,
        out_shape=(pltpu.VMEM((32, 24, 128), BF), pltpu.VMEM((rows, 256), F32)),
        scratch_shapes=[
            pltpu.VMEM((rows, 64), F32),
            pltpu.VMEM((256, 128), F32),
        ],
        name="freq_forward",
    )(pair, halo, cot, cot_edge, gathered, gain)


def freq_backward_kernel(
    flag_ref,
    pair_ref,
    hidden_ref,
    arrived_ref,
    gathered_ref,
    gain_ref,
    time_w_ref,
    time_t_ref,
    time_g_ref,
    done_ref,
    out_ref,
    tiles_ref,
    back_ref,
):
    gain = gain_ref[...]
    spread = jnp.concatenate([arrived_ref[...].astype(F32), jnp.zeros((32, 4, 128), F32)], axis=1)
    tiles_ref[...] = spread.reshape(512, 128)
    back_ref[...] = jnp.zeros_like(back_ref)
    left = flag_ref[1].astype(F32)
    for f in range(FR):
        back_ref[pl.ds(f * ROWS + LEAD, 32, stride=2), :] = tiles_ref[pl.ds(f, 32, stride=16), :]
        back_ref[pl.ds(f * ROWS + LEAD + 1, 32, stride=2), :] = tiles_ref[pl.ds(FR + f, 32, stride=16), :]
        back_ref[f * ROWS + LEAD - 1 : f * ROWS + LEAD, :] = tiles_ref[16 * EDGE + 8 + f : 16 * EDGE + 9 + f, :] * left
        back_ref[f * ROWS + LEAD + 64 : f * ROWS + LEAD + 65, :] = tiles_ref[16 * EDGE + 24 + f : 16 * EDGE + 25 + f, :]
    row = lax.broadcasted_iota(jnp.int32, (ROWS, 1), 0)
    upper = LEAD + 64 + flag_ref[0]
    one = jnp.where((row >= LEAD) & (row < upper), 1.0, 0.0).astype(F32)
    own = jnp.concatenate([one] * FR, axis=0)
    features = pair_ref[...].astype(F32)
    scale = inverse_norm(features)
    output, grad_wide = back_ref[:, :64], back_ref[:, 64:]
    grad = grad_wide.astype(BF)
    grad_own = (grad_wide * own).astype(BF)
    normed = (features * scale * gain * own).astype(BF)
    d_normed = None
    tap_halves, freq_w = [], []
    for half, lanes in enumerate(HALVES):
        weights = half_weights(gathered_ref, half, 0)
        taps = half_taps(gathered_ref, half, 0, 3)
        hidden = hidden_ref[:, lanes]
        before, after = roll_rows(hidden, 1), roll_rows(hidden, -1)
        drive = taps[0:1] * before + taps[1:2] * hidden + taps[2:3] * after
        gate = sigmoid(drive)
        active = drive * gate
        slope = gate + active * (1.0 - gate)
        grad_out = tn(active.astype(BF), grad_own)
        d_drive = nt(grad, weights[:, 64:]) * slope
        d_own = d_drive * own
        tap_halves.append(
            [jnp.sum(d_own * moved, axis=0, keepdims=True) for moved in (before, hidden, after)]
        )
        d_hidden = (
            taps[0:1] * roll_rows(d_drive, -1) + taps[1:2] * d_drive + taps[2:3] * roll_rows(d_drive, 1)
        ).astype(BF)
        grad_in = tn(d_hidden, normed)
        freq_w.append(jnp.concatenate([grad_out, grad_in], axis=1))
        part = nn(d_hidden, weights[:, :64])
        d_normed = part if d_normed is None else d_normed + part
    freq_g = jnp.sum(d_normed * features * (scale * own), axis=0, keepdims=True)
    d_signal = grad_wide + norm_back(d_normed, features, scale, gain)
    done = jnp.concatenate([output, d_signal], axis=1)
    done = jnp.concatenate([done[f * ROWS + LEAD : (f + 1) * ROWS] for f in range(FR)], axis=0).astype(BF)
    done_ref[...] = done
    gains = jnp.concatenate([freq_g, time_g_ref[...]], axis=1)
    for peer in range(4):
        half, at = peer // 2, 64 * (peer % 2)
        rows = [tap[:, at : at + 64] for tap in tap_halves[half]]
        rows.append(time_t_ref[:, 64 * peer : 64 * peer + 64])
        taps = jnp.concatenate(rows, axis=0)
        taps = jnp.concatenate([taps, jnp.zeros((12, 64), F32)], axis=1)
        taps = jnp.concatenate([taps, gains, jnp.zeros((3, 128), F32)], axis=0)
        for i in range(8):
            if i < 4:
                piece = freq_w[half][at + 16 * i : at + 16 * i + 16]
            else:
                piece = time_w_ref[64 * peer + 16 * i - 64 : 64 * peer + 16 * i - 48, :]
            small = taps[8 * i : 8 * i + 8] if i < 2 else jnp.zeros((8, 128), F32)
            out_ref[4 * i + peer] = jnp.concatenate([piece, small], axis=0).astype(BF)


def freq_backward(pair, hidden, arrived, gathered, gain, flags, sums):
    return pl.pallas_call(
        freq_backward_kernel,
        out_shape=(pltpu.VMEM((288, 128), BF), pltpu.VMEM((32, 24, 128), BF)),
        in_specs=[SMEM] + [VMEM] * 8,
        scratch_shapes=[
            pltpu.VMEM((512, 128), F32),
            pltpu.VMEM((FR * ROWS, 128), F32),
        ],
        name="freq_backward",
    )(flags, pair, near(hidden), arrived, gathered, gain, *[near(part) for part in sums])


def turned(tiles):
    return jnp.concatenate(
        [roll_rows(tiles[8 * i : 8 * i + 8], 4) for i in range(tiles.shape[0] // 8)], axis=0
    )


def groups_on(values, count):
    if count > 0:
        return jnp.concatenate([values[8 * count :], turned(values[: 8 * count])], axis=0)
    base = values.shape[0] + 8 * count
    return jnp.concatenate([turned(values[base:]), values[:base]], axis=0)


def tiled(values):
    return values.reshape(values.shape[0] // 8, 8, values.shape[1])


def next_frame(values, place, edge, amount):
    near_rows = pltpu.roll(tiled(values), amount % 8, 1)
    far_rows = pltpu.roll(tiled(groups_on(values, -amount)), (-3 * amount) % 8, 1)
    return jnp.where((place == edge)[None], far_rows, near_rows).reshape(values.shape)


def later(values, spacing, place):
    return next_frame(values, place, 3, -1) if spacing == 1 else groups_on(values, spacing // FR)


def earlier(values, spacing, place):
    return next_frame(values, place, 0, 1) if spacing == 1 else groups_on(values, -(spacing // FR))


def own_rows(values):
    tiles = values.reshape(values.shape[0] // 8, 8, values.shape[1])
    return jnp.sum(jnp.sum(tiles, axis=0)[:4], axis=0, keepdims=True)


def one_bin(message_ref, first, slot):
    if slot < 2:
        both = message_ref[:, 8 * first : 8 * first + 8].astype(F32).reshape(256, 128)
        return both[:, 64 * slot : 64 * slot + 64]
    edge = message_ref[:, 16:24].astype(F32)[:, 4 * first : 4 * first + 4]
    return jnp.concatenate([edge[:, :, :64], edge[:, :, 64:]], axis=1).reshape(256, 64)


def time_kernel(
    flag_ref,
    message_ref,
    marks_ref,
    gathered_ref,
    gain_ref,
    out_ref,
    grad_ref,
    tap_ref,
    gain_out,
):
    gain = gain_ref[...]
    valid, inside = marks_ref[:, 0:1], marks_ref[:, 1:2]
    spot = lax.broadcasted_iota(jnp.int32, (256, 1), 0)
    place = lax.broadcasted_iota(jnp.int32, (8, 128), 0) & 3

    def work(slot):
        share = jnp.where(flag_ref[0] > 0, 1.0, 0.0).astype(F32) if slot == 2 else 1.0

        def keep(ref, rows, lanes, value):
            if slot == 0:
                ref[rows, lanes] = value
            else:
                ref[rows, lanes] += value

        counted = jnp.where((spot & 7) < 4, share, 0.0).astype(F32)
        features, grad_wide = one_bin(message_ref, 0, slot), one_bin(message_ref, 1, slot)
        grad = grad_wide.astype(BF)
        grad_own = (grad_wide * counted).astype(BF)
        scale = inverse_norm(features)
        normed = features * scale * gain
        normed_own = (normed * counted).astype(BF)
        normed = normed.astype(BF)
        mixed, d_normed = features, None
        for side, lanes in enumerate(HALVES):
            weights = half_weights(gathered_ref, side, 64)
            weight_in, weight_out = weights[:, :64], weights[:, 64:]
            half = 0.5 * half_taps(gathered_ref, side, 3, 9)
            state = nt(normed, weight_in) * valid
            states, slopes = [], []
            for layer in range(3):
                spacing = (1, 4, 16)[layer]
                row = half[3 * layer : 3 * layer + 3]
                around = (earlier(state, spacing, place), state, later(state, spacing, place))
                drive = row[0:1] * around[0] + row[1:2] * state + row[2:3] * around[2]
                opened = jnp.tanh(drive) + 1.0
                active = drive * opened
                states.append(around)
                slopes.append(opened + active * (2.0 - opened))
                state = state + active
                if layer < 2:
                    state = state * inside
            top = state.astype(BF)
            mixed = mixed + nn(top, weight_out)
            keep(grad_ref, lanes, slice(0, 64), tn(top, grad_own))
            d_state = nt(grad, weight_out)
            for layer in reversed(range(3)):
                spacing = (1, 4, 16)[layer]
                row = half[3 * layer : 3 * layer + 3]
                d_drive = d_state * slopes[layer]
                if layer < 2:
                    d_drive = d_drive * inside
                for j, moved in enumerate(states[layer]):
                    at = 3 * layer + j
                    keep(tap_ref, slice(at, at + 1), lanes, own_rows(d_drive * moved) * (0.5 * share))
                d_state = d_state + (
                    row[0:1] * later(d_drive, spacing, place)
                    + row[1:2] * d_drive
                    + row[2:3] * earlier(d_drive, spacing, place)
                )
            d_pre = (d_state * valid).astype(BF)
            keep(grad_ref, lanes, slice(64, 128), tn(d_pre, normed_own))
            part = nn(d_pre, weight_in)
            d_normed = part if d_normed is None else d_normed + part
        keep(gain_out, slice(0, 1), slice(0, 64), own_rows(d_normed * features * scale) * share)
        d_one = grad_wide + norm_back(d_normed, features, scale, gain)
        both = jnp.concatenate([mixed, d_one], axis=1).reshape(32, 8, 128)
        out_ref[:, 4 * slot : 4 * slot + 4] = both[:, :4].astype(BF)

    work(0)
    work(1)

    @pl.when(flag_ref[1] > 0)
    def _():
        work(2)

    @pl.when(flag_ref[1] == 0)
    def _():
        out_ref[:, 8:12] = jnp.zeros((32, 4, 128), BF)


def time_path(message, marks, gathered, gain, flags):
    return pl.pallas_call(
        time_kernel,
        out_shape=(
            pltpu.VMEM((32, 12, 128), BF),
            pltpu.VMEM((256, 128), F32),
            pltpu.VMEM((9, 256), F32),
            pltpu.VMEM((1, 64), F32),
        ),
        in_specs=[SMEM] + [VMEM] * 4,
        name="time_path",
    )(flags, message, marks, gathered, gain)


def finish_kernel(
    scale, part_ref, freq_gain, freq_in, freq_taps, freq_out, time_gain, time_in, time_taps, time_out
):
    freq_w = jnp.concatenate([part_ref[i, 0:16, :] for i in range(4)], axis=0) * scale
    time_w = jnp.concatenate([part_ref[i, 0:16, :] for i in range(4, 8)], axis=0) * scale
    freq_out[...] = freq_w[:, :64]
    freq_in[...] = freq_w[:, 64:].T
    time_out[...] = time_w[:, :64]
    time_in[...] = time_w[:, 64:].T
    first, second = part_ref[0, 16:24, :] * scale, part_ref[1, 16:24, :] * scale
    freq_gain[...] = second[4:5, :64]
    time_gain[...] = second[4:5, 64:]
    freq_taps[...] = first[0:3, :64]
    time_taps[0] = first[3:6, :64]
    time_taps[1, 0:2] = first[6:8, :64]
    time_taps[1, 2:3] = second[0:1, :64]
    time_taps[2] = second[1:4, :64]


def finish(total, scale):
    shape = lambda *dims: jax.ShapeDtypeStruct(dims, F32)
    got = pl.pallas_call(
        functools.partial(finish_kernel, scale),
        out_shape=(
            shape(1, 64),
            shape(64, 64),
            shape(3, 64),
            shape(64, 64),
            shape(1, 64),
            shape(64, 64),
            shape(3, 3, 64),
            shape(64, 64),
        ),
        in_specs=[VMEM],
        name="finish",
    )(total)
    return (got[0][0], got[1], got[2], got[3], got[4][0], got[5], got[6], got[7])


def cot_message(own, halo):
    both = jnp.concatenate([own, halo], axis=0)
    mine = both[:, LEAD * 64 : LEAD * 64 + 4096].reshape(2 * FR, 32, 128).transpose(1, 0, 2)
    edge = jnp.stack([both[:, LEAD * 64 - 64 : LEAD * 64], both[:, LEAD * 64 + 4096 : LEAD * 64 + 4160]], axis=0)
    return near(mine), near(jnp.concatenate([edge[:, :FR], edge[:, FR:]], axis=2))


def frame_marks(counts, x_at):
    by_plane = jnp.pad(counts.reshape(4, 32), ((1, 1), (0, 0)))
    window = lax.dynamic_slice(by_plane, (x_at, 0), (3, 32))
    spot = jnp.arange(32)
    halo_count = jnp.where(spot >= 16, window[0], window[2])
    halo_in = jnp.where(spot >= 16, (spot >= 21) & (x_at > 0), (spot <= 10) & (x_at < 3))
    limit = jnp.stack([window[1], halo_count], axis=1)
    valid = (jnp.arange(4) < limit[:, :, None]) & jnp.stack([spot >= 0, halo_in], axis=1)[:, :, None]
    inside = jnp.stack([spot >= 0, halo_in], axis=1)[:, :, None] & (jnp.arange(4) >= 0)
    return jnp.stack([valid.reshape(256), inside.reshape(256)], axis=1).astype(F32)


def outputs_of(blocks, plane):
    twice = jnp.stack(blocks[::-1] + blocks[::-1], axis=0)
    rows = lax.dynamic_slice(twice, (3 - plane, 0, 0), (4, 288, 128)).reshape(4, FR, 72, 128)
    whole = jnp.concatenate([rows[0, :, :64], rows[1, :, :64], rows[2, :, :64], rows[3, :, :65]], axis=1)
    return whole[:, :, :64].reshape(FR, -1), whole[:, :, 64:].reshape(FR, -1)


def halo_pairs():
    pairs = []
    for x_at in range(4):
        for spot in range(32):
            if spot <= 10 and x_at < 3:
                pairs.append(((x_at + 1) * 32 + spot, x_at * 32 + spot))
            if spot >= 21 and x_at > 0:
                pairs.append(((x_at - 1) * 32 + spot, x_at * 32 + spot))
    return pairs


SEQ = ("x", "z", "core")


def exchange(values, axes):
    return lax.all_to_all(values, axes, 0, 0)


def near(values):
    return pltpu.with_memory_space_constraint(values, pltpu.VMEM)


def shards(
    signal, cotangent, counts, freq_gain, freq_in, freq_taps, freq_out, time_gain, time_in, time_taps, time_out
):
    plane = lax.axis_index("ch")
    x_at = lax.axis_index("x")
    spot = lax.axis_index(("z", "core"))
    grad_scale = 1.0 / math.sqrt(FR * 128 * (signal.shape[1] // 64))
    packed, lanes = pack(plane, signal, cotangent, freq_in, freq_taps, freq_out, time_in, time_taps, time_out)
    gathered = exchange(packed, "ch")
    gathered = near(gathered)
    halo = lax.ppermute(lanes, SEQ, halo_pairs())
    gain_f, gain_t = freq_gain[None], time_gain[None]
    marks = frame_marks(counts, x_at)
    beside = (spot == EDGE) | (spot == EDGE + 1)
    edge = jnp.stack([jnp.where((plane == 3) & (spot == EDGE + 1), 1, 0), jnp.where(beside, 1, 0)])
    flags = jnp.stack([jnp.where(plane == 3, 1, 0), jnp.where(plane > 0, 1, 0)])
    x_rows = lanes[0].reshape(FR * ROWS, 64)
    x_rows, marks, edge, flags = lax.optimization_barrier((x_rows, marks, edge, flags))
    marks, x_rows, x_halo = near(marks), near(x_rows), near(halo[0].reshape(FR * ROWS, 64))
    message, hidden = freq_forward(x_rows, x_halo, *cot_message(lanes[1], halo[1]), gathered, gain_f)
    bands = near(exchange(message, ("z", "core")))
    mixed, *sums = time_path(bands, marks, gathered, gain_t, edge)
    arrived = near(exchange(mixed, ("z", "core")))
    done, pieces = freq_backward(x_rows, hidden, arrived, gathered, gain_f, flags, sums)
    part = exchange(pieces, ("x", "core", "ch"))
    part = jnp.broadcast_to(jnp.sum(part.astype(F32), axis=0).astype(BF), (16, 24, 128))
    blocks = [done]
    for shift in (1, 2, 3):
        blocks.append(lax.ppermute(done, "ch", [(i, (i + shift) % 4) for i in range(4)]))
    part = exchange(part, "z")
    part = jnp.sum(part.astype(F32), axis=0)
    total = near(exchange(jnp.broadcast_to(part, (8, 24, 128)), ("x", "core")))
    return outputs_of(blocks, plane) + finish(total, grad_scale)


def solution(mesh):
    torus = Mesh(mesh.devices.reshape(4, 16, 2, 4), ("x", "z", "core", "ch"))
    return jax.shard_map(
        shards,
        mesh=torus,
        in_specs=(
            P(SEQ, None),
            P(SEQ, None),
            P(),
            P(),
            P(None, "ch"),
            P(None, "ch"),
            P("ch", None),
            P(),
            P(None, "ch"),
            P(None, None, "ch"),
            P("ch", None),
        ),
        out_specs=(
            P(SEQ, None),
            P(SEQ, None),
            P(),
            P(None, "ch"),
            P(None, "ch"),
            P("ch", None),
            P(),
            P(None, "ch"),
            P(None, None, "ch"),
            P("ch", None),
        ),
        check_vma=False,
    )
```
